32 devices in a mesh: batch: 8 (over z, y), tensor: 4 (over x, core).
Axes of the slice: x: 2, y: 2, z: 4, core: 2. Of those that a mesh axis runs over, the one named last changes fastest.
Arguments:
- inputs: bfloat16 [64, 288, 768], P('batch'), may hold values from -6 to 6
- lengths: int32 [64], P('batch'), may hold values from 50 to 288, as said below
- triple_weight: bfloat16 [3, 768, 768], P(None, 'batch', 'tensor'), may hold values from -0.21875 to 0.21875
- pair_bias: bfloat16 [2, 96, 8], P(None, 'tensor', 'batch'), may hold values from -3 to 3
- mixer_weight: bfloat16 [768, 768], P('tensor', 'batch'), may hold values from -1.75 to 1.75
- mixer_bias: bfloat16 [768], P('batch'), may hold values from -3 to 3
- first_gain: bfloat16 [768], P('batch'), may hold values from 0.099609375 to 1.8984375
- first_shift: bfloat16 [768], P('batch'), may hold values from -3 to 3
- expand_weight: bfloat16 [768, 3072], P('batch', 'tensor'), may hold values from -0.21875 to 0.21875
- expand_bias: bfloat16 [384, 8], P('tensor', 'batch'), may hold values from -3 to 3
- contract_weight: bfloat16 [3072, 768], P('tensor', 'batch'), may hold values from -0.109375 to 0.109375
- contract_bias: bfloat16 [768], P('batch'), may hold values from -3 to 3
- second_gain: bfloat16 [768], P('batch'), may hold values from 0.099609375 to 1.8984375
- second_shift: bfloat16 [768], P('batch'), may hold values from -3 to 3
- cotangent: bfloat16 [64, 288, 768], P('batch'), may hold values from -6 to 6
Outputs:
- outputs: bfloat16 [64, 288, 768], P('batch')
- input_grad: float32 [64, 288, 768], P('batch', None, 'tensor')
- triple_grad: float32 [3, 768, 768], P(None, 'batch', 'tensor')
- pair_grad: float32 [2, 96, 8], P(None, 'tensor', 'batch')
- mixer_grad: float32 [768, 768], P('tensor', 'batch')
- mixer_bias_grad: float32 [768], P('batch')
- first_gain_grad: float32 [768], P('batch')
- first_shift_grad: float32 [768], P('batch')
- expand_grad: float32 [768, 3072], P('batch', 'tensor')
- expand_bias_grad: float32 [384, 8], P('tensor', 'batch')
- contract_grad: float32 [3072, 768], P('tensor', 'batch')
- contract_bias_grad: float32 [768], P('batch')
- second_gain_grad: float32 [768], P('batch')
- second_shift_grad: float32 [768], P('batch')
The draws below stay inside these ranges and needn't reach their ends.
Inputs may be any that keep to these rules, and one draw needn't show every extreme that they name: `lengths`: every pair has at least 50 real tokens; some pair has exactly 288 and some exactly 50.
All inputs are finite; a program needn't handle non-finite values.
Results may differ from the reference program's by a relative error of at most 0.02.
Values may be sent and summed in bfloat16 or wider, within the bound.
A program may use at most 192 MiB of HBM per device.

```python
import jax
import jax.numpy as jnp
from jax import lax

HEADS = 12
HEAD = 64
FF = 3072
LEN = 288
MIN_LEN = 50
SEQ_DEV = 8
D = 768
PAIRS = 64
N_BATCH = 8


def draw_lengths(key, part):
    value_rows = jax.random.randint(jax.random.fold_in(key, 11), (PAIRS,), MIN_LEN, LEN + 1, dtype=jnp.int32)
    first = jax.random.randint(jax.random.fold_in(key, 12), (), 0, PAIRS, dtype=jnp.int32)
    offset = jax.random.randint(jax.random.fold_in(key, 13), (), 1, PAIRS, dtype=jnp.int32)
    second = (first + offset) % PAIRS
    return value_rows.at[first].set(LEN).at[second].set(MIN_LEN)


def spiked(entries, rng, source, target, blocks, factor):
    owner, partner = [(jnp.arange(entries.shape[axis_at]) // (entries.shape[axis_at] // blocks)).reshape([-1 if axis == axis_at else 1 for axis in range(entries.ndim)]) for axis_at in (source, target)]
    chosen = jax.random.permutation(rng, blocks)[partner]
    strong = (owner == chosen) | (owner == (partner + blocks // 2) % blocks)
    return jnp.where(strong, factor * entries, entries)


def block_levels(own_key, extent, shards, smallest, top_value):
    def one(axis_at, blocks):
        steps = jax.random.uniform(jax.random.fold_in(jax.random.fold_in(own_key, 6), axis_at), (blocks,), jnp.float32, smallest / len(shards), top_value / len(shards))
        return jnp.repeat(jnp.exp(steps), extent[axis_at] // blocks).reshape((-1,) + (1,) * (len(extent) - axis_at - 1))

    factor_of = one(*shards[0])
    for cut in shards[1:]:
        factor_of = factor_of * one(*cut)
    return factor_of


def normal_values(own_key, shape, scale, most, shards=(), kind=jnp.bfloat16):
    array = scale * jax.random.normal(own_key, shape, jnp.float32)
    if shards:
        array = array * block_levels(own_key, shape, shards, -0.22, 0.18)
    return jnp.clip(array, -most, most).astype(kind)


def gaussian_with(key, extent, scale, limit, split, heavy, kind=jnp.bfloat16):
    values = scale * jax.random.normal(key, extent, jnp.float32)
    if split:
        values = values * block_levels(key, extent, split, -0.22, 0.18)
    return jnp.clip(spiked(values, jax.random.fold_in(key, 3), *heavy), -limit, limit).astype(kind)


def setup_inputs(seed: int = 0) -> dict:
    seeds = jax.random.split(jax.random.key(seed), 16)
    inputs = gaussian_with(seeds[0], (PAIRS, LEN, D), 1.0, 6.0, ((0, 8),), (0, 2, 8, 2.0))
    lengths = draw_lengths(jax.random.fold_in(seeds[15], 71), 0)
    triple_weight = normal_values(seeds[2], (3, D, D), D ** -0.5, 0.21875, ((1, 8), (2, 4)))
    pair_bias = normal_values(seeds[3], (2, D // N_BATCH, N_BATCH), 0.5, 3.0, ((1, 4), (2, 8)))
    mixer_weight = normal_values(seeds[4], (D, D), (D // 64) ** -0.5, 1.75, ((0, 4), (1, 8)))
    mixer_bias = normal_values(seeds[5], (D,), 0.5, 3.0, ((0, 8),))
    first_gain = jnp.clip(1.0 + 0.18 * jax.random.normal(seeds[6], (D,), jnp.float32), 0.099609375, 1.8984375).astype(jnp.bfloat16)
    first_shift = normal_values(seeds[7], (D,), 0.5, 3.0, ((0, 8),))
    expand_weight = normal_values(seeds[8], (D, FF), D ** -0.5, 0.21875, ((0, 8), (1, 4)))
    expand_bias = normal_values(seeds[9], (FF // N_BATCH, N_BATCH), 0.5, 3.0, ((0, 4), (1, 8)))
    contract_weight = normal_values(seeds[10], (FF, D), FF ** -0.5, 0.109375, ((0, 4), (1, 8)))
    contract_bias = normal_values(seeds[11], (D,), 0.5, 3.0, ((0, 8),))
    second_gain = jnp.clip(1.0 + 0.18 * jax.random.normal(seeds[12], (D,), jnp.float32), 0.099609375, 1.8984375).astype(jnp.bfloat16)
    second_shift = normal_values(seeds[13], (D,), 0.5, 3.0, ((0, 8),))
    cotangent = gaussian_with(seeds[14], (PAIRS, LEN, D), 1.0, 6.0, ((0, 8),), (0, 2, 8, 2.0))
    return dict(inputs=inputs, lengths=lengths, triple_weight=triple_weight, pair_bias=pair_bias, mixer_weight=mixer_weight, mixer_bias=mixer_bias, first_gain=first_gain, first_shift=first_shift, expand_weight=expand_weight, expand_bias=expand_bias, contract_weight=contract_weight, contract_bias=contract_bias, second_gain=second_gain, second_shift=second_shift, cotangent=cotangent)


EPS = 1e-12
SCALE = 0.125
MASKED = -1e+30
FULL_PRECISION = lax.Precision.HIGHEST

@jax.custom_vjp
def low(v):
    return lax.optimization_barrier(v.astype(jnp.bfloat16)).astype(jnp.float32)

@jax.custom_vjp
def low_back(v):
    return v

def low_keep(v):
    return (low(v), None)

def low_pass(kept, grad):
    return (grad,)

def back_keep(v):
    return (v, None)

def back_low(kept, grad):
    return (low(grad),)
low.defvjp(low_keep, low_pass)
low_back.defvjp(back_keep, back_low)

def normalize(value_rows, gain, shift):
    centred = value_rows - lax.optimization_barrier(jnp.mean(value_rows, axis=-1, keepdims=True))
    return centred * lax.rsqrt(lax.optimization_barrier(jnp.mean(centred * centred, axis=-1, keepdims=True)) + EPS) * gain + shift

def layer(token_rows, key_valid, params):
    query_key_value, pair, mixer, mixer_shift, first_norm_gain, shift_one, expand, expand_shift, contract, contract_shift, gain_two, shift_two = params
    seqs = token_rows.shape[0]
    projected_rows = jnp.einsum('rzj,vjy->vrzy', token_rows, query_key_value, precision=FULL_PRECISION)
    queries = low(low_back(projected_rows[0] + pair[0])).reshape(seqs, LEN, HEADS, HEAD)
    keys = low(low_back(projected_rows[1])).reshape(seqs, LEN, HEADS, HEAD)
    value_rows = low(low_back(projected_rows[2] + pair[1])).reshape(seqs, LEN, HEADS, HEAD)
    scores = low_back(jnp.einsum('sqhd,skhd->shqk', queries, keys, precision=FULL_PRECISION) * SCALE)
    scores = jnp.where(key_valid[:, None, None, :], scores, MASKED)
    attention = low(jax.nn.softmax(scores, axis=-1))
    context = jnp.einsum('shqk,skhd->sqhd', attention, value_rows, precision=FULL_PRECISION)
    context = low(low_back(context)).reshape(seqs, LEN, HEADS * HEAD)
    mixed = low_back(jnp.einsum('sqc,cd->sqd', context, mixer, precision=FULL_PRECISION))
    hidden = normalize(token_rows + mixed + mixer_shift, first_norm_gain, shift_one)
    before = low_back(jnp.einsum('sqd,df->sqf', low(hidden), expand, precision=FULL_PRECISION) + expand_shift)
    activated = low(jax.nn.gelu(before, approximate=False))
    branch = low_back(jnp.einsum('sqf,fd->sqd', activated, contract, precision=FULL_PRECISION))
    return normalize(hidden + branch + contract_shift, gain_two, shift_two)

def add_trees(first, second):
    return first + second

def reference(inputs, lengths, triple_weight, pair_bias, mixer_weight, mixer_bias, first_gain, first_shift, expand_weight, expand_bias, contract_weight, contract_bias, second_gain, second_shift, cotangent):
    params = (triple_weight.astype(jnp.float32), pair_bias.astype(jnp.float32).reshape(2, D), mixer_weight.astype(jnp.float32), mixer_bias.astype(jnp.float32), first_gain.astype(jnp.float32), first_shift.astype(jnp.float32), expand_weight.astype(jnp.float32), expand_bias.astype(jnp.float32).reshape(FF), contract_weight.astype(jnp.float32), contract_bias.astype(jnp.float32), second_gain.astype(jnp.float32), second_shift.astype(jnp.float32))
    group = 2 * SEQ_DEV
    blocks = PAIRS // group
    block_inputs = inputs.astype(jnp.float32).reshape(blocks, group, LEN, D)
    block_lengths = lengths.reshape(blocks, group)
    block_cots = cotangent.astype(jnp.float32).reshape(blocks, group, LEN, D)
    positions = jnp.arange(LEN, dtype=jnp.int32)

    def step(totals, item):
        block_in, block_len, block_cot = item
        key_valid = positions[None, :] < block_len[:, None]

        def run(token_rows, weights):
            return layer(token_rows, key_valid, weights)
        result, back = jax.vjp(run, block_in, params)
        token_grad, weight_grads = back(block_cot)
        totals = jax.tree.map(add_trees, totals, weight_grads)
        return (totals, (result.astype(jnp.bfloat16), token_grad))
    zeros = jax.tree.map(jnp.zeros_like, params)
    totals, (results, token_grads) = lax.scan(step, zeros, (block_inputs, block_lengths, block_cots))
    g_triple, g_pair, g_mixer, g_mixer_shift, g_gain_one, g_shift_one, g_expand, g_expand_shift, g_contract, g_contract_shift, g_gain_two, g_shift_two = totals
    return (results.reshape(PAIRS, LEN, D), token_grads.reshape(PAIRS, LEN, D), g_triple, g_pair.reshape(2, D // N_BATCH, N_BATCH), g_mixer, g_mixer_shift, g_gain_one, g_shift_one, g_expand, g_expand_shift.reshape(FF // N_BATCH, N_BATCH), g_contract, g_contract_shift, g_gain_two, g_shift_two)
```

```python
from functools import partial

import jax
import jax.numpy as jnp
from jax import lax
from jax.experimental import pallas as pl
from jax.experimental.pallas import tpu as pltpu
from jax.sharding import PartitionSpec as P

HEAD = 64
EPS = 1e-12
SCALE = 0.125
MASKED = -1e30
MESH = pl.DeviceIdType.MESH
F32 = jnp.float32
BF16 = jnp.bfloat16
NZ, NY, NX, NC = 4, 2, 2, 2


class Place:
    def __init__(self):
        b = lax.axis_index("batch")
        t = lax.axis_index("tensor")
        self.z, self.y = b // NY, b % NY
        self.x, self.c = t // NC, t % NC

    def at(self, z=None, y=None, x=None, c=None):
        z = self.z if z is None else z
        y = self.y if y is None else y
        x = self.x if x is None else x
        c = self.c if c is None else c
        return (z * NY + y, x * NC + c)

    def core(self):
        return self.at(c=1 - self.c)

    def xp(self):
        return self.at(x=1 - self.x)

    def yp(self):
        return self.at(y=1 - self.y)

    def zp(self, step):
        return self.at(z=(self.z + step) % NZ)

    def greet(self):
        barrier = pltpu.get_barrier_semaphore()
        peers = [self.core(), self.xp(), self.yp()] + [self.zp(s) for s in range(1, NZ)]
        for peer in peers:
            pl.semaphore_signal(barrier, inc=1, device_id=peer, device_id_type=MESH)
        pl.semaphore_wait(barrier, len(peers))


def remote(src, dst, sems, index, peer):
    return pltpu.make_async_remote_copy(
        src_ref=src,
        dst_ref=dst,
        send_sem=sems.at[0, index],
        recv_sem=sems.at[1, index],
        device_id=peer,
        device_id_type=MESH,
    )


def gather_kernel(pack_ref, vec_ref, w_ref, v_ref, sems, vsems, lsems):
    me = Place()
    z, y, x, c = me.z, me.y, me.x, me.c
    packs = pack_ref.shape[0]
    half = pack_ref.shape[2] // 2
    lo, hi = pl.ds(0, half), pl.ds(half, half)
    own = [
        pltpu.make_async_copy(pack_ref.at[p], w_ref.at[p, c, x, z, y], lsems.at[p])
        for p in range(packs)
    ]
    own_vec = pltpu.make_async_copy(vec_ref, v_ref.at[c, x, z, y], lsems.at[packs])
    for copy in own:
        copy.start()
    own_vec.start()
    me.greet()
    started = []

    def send(src, dst, table, index, peer):
        copy = remote(src, dst, table, index, peer)
        copy.start()
        started.append(copy)
        return copy

    own_vec.wait()
    first = []
    vfirst = [
        send(v_ref.at[c, x, z, y], v_ref.at[c, x, z, y], vsems, s - 1, me.zp(s))
        for s in range(1, NZ)
    ]
    for p in range(packs):
        own[p].wait()
        slot = w_ref.at[p, c, x, z, y]
        first.append([send(slot, slot, sems, 8 * p + s - 1, me.zp(s)) for s in range(1, NZ)])
    for copy in vfirst:
        copy.wait_recv()
    slot = v_ref.at[c, x, :, y]
    vx = send(slot, slot, vsems, 3, me.xp())
    second = []

    def stage2(p):
        for copy in first[p]:
            copy.wait_recv()
        a = w_ref.at[p, c, x, :, y, :, lo]
        b = w_ref.at[p, c, x, :, y, :, hi]
        second.append((send(a, a, sems, 8 * p + 3, me.xp()), send(b, b, sems, 8 * p + 4, me.yp())))

    third = []

    def stage3(p):
        for copy in second[p]:
            copy.wait_recv()
        a = w_ref.at[p, c, :, :, y, :, lo]
        b = w_ref.at[p, c, x, :, :, :, hi]
        third.append((send(a, a, sems, 8 * p + 5, me.yp()), send(b, b, sems, 8 * p + 6, me.xp())))

    fourth = []

    def stage4(p):
        for copy in third[p]:
            copy.wait_recv()
        a = w_ref.at[p, c]
        fourth.append(send(a, a, sems, 8 * p + 7, me.core()))

    stage2(0)
    vx.wait_recv()
    slot = v_ref.at[c, :, :, y]
    vy = send(slot, slot, vsems, 4, me.yp())
    stage3(0)
    vy.wait_recv()
    slot = v_ref.at[c]
    vc = send(slot, slot, vsems, 5, me.core())
    for p in range(1, packs):
        stage2(p)
        stage4(p - 1)
        stage3(p)
    stage4(packs - 1)
    vc.wait_recv()
    for copy in fourth:
        copy.wait_recv()
    for copy in started:
        copy.wait_send()


def gather_all(pack, vec):
    packs, nr, width = pack.shape
    shape = (packs, NC, NX, NZ, NY, nr, width)
    vshape = (NC, NX, NZ, NY) + vec.shape
    return pl.pallas_call(
        gather_kernel,
        out_shape=(jax.ShapeDtypeStruct(shape, BF16), jax.ShapeDtypeStruct(vshape, BF16)),
        in_specs=[pl.BlockSpec(memory_space=pltpu.VMEM)] * 2,
        out_specs=(pl.BlockSpec(memory_space=pltpu.VMEM),) * 2,
        scratch_shapes=[
            pltpu.SemaphoreType.DMA((2, 8 * packs)),
            pltpu.SemaphoreType.DMA((2, 6)),
            pltpu.SemaphoreType.DMA((packs + 1,)),
        ],
        compiler_params=pltpu.CompilerParams(
            collective_id=0, has_side_effects=True, vmem_limit_bytes=60 << 20
        ),
    )(pack, vec)


YFIRST = 640


def scatter_kernel(
    g_in, v_in, out_in, ig_in,
    red_ref, vred_ref, outs_ref, ig_ref,
    g_ref, v_ref, rc, ry0, rx1, rx0, ry1, rz, vc, vy, vx, vz,
    sems, vsems, osems, lsems,
):
    me = Place()
    z, y, x, c = me.z, me.y, me.x, me.c
    packs = g_in.shape[0]
    width = g_in.shape[-1]
    lo, hi = pl.ds(0, YFIRST), pl.ds(YFIRST, width - YFIRST)
    order = list(reversed(range(packs)))
    loads = [pltpu.make_async_copy(g_in.at[p], g_ref.at[p], lsems.at[p]) for p in range(packs)]
    for p in order:
        loads[p].start()
    load_v = pltpu.make_async_copy(v_in, v_ref, lsems.at[packs])
    load_v.start()
    rows = pl.ds(0, 1)
    t_own = x * NC + c
    out_own = pltpu.make_async_copy(out_in, outs_ref.at[t_own], lsems.at[packs + 1])
    out_own.start()
    ig_own = pltpu.make_async_copy(ig_in.at[x], ig_ref.at[t_own], lsems.at[packs + 2])
    ig_own.start()
    me.greet()
    started = []

    def send(src, dst, table, index, peer):
        copy = remote(src, dst, table, index, peer)
        copy.start()
        started.append(copy)
        return copy

    def add(dst, src, at):
        @pl.loop(0, dst.shape[0])
        def _(i):
            dst[i] = dst[i] + src[i]

    ox = send(out_in, outs_ref.at[t_own], osems, 0, me.xp())
    oc = send(out_in, outs_ref.at[t_own], osems, 1, me.core())
    ix = send(ig_in.at[1 - x], ig_ref.at[t_own], osems, 2, me.xp())
    ic = send(ig_in.at[x], ig_ref.at[t_own], osems, 3, me.core())

    cs = {}
    for p in order:
        loads[p].wait()
        cs[p] = send(g_ref.at[p, 1 - c], rc.at[p], sems, 6 * p, me.core())
    load_v.wait()
    vcs = send(v_ref.at[1 - c], vc, vsems, 0, me.core())
    s1, s2 = {}, {}

    def stage1(p):
        cs[p].wait_recv()
        for i in range(NX):
            for j in range(NZ):
                for k in range(NY):
                    g_ref[p, c, i, j, k] = g_ref[p, c, i, j, k] + rc[p, i, j, k]
        s1[p] = (
            send(g_ref.at[p, c, :, :, 1 - y, :, lo], ry0.at[p], sems, 6 * p + 1, me.yp()),
            send(g_ref.at[p, c, 1 - x, :, :, :, hi], rx1.at[p], sems, 6 * p + 2, me.xp()),
        )

    def stage2(p):
        for copy in s1[p]:
            copy.wait_recv()
        for j in range(NZ):
            for i in range(NX):
                g_ref[p, c, i, j, y, :, lo] = g_ref[p, c, i, j, y, :, lo] + ry0[p, i, j]
            for k in range(NY):
                g_ref[p, c, x, j, k, :, hi] = g_ref[p, c, x, j, k, :, hi] + rx1[p, j, k]
        s2[p] = (
            send(g_ref.at[p, c, 1 - x, :, y, :, lo], rx0.at[p], sems, 6 * p + 3, me.xp()),
            send(g_ref.at[p, c, x, :, 1 - y, :, hi], ry1.at[p], sems, 6 * p + 4, me.yp()),
        )

    s3 = {}

    def stage3(p):
        for copy in s2[p]:
            copy.wait_recv()
        for j in range(NZ):
            g_ref[p, c, x, j, y, :, lo] = g_ref[p, c, x, j, y, :, lo] + rx0[p, j]
            g_ref[p, c, x, j, y, :, hi] = g_ref[p, c, x, j, y, :, hi] + ry1[p, j]
        s3[p] = []
        for s in range(1, NZ):
            s3[p].append(
                send(
                    g_ref.at[p, c, x, (z + s) % NZ, y], rz.at[p, s - 1],
                    sems, 6 * packs + 3 * p + s - 1, me.zp(s),
                )
            )

    def stage4(p):
        for copy in s3[p]:
            copy.wait_recv()
        total = g_ref[p, c, x, z, y].astype(F32)
        for s in range(1, NZ):
            total = total + rz[p, s - 1].astype(F32)
        red_ref[p] = total

    for i, p in enumerate(order):
        stage1(p)
    vcs.wait_recv()
    for i in range(NX):
        v_ref[c, i] = v_ref[c, i] + vc[i]
    vys = send(v_ref.at[c, :, :, 1 - y], vy, vsems, 1, me.yp())
    for p in order:
        stage2(p)
    vys.wait_recv()
    for i in range(NX):
        for j in range(NZ):
            v_ref[c, i, j, y] = v_ref[c, i, j, y] + vy[i, j]
    vxs = send(v_ref.at[c, 1 - x, :, y], vx, vsems, 2, me.xp())
    for p in order:
        stage3(p)
    vxs.wait_recv()
    for j in range(NZ):
        v_ref[c, x, j, y] = v_ref[c, x, j, y] + vx[j]
    vzs = [
        send(v_ref.at[c, x, (z + s) % NZ, y], vz.at[s - 1], vsems, 2 + s, me.zp(s))
        for s in range(1, NZ)
    ]
    t_x = (1 - x) * NC + c
    ox.wait_recv()
    of = send(outs_ref.at[t_x], outs_ref.at[t_x], osems, 4, me.core())
    ix.wait_recv()
    jf = send(ig_ref.at[t_x], ig_ref.at[t_x], osems, 5, me.core())
    for p in order:
        stage4(p)
    for copy in vzs:
        copy.wait_recv()
    total = v_ref[c, x, z, y]
    for s in range(1, NZ):
        total = total + vz[s - 1]
    vred_ref[...] = total
    for copy in (oc, ic, of, jf):
        copy.wait_recv()
    for copy in started:
        copy.wait_send()
    out_own.wait()
    ig_own.wait()


def scatter_all(g, v, out, ig):
    packs, width = g.shape[0], g.shape[-1]
    nr = g.shape[-2]
    rows = out.shape[0]
    rest = width - YFIRST
    return pl.pallas_call(
        scatter_kernel,
        out_shape=(
            jax.ShapeDtypeStruct((packs, nr, width), F32),
            jax.ShapeDtypeStruct(v.shape[-2:], F32),
            jax.ShapeDtypeStruct((NX * NC, rows, width), BF16),
            jax.ShapeDtypeStruct((NX * NC, rows, width // NX), BF16),
        ),
        in_specs=[pl.BlockSpec(memory_space=pl.ANY)] * 4,
        out_specs=(
            pl.BlockSpec(memory_space=pltpu.VMEM),
            pl.BlockSpec(memory_space=pltpu.VMEM),
            pl.BlockSpec(memory_space=pl.ANY),
            pl.BlockSpec(memory_space=pl.ANY),
        ),
        scratch_shapes=[
            pltpu.VMEM(g.shape, BF16),
            pltpu.VMEM(v.shape, F32),
            pltpu.VMEM((packs, NX, NZ, NY, nr, width), BF16),
            pltpu.VMEM((packs, NX, NZ, nr, YFIRST), BF16),
            pltpu.VMEM((packs, NZ, NY, nr, rest), BF16),
            pltpu.VMEM((packs, NZ, nr, YFIRST), BF16),
            pltpu.VMEM((packs, NZ, nr, rest), BF16),
            pltpu.VMEM((packs, NZ - 1, nr, width), BF16),
            pltpu.VMEM((NX, NZ, NY) + v.shape[-2:], F32),
            pltpu.VMEM((NX, NZ) + v.shape[-2:], F32),
            pltpu.VMEM((NZ,) + v.shape[-2:], F32),
            pltpu.VMEM((NZ - 1,) + v.shape[-2:], F32),
            pltpu.SemaphoreType.DMA((2, 9 * packs)),
            pltpu.SemaphoreType.DMA((2, 6)),
            pltpu.SemaphoreType.DMA((2, 6)),
            pltpu.SemaphoreType.DMA((packs + 3,)),
        ],
        compiler_params=pltpu.CompilerParams(
            collective_id=1, has_side_effects=True, vmem_limit_bytes=60 << 20
        ),
    )(g, v, out, ig)


def normalize(value_rows, gain, shift):
    centred = value_rows - jnp.mean(value_rows, axis=-1, keepdims=True)
    scaled = lax.rsqrt(jnp.mean(centred * centred, axis=-1, keepdims=True) + EPS)
    normed = centred * scaled
    return (normed * gain + shift, normed, scaled)


def normalize_back(grad, normed, scaled, gain):
    weighted = grad * gain
    inner = jnp.mean(weighted * normed, axis=-1, keepdims=True)
    return scaled * (weighted - jnp.mean(weighted, axis=-1, keepdims=True) - normed * inner)


def layer_step(x_seq, lengths, cot, w, d_vec, e_bias, p_bias):
    seqs, length, width = x_seq.shape
    rows = seqs * length
    blocks = w.shape[1]
    feat = width // blocks
    heads = feat // HEAD
    mixer_shift, gain_one, shift_one, contract_shift, gain_two, shift_two = d_vec
    x = x_seq.reshape(rows, width)
    att = w[0]
    cut = 2 * HEAD
    def columns(i):
        return jnp.concatenate(
            [att[:, :, i * cut:(i + 1) * cut], att[:, :, 4 * cut + i * HEAD:4 * cut + (i + 1) * HEAD]], axis=2
        )
    wq, wk, wv, wm = (columns(i) for i in range(4))
    def project(weight, bias):
        out = jnp.einsum("rd,tde->rte", x, weight, preferred_element_type=F32)
        if bias is not None:
            out = out + bias
        return out.astype(BF16).reshape(seqs, length, blocks * heads, HEAD)
    queries = project(wq, p_bias[0])
    keys = project(wk, None)
    values = project(wv, p_bias[1])
    valid = lax.broadcasted_iota(jnp.int32, (seqs, 1, 1, length), 3) < lengths[:, None, None, None]
    raw = jnp.einsum("sqhd,skhd->shqk", queries, keys, preferred_element_type=F32) * SCALE
    raw = jnp.where(valid, raw, MASKED)
    peak = jnp.max(raw, axis=-1, keepdims=True)
    powers = jnp.exp(raw - peak)
    probs = powers / jnp.sum(powers, axis=-1, keepdims=True)
    attention = probs.astype(BF16)
    context = jnp.einsum("shqk,skhd->sqhd", attention, values, preferred_element_type=F32)
    context = context.astype(BF16).reshape(rows, blocks, feat)
    mixed = jnp.einsum("rtc,tdc->rd", context, wm, preferred_element_type=F32)
    hidden, normed_one, scaled_one = normalize(x.astype(F32) + mixed + mixer_shift, gain_one, shift_one)
    hidden_low = hidden.astype(BF16)
    before = jnp.einsum("rd,tdf->rtf", hidden_low, w[1], preferred_element_type=F32) + e_bias
    activated = jax.nn.gelu(before, approximate=False).astype(BF16)
    branch = jnp.einsum("rtf,tdf->rd", activated, w[2], preferred_element_type=F32)
    result, normed_two, scaled_two = normalize(hidden + branch + contract_shift, gain_two, shift_two)
    outputs = result.astype(BF16)
    up = cot.reshape(rows, width).astype(F32)
    gain_two_grad = jnp.sum(up * normed_two, axis=0)
    shift_two_grad = jnp.sum(up, axis=0)
    after_two = normalize_back(up, normed_two, scaled_two, gain_two)
    contract_shift_grad = jnp.sum(after_two, axis=0)
    two_low = after_two.astype(BF16)
    contract_grad = jnp.einsum("rd,rtf->tdf", two_low, activated, preferred_element_type=F32)
    act_grad = jnp.einsum("rd,tdf->rtf", two_low, w[2], preferred_element_type=F32)
    _, gelu_back = jax.vjp(partial(jax.nn.gelu, approximate=False), before)
    before_grad = gelu_back(act_grad)[0].astype(BF16)
    expand_grad = jnp.einsum("rd,rtf->tdf", hidden_low, before_grad, preferred_element_type=F32)
    e_bias_grad = jnp.sum(before_grad, axis=0, dtype=F32)
    hidden_part = jnp.einsum("rtf,tdf->rd", before_grad, w[1], preferred_element_type=F32)
    hidden_grad = after_two + hidden_part
    after_one = normalize_back(hidden_grad, normed_one, scaled_one, gain_one)
    gain_one_grad = jnp.sum(hidden_grad * normed_one, axis=0)
    shift_one_grad = jnp.sum(hidden_grad, axis=0)
    mixer_shift_grad = jnp.sum(after_one, axis=0)
    one_low = after_one.astype(BF16)
    mixer_grad = jnp.einsum("rd,rtc->tdc", one_low, context, preferred_element_type=F32)
    context_grad = jnp.einsum("rd,tdc->rtc", one_low, wm, preferred_element_type=F32).astype(BF16)
    context_grad = context_grad.reshape(seqs, length, blocks * heads, HEAD)
    value_grad = jnp.einsum("shqk,sqhd->skhd", attention, context_grad, preferred_element_type=F32)
    weight_grad = jnp.einsum("sqhd,skhd->shqk", context_grad, values, preferred_element_type=F32)
    score_grad = probs * (weight_grad - jnp.sum(probs * weight_grad, axis=-1, keepdims=True))
    score_grad = score_grad.astype(BF16)
    query_grad = jnp.einsum("shqk,skhd->sqhd", score_grad, keys, preferred_element_type=F32) * SCALE
    key_grad = jnp.einsum("shqk,sqhd->skhd", score_grad, queries, preferred_element_type=F32) * SCALE
    streams = [g.astype(BF16).reshape(rows, blocks, feat) for g in (query_grad, key_grad, value_grad)]
    p_grad = [jnp.sum(streams[i], axis=0, dtype=F32) for i in (0, 2)]
    tgrads = [jnp.einsum("rd,rte->tde", x, s, preferred_element_type=F32) for s in streams] + [mixer_grad]
    att_grad = jnp.concatenate([g[:, :, :cut] for g in tgrads] + [g[:, :, cut:] for g in tgrads], axis=2)
    part = sum(
        jnp.einsum("rte,tde->rd", s, wt, preferred_element_type=F32) for s, wt in zip(streams, (wq, wk, wv))
    )
    input_grad = (after_one + part).astype(BF16)
    grads = jnp.stack([att_grad, expand_grad, contract_grad]).astype(BF16)
    vecs = jnp.stack(
        [mixer_shift_grad, gain_one_grad, shift_one_grad, contract_shift_grad, gain_two_grad, shift_two_grad]
    )
    return outputs, input_grad, grads, vecs, e_bias_grad, jnp.stack(p_grad)


def make_on_device(sizes):
    fast = sizes == {"batch": NZ * NY, "tensor": NX * NC}

    def on_device(
        inputs, lengths, triple_weight, pair_bias, mixer_weight, mixer_bias, first_gain, first_shift,
        expand_weight, expand_bias, contract_weight, contract_bias, second_gain, second_shift, cotangent,
    ):
        pairs, length, width = inputs.shape
        n_tensor, n_batch = sizes["tensor"], sizes["batch"]
        nr = width // n_batch
        own_pairs = pairs // n_tensor
        t = lax.axis_index("tensor")
        cut = 2 * HEAD
        four = [triple_weight[0], triple_weight[1], triple_weight[2], mixer_weight.T]
        att = jnp.concatenate([m[:, :cut] for m in four] + [m[:, cut:] for m in four], axis=1)
        pack = jnp.stack([att, expand_weight, contract_weight.T])
        def row(v):
            return jnp.pad(v.reshape(1, -1), ((0, 0), (0, 128 - v.size)))
        vec = jnp.concatenate(
            [row(v) for v in (mixer_bias, first_gain, first_shift, contract_bias, second_gain, second_shift,
                              expand_bias, pair_bias)] + [jnp.zeros((8, 128), BF16)], axis=0
        )
        feat = width // n_tensor
        if fast:
            w, v = gather_all(pack, vec)
            w = w.reshape(3, n_tensor, width, width)
            v = v.reshape(n_tensor, n_batch, 16, 128)
            order = [k % NX * NC + k // NX for k in range(n_tensor)]
        else:
            w = lax.all_gather(lax.all_gather(pack, "batch", axis=1, tiled=True), "tensor", axis=1)
            v = lax.all_gather(lax.all_gather(vec, "batch"), "tensor")
        d_vec = v[0, :, :6, :nr].transpose(1, 0, 2).reshape(6, width).astype(F32)
        e_bias = v[:, :, 6, :nr].transpose(0, 2, 1).reshape(n_tensor, width).astype(F32)
        p_bias = v[:, :, 7, :2 * feat // n_batch].reshape(n_tensor, n_batch, 2, feat // n_batch)
        p_bias = p_bias.transpose(2, 0, 3, 1).reshape(2, n_tensor, feat).astype(F32)
        mine = partial(lax.dynamic_slice_in_dim, start_index=t * own_pairs, slice_size=own_pairs, axis=0)
        outputs, input_grad, grads, vecs, e_grad, p_grad = layer_step(
            mine(inputs), mine(lengths), mine(cotangent), w, d_vec, e_bias, p_bias
        )
        rows = own_pairs * length
        dv = jnp.broadcast_to(vecs.reshape(1, 6, n_batch, nr).transpose(0, 2, 1, 3), (n_tensor, n_batch, 6, nr))
        ev = e_grad.reshape(n_tensor, nr, n_batch).transpose(0, 2, 1)[:, :, None]
        pv = p_grad.reshape(2, n_tensor, feat // n_batch, n_batch).transpose(1, 3, 0, 2)
        pv = pv.reshape(n_tensor, n_batch, 1, 2 * feat // n_batch)
        lanes = lambda a: jnp.pad(a, ((0, 0), (0, 0), (0, 0), (0, 128 - a.shape[-1])))
        tiles = jnp.concatenate([lanes(dv), lanes(ev), lanes(pv)], axis=2)
        if fast:
            red, vred, outs, ig = scatter_all(
                grads.reshape(3, NC, NX, NZ, NY, nr, width),
                tiles.reshape(NC, NX, NZ, NY, 8, 128),
                outputs,
                input_grad.reshape(rows, NX, width // NX).transpose(1, 0, 2),
            )
            outs = outs.reshape(pairs, length, width)
            ig = lax.dynamic_slice_in_dim(ig, t % NC * feat, feat, 2)
            ig = ig.reshape(pairs, length, feat).astype(F32)
        else:
            grads = lax.psum_scatter(grads.astype(F32), "tensor", scatter_dimension=1)
            red = lax.psum_scatter(grads, "batch", scatter_dimension=1, tiled=True)
            vred = lax.psum_scatter(lax.psum_scatter(tiles, "tensor"), "batch")
            outs = lax.all_gather(outputs, "tensor").reshape(pairs, length, width)
            ig = lax.all_to_all(
                input_grad.reshape(rows, n_tensor, feat), "tensor", split_axis=1, concat_axis=0, tiled=True
            )
            ig = ig.reshape(pairs, length, feat).astype(F32)
        att_g = red[0]
        four_g = [
            jnp.concatenate([att_g[:, i * cut:(i + 1) * cut], att_g[:, 4 * cut + i * HEAD:4 * cut + (i + 1) * HEAD]], axis=1)
            for i in range(4)
        ]
        return (
            outs,
            ig,
            jnp.stack(four_g[:3]),
            vred[7, :2 * feat // n_batch].reshape(pair_bias.shape),
            four_g[3].T,
            vred[0, :nr],
            vred[1, :nr],
            vred[2, :nr],
            red[1],
            vred[6, :nr].reshape(expand_bias.shape),
            red[2].T,
            vred[3, :nr],
            vred[4, :nr],
            vred[5, :nr],
        )

    return on_device


def solution(mesh):
    return jax.shard_map(
        make_on_device(dict(mesh.shape)),
        mesh=mesh,
        in_specs=(
            P("batch", None, None),
            P("batch"),
            P(None, "batch", "tensor"),
            P(None, "tensor", "batch"),
            P("tensor", "batch"),
            P("batch"),
            P("batch"),
            P("batch"),
            P("batch", "tensor"),
            P("tensor", "batch"),
            P("tensor", "batch"),
            P("batch"),
            P("batch"),
            P("batch"),
            P("batch", None, None),
        ),
        out_specs=(
            P("batch", None, None),
            P("batch", None, "tensor"),
            P(None, "batch", "tensor"),
            P(None, "tensor", "batch"),
            P("tensor", "batch"),
            P("batch"),
            P("batch"),
            P("batch"),
            P("batch", "tensor"),
            P("tensor", "batch"),
            P("tensor", "batch"),
            P("batch"),
            P("batch"),
            P("batch"),
        ),
        check_vma=False,
    )
```

```python
from functools import partial

import jax
import jax.numpy as jnp
from jax import lax
from jax.experimental import pallas as pl
from jax.experimental.pallas import tpu as pltpu
from jax.sharding import PartitionSpec as P

HEAD = 64
EPS = 1e-12
SCALE = 0.125
MASKED = -1e30
MESH = pl.DeviceIdType.MESH
F32 = jnp.float32
BF16 = jnp.bfloat16
NZ, NY, NX, NC = 4, 2, 2, 2


class Place:
    def __init__(self):
        b = lax.axis_index("batch")
        t = lax.axis_index("tensor")
        self.z, self.y = b // NY, b % NY
        self.x, self.c = t // NC, t % NC

    def at(self, z=None, y=None, x=None, c=None):
        z = self.z if z is None else z
        y = self.y if y is None else y
        x = self.x if x is None else x
        c = self.c if c is None else c
        return (z * NY + y, x * NC + c)

    def core(self):
        return self.at(c=1 - self.c)

    def xp(self):
        return self.at(x=1 - self.x)

    def yp(self):
        return self.at(y=1 - self.y)

    def zp(self, step):
        return self.at(z=(self.z + step) % NZ)

    def greet(self):
        barrier = pltpu.get_barrier_semaphore()
        peers = [self.core(), self.xp(), self.yp()] + [self.zp(s) for s in range(1, NZ)]
        for peer in peers:
            pl.semaphore_signal(barrier, inc=1, device_id=peer, device_id_type=MESH)
        pl.semaphore_wait(barrier, len(peers))


def remote(src, dst, sems, index, peer):
    return pltpu.make_async_remote_copy(
        src_ref=src,
        dst_ref=dst,
        send_sem=sems.at[0, index],
        recv_sem=sems.at[1, index],
        device_id=peer,
        device_id_type=MESH,
    )


def gather_kernel(pack_ref, vec_ref, w_ref, v_ref, sems, vsems, lsems):
    me = Place()
    z, y, x, c = me.z, me.y, me.x, me.c
    packs = pack_ref.shape[0]
    half = pack_ref.shape[2] // 2
    lo, hi = pl.ds(0, half), pl.ds(half, half)
    own = [
        pltpu.make_async_copy(pack_ref.at[p], w_ref.at[p, c, x, z, y], lsems.at[p])
        for p in range(packs)
    ]
    own_vec = pltpu.make_async_copy(vec_ref, v_ref.at[c, x, z, y], lsems.at[packs])
    for copy in own:
        copy.start()
    own_vec.start()
    me.greet()
    started = []

    def send(src, dst, table, index, peer):
        copy = remote(src, dst, table, index, peer)
        copy.start()
        started.append(copy)
        return copy

    own_vec.wait()
    first = []
    vfirst = [
        send(v_ref.at[c, x, z, y], v_ref.at[c, x, z, y], vsems, s - 1, me.zp(s))
        for s in range(1, NZ)
    ]
    for p in range(packs):
        own[p].wait()
        slot = w_ref.at[p, c, x, z, y]
        first.append([send(slot, slot, sems, 8 * p + s - 1, me.zp(s)) for s in range(1, NZ)])
    for copy in vfirst:
        copy.wait_recv()
    slot = v_ref.at[c, x, :, y]
    vx = send(slot, slot, vsems, 3, me.xp())
    second = []

    def stage2(p):
        for copy in first[p]:
            copy.wait_recv()
        a = w_ref.at[p, c, x, :, y, :, lo]
        b = w_ref.at[p, c, x, :, y, :, hi]
        second.append((send(a, a, sems, 8 * p + 3, me.xp()), send(b, b, sems, 8 * p + 4, me.yp())))

    third = []

    def stage3(p):
        for copy in second[p]:
            copy.wait_recv()
        a = w_ref.at[p, c, :, :, y, :, lo]
        b = w_ref.at[p, c, x, :, :, :, hi]
        third.append((send(a, a, sems, 8 * p + 5, me.yp()), send(b, b, sems, 8 * p + 6, me.xp())))

    fourth = []

    def stage4(p):
        for copy in third[p]:
            copy.wait_recv()
        a = w_ref.at[p, c]
        fourth.append(send(a, a, sems, 8 * p + 7, me.core()))

    stage2(0)
    vx.wait_recv()
    slot = v_ref.at[c, :, :, y]
    vy = send(slot, slot, vsems, 4, me.yp())
    stage3(0)
    vy.wait_recv()
    slot = v_ref.at[c]
    vc = send(slot, slot, vsems, 5, me.core())
    for p in range(1, packs):
        stage2(p)
        stage4(p - 1)
        stage3(p)
    stage4(packs - 1)
    vc.wait_recv()
    for copy in fourth:
        copy.wait_recv()
    for copy in started:
        copy.wait_send()


def gather_all(pack, vec):
    packs, nr, width = pack.shape
    shape = (packs, NC, NX, NZ, NY, nr, width)
    vshape = (NC, NX, NZ, NY) + vec.shape
    return pl.pallas_call(
        gather_kernel,
        out_shape=(jax.ShapeDtypeStruct(shape, BF16), jax.ShapeDtypeStruct(vshape, BF16)),
        in_specs=[pl.BlockSpec(memory_space=pltpu.VMEM)] * 2,
        out_specs=(pl.BlockSpec(memory_space=pltpu.VMEM),) * 2,
        scratch_shapes=[
            pltpu.SemaphoreType.DMA((2, 8 * packs)),
            pltpu.SemaphoreType.DMA((2, 6)),
            pltpu.SemaphoreType.DMA((packs + 1,)),
        ],
        compiler_params=pltpu.CompilerParams(
            collective_id=0, has_side_effects=True, vmem_limit_bytes=60 << 20
        ),
    )(pack, vec)


YFIRST = 640


def scatter_kernel(
    g_in, v_in, out_in, ig_in,
    red_ref, vred_ref, outs_ref, ig_ref,
    g_ref, v_ref, rc, ry0, rx1, rx0, ry1, rz, vc, vy, vx, vz,
    sems, vsems, osems, lsems,
):
    me = Place()
    z, y, x, c = me.z, me.y, me.x, me.c
    packs = g_in.shape[0]
    width = g_in.shape[-1]
    lo, hi = pl.ds(0, YFIRST), pl.ds(YFIRST, width - YFIRST)
    order = list(reversed(range(packs)))
    loads = [pltpu.make_async_copy(g_in.at[p], g_ref.at[p], lsems.at[p]) for p in range(packs)]
    for p in order:
        loads[p].start()
    load_v = pltpu.make_async_copy(v_in, v_ref, lsems.at[packs])
    load_v.start()
    rows = pl.ds(0, 1)
    t_own = x * NC + c
    out_own = pltpu.make_async_copy(out_in, outs_ref.at[t_own], lsems.at[packs + 1])
    out_own.start()
    ig_own = pltpu.make_async_copy(ig_in.at[x], ig_ref.at[t_own], lsems.at[packs + 2])
    ig_own.start()
    me.greet()
    started = []

    def send(src, dst, table, index, peer):
        copy = remote(src, dst, table, index, peer)
        copy.start()
        started.append(copy)
        return copy

    def add(dst, src, at):
        @pl.loop(0, dst.shape[0])
        def _(i):
            dst[i] = dst[i] + src[i]

    ox = send(out_in, outs_ref.at[t_own], osems, 0, me.xp())
    oc = send(out_in, outs_ref.at[t_own], osems, 1, me.core())
    ix = send(ig_in.at[1 - x], ig_ref.at[t_own], osems, 2, me.xp())
    ic = send(ig_in.at[x], ig_ref.at[t_own], osems, 3, me.core())

    cs = {}
    for p in order:
        loads[p].wait()
        cs[p] = send(g_ref.at[p, 1 - c], rc.at[p], sems, 6 * p, me.core())
    load_v.wait()
    vcs = send(v_ref.at[1 - c], vc, vsems, 0, me.core())
    s1, s2 = {}, {}

    def stage1(p):
        cs[p].wait_recv()
        for i in range(NX):
            for j in range(NZ):
                for k in range(NY):
                    g_ref[p, c, i, j, k] = g_ref[p, c, i, j, k] + rc[p, i, j, k]
        s1[p] = (
            send(g_ref.at[p, c, :, :, 1 - y, :, lo], ry0.at[p], sems, 6 * p + 1, me.yp()),
            send(g_ref.at[p, c, 1 - x, :, :, :, hi], rx1.at[p], sems, 6 * p + 2, me.xp()),
        )

    def stage2(p):
        for copy in s1[p]:
            copy.wait_recv()
        for j in range(NZ):
            for i in range(NX):
                g_ref[p, c, i, j, y, :, lo] = g_ref[p, c, i, j, y, :, lo] + ry0[p, i, j]
            for k in range(NY):
                g_ref[p, c, x, j, k, :, hi] = g_ref[p, c, x, j, k, :, hi] + rx1[p, j, k]
        s2[p] = (
            send(g_ref.at[p, c, 1 - x, :, y, :, lo], rx0.at[p], sems, 6 * p + 3, me.xp()),
            send(g_ref.at[p, c, x, :, 1 - y, :, hi], ry1.at[p], sems, 6 * p + 4, me.yp()),
        )

    s3 = {}

    def stage3(p):
        for copy in s2[p]:
            copy.wait_recv()
        for j in range(NZ):
            g_ref[p, c, x, j, y, :, lo] = g_ref[p, c, x, j, y, :, lo] + rx0[p, j]
            g_ref[p, c, x, j, y, :, hi] = g_ref[p, c, x, j, y, :, hi] + ry1[p, j]
        s3[p] = []
        for s in range(1, NZ):
            s3[p].append(
                send(
                    g_ref.at[p, c, x, (z + s) % NZ, y], rz.at[p, s - 1],
                    sems, 6 * packs + 3 * p + s - 1, me.zp(s),
                )
            )

    def stage4(p):
        for copy in s3[p]:
            copy.wait_recv()
        total = g_ref[p, c, x, z, y].astype(F32)
        for s in range(1, NZ):
            total = total + rz[p, s - 1].astype(F32)
        red_ref[p] = total

    for i, p in enumerate(order):
        stage1(p)
    vcs.wait_recv()
    for i in range(NX):
        v_ref[c, i] = v_ref[c, i] + vc[i]
    vys = send(v_ref.at[c, :, :, 1 - y], vy, vsems, 1, me.yp())
    for p in order:
        stage2(p)
    vys.wait_recv()
    for i in range(NX):
        for j in range(NZ):
            v_ref[c, i, j, y] = v_ref[c, i, j, y] + vy[i, j]
    vxs = send(v_ref.at[c, 1 - x, :, y], vx, vsems, 2, me.xp())
    for p in order:
        stage3(p)
    vxs.wait_recv()
    for j in range(NZ):
        v_ref[c, x, j, y] = v_ref[c, x, j, y] + vx[j]
    vzs = [
        send(v_ref.at[c, x, (z + s) % NZ, y], vz.at[s - 1], vsems, 2 + s, me.zp(s))
        for s in range(1, NZ)
    ]
    t_x = (1 - x) * NC + c
    ox.wait_recv()
    of = send(outs_ref.at[t_x], outs_ref.at[t_x], osems, 4, me.core())
    ix.wait_recv()
    jf = send(ig_ref.at[t_x], ig_ref.at[t_x], osems, 5, me.core())
    for p in order:
        stage4(p)
    for copy in vzs:
        copy.wait_recv()
    total = v_ref[c, x, z, y]
    for s in range(1, NZ):
        total = total + vz[s - 1]
    vred_ref[...] = total
    for copy in (oc, ic, of, jf):
        copy.wait_recv()
    for copy in started:
        copy.wait_send()
    out_own.wait()
    ig_own.wait()


def scatter_all(g, v, out, ig):
    packs, width = g.shape[0], g.shape[-1]
    nr = g.shape[-2]
    rows = out.shape[0]
    rest = width - YFIRST
    return pl.pallas_call(
        scatter_kernel,
        out_shape=(
            jax.ShapeDtypeStruct((packs, nr, width), F32),
            jax.ShapeDtypeStruct(v.shape[-2:], F32),
            jax.ShapeDtypeStruct((NX * NC, rows, width), BF16),
            jax.ShapeDtypeStruct((NX * NC, rows, width // NX), BF16),
        ),
        in_specs=[pl.BlockSpec(memory_space=pl.ANY)] * 4,
        out_specs=(
            pl.BlockSpec(memory_space=pltpu.VMEM),
            pl.BlockSpec(memory_space=pltpu.VMEM),
            pl.BlockSpec(memory_space=pl.ANY),
            pl.BlockSpec(memory_space=pl.ANY),
        ),
        scratch_shapes=[
            pltpu.VMEM(g.shape, BF16),
            pltpu.VMEM(v.shape, F32),
            pltpu.VMEM((packs, NX, NZ, NY, nr, width), BF16),
            pltpu.VMEM((packs, NX, NZ, nr, YFIRST), BF16),
            pltpu.VMEM((packs, NZ, NY, nr, rest), BF16),
            pltpu.VMEM((packs, NZ, nr, YFIRST), BF16),
            pltpu.VMEM((packs, NZ, nr, rest), BF16),
            pltpu.VMEM((packs, NZ - 1, nr, width), BF16),
            pltpu.VMEM((NX, NZ, NY) + v.shape[-2:], F32),
            pltpu.VMEM((NX, NZ) + v.shape[-2:], F32),
            pltpu.VMEM((NZ,) + v.shape[-2:], F32),
            pltpu.VMEM((NZ - 1,) + v.shape[-2:], F32),
            pltpu.SemaphoreType.DMA((2, 9 * packs)),
            pltpu.SemaphoreType.DMA((2, 6)),
            pltpu.SemaphoreType.DMA((2, 6)),
            pltpu.SemaphoreType.DMA((packs + 3,)),
        ],
        compiler_params=pltpu.CompilerParams(
            collective_id=1, has_side_effects=True, vmem_limit_bytes=60 << 20
        ),
    )(g, v, out, ig)


def normalize(value_rows, gain, shift):
    centred = value_rows - jnp.mean(value_rows, axis=-1, keepdims=True)
    scaled = lax.rsqrt(jnp.mean(centred * centred, axis=-1, keepdims=True) + EPS)
    normed = centred * scaled
    return (normed * gain + shift, normed, scaled)


def normalize_back(grad, normed, scaled, gain):
    weighted = grad * gain
    inner = jnp.mean(weighted * normed, axis=-1, keepdims=True)
    return scaled * (weighted - jnp.mean(weighted, axis=-1, keepdims=True) - normed * inner)


SQRT_HALF = 0.7071067811865476
INV_SQRT_2PI = 0.3989422804014327
ERF_P = 0.3275911
ERF_A = (0.254829592, -0.284496736, 1.421413741, -1.453152027, 1.061405429)
TILE = 96
CUT = 2 * HEAD


def dot(a, b):
    return lax.dot_general(a, b, (((1,), (0,)), ((), ())), preferred_element_type=F32)


def dot_nt(a, b):
    return lax.dot_general(a, b, (((1,), (1,)), ((), ())), preferred_element_type=F32)


def gelu_parts(v):
    size = jnp.abs(v) * SQRT_HALF
    t = 1.0 / (1.0 + ERF_P * size)
    bell = jnp.exp(-0.5 * v * v)
    poly = ERF_A[4]
    for a in ERF_A[3::-1]:
        poly = poly * t + a
    tail = 0.5 * poly * t * bell
    phi = jnp.where(v < 0.0, tail, 1.0 - tail)
    return v * phi, phi + v * bell * INV_SQRT_2PI


def low_lanes():
    return lax.broadcasted_iota(jnp.int32, (1, CUT), 1) < HEAD


def half_rows():
    lane = lax.broadcasted_iota(jnp.int32, (1, CUT), 1)
    low = jnp.where(lane < HEAD, 1.0, 0.0)
    return low.astype(BF16), (1.0 - low).astype(BF16)


def swap(a):
    return pltpu.roll(a, HEAD, 1)


def sel_matrix(key, b):
    lane = lax.broadcasted_iota(jnp.int32, (128, key.shape[1]), 0) * (NZ * NY) + b
    return jnp.where(lane == key, 1.0, 0.0).astype(BF16)


def sel_keys(width):
    col = lax.broadcasted_iota(jnp.int32, (1, width), 1)
    nr = width // (NZ * NY)
    q = jnp.where(col < CUT, col, col - 3 * CUT)
    v = jnp.where(col < 3 * CUT, col - 2 * CUT, col - 4 * CUT)
    is_q = (col < CUT) | ((col >= 4 * CUT) & (col < 4 * CUT + HEAD))
    is_v = ((col >= 2 * CUT) & (col < 3 * CUT)) | ((col >= 5 * CUT) & (col < 5 * CUT + HEAD))
    head = jnp.where(is_q, q, jnp.where(is_v, v + 3 * HEAD, -1))
    return (col % nr) * (NZ * NY) + col // nr, col, head


class Layer:
    def __init__(self, **refs):
        self.__dict__.update(refs)
        self.tiles = self.x.shape[0]
        self.width = self.x.shape[2]
        self.rows = self.tiles * TILE
        self.seqs = self.qkv.shape[2]
        self.length = self.qkv.shape[3]
        self.per = self.length // TILE

    def weight(self, p, t, lo, size):
        c, x = t // NX, t % NX
        return self.w[p, c, x, :, :, :, lo:lo + size].reshape(self.width, size)

    def put_weight(self, p, t, lo, value):
        c, x = t // NX, t % NX
        size = value.shape[1]
        nr = self.width // (NZ * NY)
        self.w[p, c, x, :, :, :, lo:lo + size] = value.astype(BF16).reshape(NZ, NY, nr, size)

    def all_rows(self, ref, *at):
        a = ref[at] if at else ref[...]
        return a.reshape(self.rows, a.shape[-1])

    def seq_rows(self, ref, s, *at):
        a = ref[at + (pl.ds(self.per * s, self.per),)]
        return a.reshape(self.length, a.shape[-1])

    def transposed(self, ref, out):
        a = self.all_rows(ref)
        out[0:self.width, :] = a.T
        out[self.width:, :] = jnp.ones((out.shape[0] - self.width, self.rows), BF16)

    def vectors(self):
        keys = sel_keys(self.width)
        self.vec[...] = jnp.zeros(self.vec.shape, F32)

        @pl.loop(0, NZ * NY)
        def _(b):
            z, y = b // NY, b % NY
            own = self.v[:, :, z, y].reshape(NC * NX * 16, 128)
            for i, key in enumerate(keys):
                part = dot(own, sel_matrix(key, b)).reshape(NC * NX, 16, self.width)
                self.vec[i] = self.vec[i] + part

    def row(self, i):
        return self.vec[0, 0, i:i + 1, :]

    def projections(self):
        low = low_lanes()

        @pl.loop(0, NC)
        def _(u):
            third = []
            for d in range(NX):
                t = NX * u + d
                xv = self.all_rows(self.x)
                for n in range(3):
                    a = dot(xv, self.weight(0, t, 256 * n, 256)) + self.vec[2, t, 7:8, 256 * n:256 * n + 256]
                    if n == 2:
                        third.append(a)
                    else:
                        for h in range(2 if n == 0 else 1):
                            part = a[:, CUT * h:CUT * h + CUT].astype(BF16)
                            self.qkv[2 * n + h, t] = part.reshape(self.seqs, self.length, CUT)
            a, b = third
            q = jnp.where(low, a[:, :CUT], swap(b[:, :CUT]))
            k = jnp.where(low, swap(a[:, :CUT]), b[:, :CUT])
            v = jnp.where(low, a[:, CUT:], swap(b[:, CUT:]))
            for i, part in enumerate((q, k, v)):
                self.qkv[i, NC * NX + u] = part.astype(BF16).reshape(self.seqs, self.length, CUT)

    def heads(self, p, s):
        halves = half_rows()
        q, k, v = (self.qkv[i, p, s] for i in range(3))
        valid = lax.broadcasted_iota(jnp.int32, (1, self.length), 1) < self.lens[self.first + s]
        context = []
        for j in range(2):
            scores = jnp.where(valid, dot_nt(q * halves[j], k) * SCALE, MASKED)
            powers = jnp.exp(scores - jnp.max(scores, axis=1, keepdims=True))
            probs = (powers * (1.0 / jnp.sum(powers, axis=1, keepdims=True))).astype(BF16)
            self.probs[p, s, j] = probs
            context.append(dot(probs, v))
        return jnp.where(low_lanes(), *context)

    def put_context(self, t, s, lo, value):
        value = value.astype(BF16).reshape(self.per, TILE, CUT)
        self.ctx[t, pl.ds(self.per * s, self.per), :, lo:lo + CUT] = value

    def attention_first(self):
        @pl.loop(0, NC * NX * self.seqs)
        def _(i):
            t, s = i // self.seqs, i % self.seqs
            self.put_context(t, s, 0, self.heads(t, s))

    def attention_third(self):
        low = low_lanes()

        @pl.loop(0, NC * self.seqs)
        def _(i):
            u, s = i // self.seqs, i % self.seqs
            context = self.heads(NC * NX + u, s)
            self.put_context(NX * u, s, CUT, jnp.where(low, 0.0, swap(context)))
            self.put_context(NX * u + 1, s, CUT, jnp.where(low, 0.0, context))

    def mixer_weight(self, t):
        return jnp.concatenate([self.weight(0, t, 3 * CUT, CUT), self.weight(0, t, 5 * CUT, CUT)], axis=1)

    def put_rows(self, ref, s, value):
        ref[pl.ds(self.per * s, self.per)] = value.reshape(self.per, TILE, value.shape[1])

    def mix(self):
        @pl.loop(0, self.seqs)
        def _(s):
            total = None
            for t in range(NC * NX):
                part = dot_nt(self.seq_rows(self.ctx, s, t), self.mixer_weight(t))
                total = part if total is None else total + part
            self.put_rows(self.tmp, s, total)

    def norm_first(self):
        @pl.loop(0, self.tiles)
        def _(i):
            total = self.x[i].astype(F32) + self.tmp[i] + self.row(0)
            _, normed, scaled = normalize(total, 1.0, 0.0)
            self.norm[i] = normed
            self.scaled[i] = scaled
            self.hidden[i] = (normed * self.row(1) + self.row(2)).astype(BF16)

    def expand(self):
        @pl.loop(0, NC * NX)
        def _(t):
            hidden = self.all_rows(self.hidden)
            for n in range(3):
                cols = slice(256 * n, 256 * n + 256)
                before = dot(hidden, self.weight(1, t, 256 * n, 256)) + self.vec[1, t, 6:7, cols]
                act, slope = gelu_parts(before)
                self.act[t, :, :, cols] = act.astype(BF16).reshape(self.tiles, TILE, 256)
                self.slope[t, :, :, cols] = slope.astype(BF16).reshape(self.tiles, TILE, 256)

    def times_back(self, p, ref):
        @pl.loop(0, self.seqs)
        def _(s):
            total = None
            for t in range(NC * NX):
                part = dot_nt(self.seq_rows(ref, s, t), self.weight(p, t, 0, self.width))
                total = part if total is None else total + part
            self.put_rows(self.tmp, s, total)

    def add_sum(self, i, value):
        self.sums[i] = self.sums[i] + jnp.sum(value.reshape(TILE // 8, 8, self.width), axis=0)

    def clear_sums(self):
        self.sums[...] = jnp.zeros(self.sums.shape, F32)

    def norm_second(self):
        @pl.loop(0, self.tiles)
        def _(i):
            hidden = self.norm[i] * self.row(1) + self.row(2)
            _, normed, scaled = normalize(hidden + self.tmp[i] + self.row(3), 1.0, 0.0)
            self.out[i] = (normed * self.row(4) + self.row(5)).astype(BF16)
            up = self.cot[i].astype(F32)
            self.add_sum(4, up * normed)
            self.add_sum(5, up)
            after = normalize_back(up, normed, scaled, self.row(4))
            self.add_sum(3, after)
            self.grad[i] = after
            self.low[i] = after.astype(BF16)

    def act_back(self):
        @pl.loop(0, NC * NX)
        def _(t):
            low = self.all_rows(self.low)
            for n in range(3):
                cols = slice(256 * n, 256 * n + 256)
                up = dot(low, self.weight(2, t, 256 * n, 256)).reshape(self.tiles, TILE, 256)
                self.slope[t, :, :, cols] = (up * self.slope[t, :, :, cols].astype(F32)).astype(BF16)

    def contract_grad(self):
        @pl.loop(0, NC * NX)
        def _(t):
            left = self.left[0:self.width, :]
            for n in range(3):
                right = self.all_rows(self.act, t, slice(None), slice(None), slice(256 * n, 256 * n + 256))
                self.put_weight(2, t, 256 * n, dot(left, right))

    def expand_grad(self):
        @pl.loop(0, NC * NX)
        def _(t):
            for n in range(3):
                cols = slice(256 * n, 256 * n + 256)
                grad = dot(self.left[...], self.all_rows(self.slope, t, slice(None), slice(None), cols))
                self.put_weight(1, t, 256 * n, grad[:self.width])
                self.unit_sums[0, t, :, cols] = grad[self.width:self.width + 8]

    def norm_first_back(self):
        @pl.loop(0, self.tiles)
        def _(i):
            grad = self.grad[i] + self.tmp[i]
            normed = self.norm[i]
            self.add_sum(1, grad * normed)
            self.add_sum(2, grad)
            after = normalize_back(grad, normed, self.scaled[i], self.row(1))
            self.add_sum(0, after)
            self.grad[i] = after
            self.low[i] = after.astype(BF16)

    def context_back(self):
        low = low_lanes()

        @pl.loop(0, NC)
        def _(u):
            third = []
            for d in range(NX):
                t = NX * u + d
                grad = dot(self.all_rows(self.low), self.mixer_weight(t))
                self.cgrad[t] = grad[:, :CUT].astype(BF16).reshape(self.seqs, self.length, CUT)
                third.append(grad[:, CUT:])
            pair = jnp.where(low, swap(third[0]), third[1])
            self.cgrad[NC * NX + u] = pair.astype(BF16).reshape(self.seqs, self.length, CUT)

    def heads_back(self, p, s):
        halves = half_rows()
        q, k, v = (self.qkv[i, p, s] for i in range(3))
        up = self.cgrad[p, s]
        up_t = up.T
        q_t = q.T
        dq, dk, dv = [], [], []
        for j in range(2):
            probs = self.probs[p, s, j]
            dv.append(dot(up_t[HEAD * j:HEAD * j + HEAD], probs))
            weight = dot_nt(up * halves[j], v)
            wide = probs.astype(F32)
            grad = wide * (weight - jnp.sum(wide * weight, axis=1, keepdims=True))
            grad = grad.astype(BF16)
            dq.append(dot(grad, k))
            dk.append(dot(q_t[HEAD * j:HEAD * j + HEAD], grad))
        dq = jnp.where(low_lanes(), *dq) * SCALE
        dk = jnp.concatenate(dk, axis=0).T * SCALE
        dv = jnp.concatenate(dv, axis=0).T
        return dq, dk, dv

    def put_stream(self, t, s, lo, value):
        value = value.astype(BF16).reshape(self.per, TILE, CUT)
        self.act[t, pl.ds(self.per * s, self.per), :, lo:lo + CUT] = value

    def attention_back_first(self):
        @pl.loop(0, NC * NX * self.seqs)
        def _(i):
            t, s = i // self.seqs, i % self.seqs
            grads = self.heads_back(t, s)
            for j in range(3):
                self.put_stream(t, s, CUT * j, grads[j])
            self.put_stream(t, s, 3 * CUT, jnp.zeros((self.length, CUT), F32))

    def attention_back_third(self):
        low = low_lanes()

        @pl.loop(0, NC * self.seqs)
        def _(i):
            u, s = i // self.seqs, i % self.seqs
            dq, dk, dv = self.heads_back(NC * NX + u, s)
            self.put_stream(NX * u, s, 4 * CUT, jnp.where(low, dq, swap(dk)))
            self.put_stream(NX * u + 1, s, 4 * CUT, jnp.where(low, swap(dq), dk))
            self.put_stream(NX * u, s, 5 * CUT, jnp.where(low, dv, 0.0))
            self.put_stream(NX * u + 1, s, 5 * CUT, jnp.where(low, swap(dv), 0.0))

    def input_back(self):
        half = self.width // NX

        @pl.loop(0, self.tiles)
        def _(i):
            total = (self.grad[i] + self.tmp[i]).astype(BF16)
            for x in range(NX):
                self.igrad[x, i] = total[:, half * x:half * x + half]

    def attention_grad(self):
        @pl.loop(0, NC * NX)
        def _(t):
            mixer = dot(self.left2[0:self.width, :], self.all_rows(self.ctx, t))
            for n in range(3):
                cols = slice(256 * n, 256 * n + 256)
                grad = dot(self.left[...], self.all_rows(self.act, t, slice(None), slice(None), cols))
                self.unit_sums[1, t, :, cols] = grad[self.width:self.width + 8]
                grad = grad[:self.width]
                if n > 0:
                    part = mixer[:, CUT * (n - 1):CUT * n]
                    grad = jnp.concatenate([grad[:, :CUT], grad[:, CUT:] + part], axis=1)
                self.put_weight(0, t, 256 * n, grad)

    def vector_tiles(self):
        keys = sel_keys(self.width)
        rows = [jnp.sum(self.sums[i], axis=0, keepdims=True) for i in range(6)]
        rows.append(jnp.zeros((2, self.width), F32))
        parts = [jnp.concatenate(rows, axis=0)]
        for i in range(2):
            units = [self.unit_sums[i, t, 0:1, :] for t in range(NC * NX)]
            parts.append(jnp.concatenate(units + [jnp.zeros((4, self.width), F32)], axis=0))
        split = []
        for part in parts:
            high = part.astype(BF16)
            split.append(jnp.concatenate([high, (part - high.astype(F32)).astype(BF16)], axis=0))

        @pl.loop(0, NZ * NY)
        def _(b):
            z, y = b // NY, b % NY
            got = []
            for key, part in zip(keys, split):
                both = dot_nt(part, sel_matrix(key, b))
                got.append(both[:8] + both[8:])
            for t in range(NC * NX):
                self.vtiles[t // NX, t % NX, z, y] = jnp.concatenate(
                    [got[0][:6], got[1][t:t + 1], got[2][t:t + 1]], axis=0
                )


def layer_kernel(
    x_in, cot_in, lens, w_in, v_in,
    outs_ref, ig_ref, g_ref, tiles_ref,
    w, x, cot, qkv, probs, ctx, tmp, norm, scaled, hidden, act, slope, grad, low, cgrad, left, left2, vec, sums,
    unit_sums, sems,
):
    t = lax.axis_index("tensor")
    seqs = qkv.shape[2]
    loads = [
        pltpu.make_async_copy(w_in.at[p], w.at[p], sems.at[p]) for p in range(3)
    ] + [
        pltpu.make_async_copy(x_in.at[t], x, sems.at[3]),
        pltpu.make_async_copy(cot_in.at[t], cot, sems.at[4]),
    ]
    for copy in loads:
        copy.start()
    layer = Layer(
        w=w, x=x, cot=cot, qkv=qkv, probs=probs, ctx=ctx, tmp=tmp, norm=norm, scaled=scaled, hidden=hidden, act=act,
        slope=slope, grad=grad, low=low, cgrad=cgrad, left=left, left2=left2, vec=vec, sums=sums, unit_sums=unit_sums,
        v=v_in, out=outs_ref, igrad=ig_ref, vtiles=tiles_ref, lens=lens, first=t * seqs,
    )
    layer.vectors()
    layer.clear_sums()
    for copy in loads:
        copy.wait()
    layer.projections()
    layer.attention_first()
    layer.attention_third()
    layer.mix()
    layer.norm_first()
    layer.expand()
    layer.times_back(2, act)
    layer.norm_second()
    layer.transposed(low, left)
    layer.act_back()
    layer.contract_grad()
    layer.times_back(1, slope)
    layer.transposed(hidden, left)
    layer.expand_grad()
    layer.norm_first_back()
    layer.transposed(low, left2)
    layer.context_back()
    layer.attention_back_first()
    layer.attention_back_third()
    layer.times_back(0, act)
    layer.input_back()
    layer.transposed(x, left)
    layer.attention_grad()
    layer.vector_tiles()
    stores = [pltpu.make_async_copy(w.at[p], g_ref.at[p], sems.at[p]) for p in range(3)]
    for copy in stores:
        copy.start()
    for copy in stores:
        copy.wait()


def layer_scratch(seqs, length, width):
    tiles = seqs * length // TILE
    blocks = NC * NX
    pairs = 3 * blocks // 2
    rows = seqs * length
    nr = width // (NZ * NY)
    return [
        pltpu.VMEM((3, NC, NX, NZ, NY, nr, width), BF16),
        pltpu.VMEM((tiles, TILE, width), BF16),
        pltpu.VMEM((tiles, TILE, width), BF16),
        pltpu.VMEM((3, pairs, seqs, length, CUT), BF16),
        pltpu.VMEM((pairs, seqs, 2, length, length), BF16),
        pltpu.VMEM((blocks, tiles, TILE, 2 * CUT), BF16),
        pltpu.VMEM((tiles, TILE, width), F32),
        pltpu.VMEM((tiles, TILE, width), F32),
        pltpu.VMEM((tiles, TILE, 1), F32),
        pltpu.VMEM((tiles, TILE, width), BF16),
        pltpu.VMEM((blocks, tiles, TILE, width), BF16),
        pltpu.VMEM((blocks, tiles, TILE, width), BF16),
        pltpu.VMEM((tiles, TILE, width), F32),
        pltpu.VMEM((tiles, TILE, width), BF16),
        pltpu.VMEM((pairs, seqs, length, CUT), BF16),
        pltpu.VMEM((width + 16, rows), BF16),
        pltpu.VMEM((width + 16, rows), BF16),
        pltpu.VMEM((3, blocks, 16, width), F32),
        pltpu.VMEM((6, 8, width), F32),
        pltpu.VMEM((2, blocks, 8, width), F32),
    ]


def layer_call(x, cot, lengths, w, v, seqs):
    pairs, length, width = x.shape
    tiles = seqs * length // TILE
    shape = (NX * NC, tiles, TILE, width)
    vmem = pl.BlockSpec(memory_space=pltpu.VMEM)
    hbm = pl.BlockSpec(memory_space=pl.ANY)
    return pl.pallas_call(
        layer_kernel,
        out_shape=(
            jax.ShapeDtypeStruct((tiles, TILE, width), BF16),
            jax.ShapeDtypeStruct((NX, tiles, TILE, width // NX), BF16),
            jax.ShapeDtypeStruct(w.shape, BF16),
            jax.ShapeDtypeStruct((NC, NX, NZ, NY, 8, 128), F32),
        ),
        in_specs=[hbm, hbm, pl.BlockSpec(memory_space=pltpu.SMEM), hbm, vmem],
        out_specs=(vmem, vmem, hbm, vmem),
        scratch_shapes=layer_scratch(seqs, length, width) + [pltpu.SemaphoreType.DMA((5,))],
        compiler_params=pltpu.CompilerParams(vmem_limit_bytes=63 << 20),
    )(x.reshape(shape), cot.reshape(shape), lengths, w, v)


def layer_step(x_seq, lengths, cot, w, d_vec, e_bias, p_bias):
    seqs, length, width = x_seq.shape
    rows = seqs * length
    blocks = w.shape[1]
    feat = width // blocks
    heads = feat // HEAD
    mixer_shift, gain_one, shift_one, contract_shift, gain_two, shift_two = d_vec
    x = x_seq.reshape(rows, width)
    att = w[0]
    cut = 2 * HEAD
    def columns(i):
        return jnp.concatenate(
            [att[:, :, i * cut:(i + 1) * cut], att[:, :, 4 * cut + i * HEAD:4 * cut + (i + 1) * HEAD]], axis=2
        )
    wq, wk, wv, wm = (columns(i) for i in range(4))
    def project(weight, bias):
        out = jnp.einsum("rd,tde->rte", x, weight, preferred_element_type=F32)
        if bias is not None:
            out = out + bias
        return out.astype(BF16).reshape(seqs, length, blocks * heads, HEAD)
    queries = project(wq, p_bias[0])
    keys = project(wk, None)
    values = project(wv, p_bias[1])
    valid = lax.broadcasted_iota(jnp.int32, (seqs, 1, 1, length), 3) < lengths[:, None, None, None]
    raw = jnp.einsum("sqhd,skhd->shqk", queries, keys, preferred_element_type=F32) * SCALE
    raw = jnp.where(valid, raw, MASKED)
    peak = jnp.max(raw, axis=-1, keepdims=True)
    powers = jnp.exp(raw - peak)
    probs = powers / jnp.sum(powers, axis=-1, keepdims=True)
    attention = probs.astype(BF16)
    context = jnp.einsum("shqk,skhd->sqhd", attention, values, preferred_element_type=F32)
    context = context.astype(BF16).reshape(rows, blocks, feat)
    mixed = jnp.einsum("rtc,tdc->rd", context, wm, preferred_element_type=F32)
    hidden, normed_one, scaled_one = normalize(x.astype(F32) + mixed + mixer_shift, gain_one, shift_one)
    hidden_low = hidden.astype(BF16)
    before = jnp.einsum("rd,tdf->rtf", hidden_low, w[1], preferred_element_type=F32) + e_bias
    activated = jax.nn.gelu(before, approximate=False).astype(BF16)
    branch = jnp.einsum("rtf,tdf->rd", activated, w[2], preferred_element_type=F32)
    result, normed_two, scaled_two = normalize(hidden + branch + contract_shift, gain_two, shift_two)
    outputs = result.astype(BF16)
    up = cot.reshape(rows, width).astype(F32)
    gain_two_grad = jnp.sum(up * normed_two, axis=0)
    shift_two_grad = jnp.sum(up, axis=0)
    after_two = normalize_back(up, normed_two, scaled_two, gain_two)
    contract_shift_grad = jnp.sum(after_two, axis=0)
    two_low = after_two.astype(BF16)
    contract_grad = jnp.einsum("rd,rtf->tdf", two_low, activated, preferred_element_type=F32)
    act_grad = jnp.einsum("rd,tdf->rtf", two_low, w[2], preferred_element_type=F32)
    _, gelu_back = jax.vjp(partial(jax.nn.gelu, approximate=False), before)
    before_grad = gelu_back(act_grad)[0].astype(BF16)
    expand_grad = jnp.einsum("rd,rtf->tdf", hidden_low, before_grad, preferred_element_type=F32)
    e_bias_grad = jnp.sum(before_grad, axis=0, dtype=F32)
    hidden_part = jnp.einsum("rtf,tdf->rd", before_grad, w[1], preferred_element_type=F32)
    hidden_grad = after_two + hidden_part
    after_one = normalize_back(hidden_grad, normed_one, scaled_one, gain_one)
    gain_one_grad = jnp.sum(hidden_grad * normed_one, axis=0)
    shift_one_grad = jnp.sum(hidden_grad, axis=0)
    mixer_shift_grad = jnp.sum(after_one, axis=0)
    one_low = after_one.astype(BF16)
    mixer_grad = jnp.einsum("rd,rtc->tdc", one_low, context, preferred_element_type=F32)
    context_grad = jnp.einsum("rd,tdc->rtc", one_low, wm, preferred_element_type=F32).astype(BF16)
    context_grad = context_grad.reshape(seqs, length, blocks * heads, HEAD)
    value_grad = jnp.einsum("shqk,sqhd->skhd", attention, context_grad, preferred_element_type=F32)
    weight_grad = jnp.einsum("sqhd,skhd->shqk", context_grad, values, preferred_element_type=F32)
    score_grad = probs * (weight_grad - jnp.sum(probs * weight_grad, axis=-1, keepdims=True))
    score_grad = score_grad.astype(BF16)
    query_grad = jnp.einsum("shqk,skhd->sqhd", score_grad, keys, preferred_element_type=F32) * SCALE
    key_grad = jnp.einsum("shqk,sqhd->skhd", score_grad, queries, preferred_element_type=F32) * SCALE
    streams = [g.astype(BF16).reshape(rows, blocks, feat) for g in (query_grad, key_grad, value_grad)]
    p_grad = [jnp.sum(streams[i], axis=0, dtype=F32) for i in (0, 2)]
    tgrads = [jnp.einsum("rd,rte->tde", x, s, preferred_element_type=F32) for s in streams] + [mixer_grad]
    att_grad = jnp.concatenate([g[:, :, :cut] for g in tgrads] + [g[:, :, cut:] for g in tgrads], axis=2)
    part = sum(
        jnp.einsum("rte,tde->rd", s, wt, preferred_element_type=F32) for s, wt in zip(streams, (wq, wk, wv))
    )
    input_grad = (after_one + part).astype(BF16)
    grads = jnp.stack([att_grad, expand_grad, contract_grad]).astype(BF16)
    vecs = jnp.stack(
        [mixer_shift_grad, gain_one_grad, shift_one_grad, contract_shift_grad, gain_two_grad, shift_two_grad]
    )
    return outputs, input_grad, grads, vecs, e_bias_grad, jnp.stack(p_grad)


def make_on_device(sizes):
    fast = sizes == {"batch": NZ * NY, "tensor": NX * NC}

    def on_device(
        inputs, lengths, triple_weight, pair_bias, mixer_weight, mixer_bias, first_gain, first_shift,
        expand_weight, expand_bias, contract_weight, contract_bias, second_gain, second_shift, cotangent,
    ):
        pairs, length, width = inputs.shape
        n_tensor, n_batch = sizes["tensor"], sizes["batch"]
        nr = width // n_batch
        own_pairs = pairs // n_tensor
        t = lax.axis_index("tensor")
        cut = 2 * HEAD
        four = [triple_weight[0], triple_weight[1], triple_weight[2], mixer_weight.T]
        att = jnp.concatenate([m[:, :cut] for m in four] + [m[:, cut:] for m in four], axis=1)
        pack = jnp.stack([att, expand_weight, contract_weight.T])
        def row(v):
            return jnp.pad(v.reshape(1, -1), ((0, 0), (0, 128 - v.size)))
        vec = jnp.concatenate(
            [row(v) for v in (mixer_bias, first_gain, first_shift, contract_bias, second_gain, second_shift,
                              expand_bias, pair_bias)] + [jnp.zeros((8, 128), BF16)], axis=0
        )
        feat = width // n_tensor
        if fast:
            w, v = gather_all(pack, vec)
            outputs, input_grad, grads, tiles = layer_call(inputs, cotangent, lengths, w, v, own_pairs)
            rows = own_pairs * length
            outputs = outputs.reshape(rows, width)
            input_grad = input_grad.reshape(NX, rows, width // NX)
        else:
            w = lax.all_gather(lax.all_gather(pack, "batch", axis=1, tiled=True), "tensor", axis=1)
            v = lax.all_gather(lax.all_gather(vec, "batch"), "tensor")
            d_vec = v[0, :, :6, :nr].transpose(1, 0, 2).reshape(6, width).astype(F32)
            e_bias = v[:, :, 6, :nr].transpose(0, 2, 1).reshape(n_tensor, width).astype(F32)
            p_bias = v[:, :, 7, :2 * feat // n_batch].reshape(n_tensor, n_batch, 2, feat // n_batch)
            p_bias = p_bias.transpose(2, 0, 3, 1).reshape(2, n_tensor, feat).astype(F32)
            mine = partial(lax.dynamic_slice_in_dim, start_index=t * own_pairs, slice_size=own_pairs, axis=0)
            outputs, input_grad, grads, vecs, e_grad, p_grad = layer_step(
                mine(inputs), mine(lengths), mine(cotangent), w, d_vec, e_bias, p_bias
            )
            rows = own_pairs * length
            dv = jnp.broadcast_to(vecs.reshape(1, 6, n_batch, nr).transpose(0, 2, 1, 3), (n_tensor, n_batch, 6, nr))
            ev = e_grad.reshape(n_tensor, nr, n_batch).transpose(0, 2, 1)[:, :, None]
            pv = p_grad.reshape(2, n_tensor, feat // n_batch, n_batch).transpose(1, 3, 0, 2)
            pv = pv.reshape(n_tensor, n_batch, 1, 2 * feat // n_batch)
            lanes = lambda a: jnp.pad(a, ((0, 0), (0, 0), (0, 0), (0, 128 - a.shape[-1])))
            tiles = jnp.concatenate([lanes(dv), lanes(ev), lanes(pv)], axis=2)
        if fast:
            red, vred, outs, ig = scatter_all(
                grads, tiles, outputs, input_grad,
            )
            outs = outs.reshape(pairs, length, width)
            ig = lax.dynamic_slice_in_dim(ig, t % NC * feat, feat, 2)
            ig = ig.reshape(pairs, length, feat).astype(F32)
        else:
            grads = lax.psum_scatter(grads.astype(F32), "tensor", scatter_dimension=1)
            red = lax.psum_scatter(grads, "batch", scatter_dimension=1, tiled=True)
            vred = lax.psum_scatter(lax.psum_scatter(tiles, "tensor"), "batch")
            outs = lax.all_gather(outputs, "tensor").reshape(pairs, length, width)
            ig = lax.all_to_all(
                input_grad.reshape(rows, n_tensor, feat), "tensor", split_axis=1, concat_axis=0, tiled=True
            )
            ig = ig.reshape(pairs, length, feat).astype(F32)
        att_g = red[0]
        four_g = [
            jnp.concatenate([att_g[:, i * cut:(i + 1) * cut], att_g[:, 4 * cut + i * HEAD:4 * cut + (i + 1) * HEAD]], axis=1)
            for i in range(4)
        ]
        return (
            outs,
            ig,
            jnp.stack(four_g[:3]),
            vred[7, :2 * feat // n_batch].reshape(pair_bias.shape),
            four_g[3].T,
            vred[0, :nr],
            vred[1, :nr],
            vred[2, :nr],
            red[1],
            vred[6, :nr].reshape(expand_bias.shape),
            red[2].T,
            vred[3, :nr],
            vred[4, :nr],
            vred[5, :nr],
        )

    return on_device


def solution(mesh):
    return jax.shard_map(
        make_on_device(dict(mesh.shape)),
        mesh=mesh,
        in_specs=(
            P("batch", None, None),
            P("batch"),
            P(None, "batch", "tensor"),
            P(None, "tensor", "batch"),
            P("tensor", "batch"),
            P("batch"),
            P("batch"),
            P("batch"),
            P("batch", "tensor"),
            P("tensor", "batch"),
            P("tensor", "batch"),
            P("batch"),
            P("batch"),
            P("batch"),
            P("batch", None, None),
        ),
        out_specs=(
            P("batch", None, None),
            P("batch", None, "tensor"),
            P(None, "batch", "tensor"),
            P(None, "tensor", "batch"),
            P("tensor", "batch"),
            P("batch"),
            P("batch"),
            P("batch"),
            P("batch", "tensor"),
            P("tensor", "batch"),
            P("tensor", "batch"),
            P("batch"),
            P("batch"),
            P("batch"),
        ),
        check_vma=False,
    )
```

```python
from functools import partial

import jax
import jax.numpy as jnp
from jax import lax
from jax.experimental import pallas as pl
from jax.experimental.pallas import tpu as pltpu
from jax.sharding import PartitionSpec as P

HEAD = 64
EPS = 1e-12
SCALE = 0.125
MASKED = -1e30
MESH = pl.DeviceIdType.MESH
F32 = jnp.float32
BF16 = jnp.bfloat16
NZ, NY, NX, NC = 4, 2, 2, 2


class Place:
    def __init__(self):
        b = lax.axis_index("batch")
        t = lax.axis_index("tensor")
        self.z, self.y = b // NY, b % NY
        self.x, self.c = t // NC, t % NC

    def at(self, z=None, y=None, x=None, c=None):
        z = self.z if z is None else z
        y = self.y if y is None else y
        x = self.x if x is None else x
        c = self.c if c is None else c
        return (z * NY + y, x * NC + c)

    def core(self):
        return self.at(c=1 - self.c)

    def xp(self):
        return self.at(x=1 - self.x)

    def yp(self):
        return self.at(y=1 - self.y)

    def zp(self, step):
        return self.at(z=(self.z + step) % NZ)

    def greet(self):
        barrier = pltpu.get_barrier_semaphore()
        peers = [self.core(), self.xp(), self.yp()] + [self.zp(s) for s in range(1, NZ)]
        for peer in peers:
            pl.semaphore_signal(barrier, inc=1, device_id=peer, device_id_type=MESH)
        pl.semaphore_wait(barrier, len(peers))


def remote(src, dst, sems, index, peer):
    return pltpu.make_async_remote_copy(
        src_ref=src,
        dst_ref=dst,
        send_sem=sems.at[0, index],
        recv_sem=sems.at[1, index],
        device_id=peer,
        device_id_type=MESH,
    )


def normalize(value_rows, gain, shift):
    centred = value_rows - jnp.mean(value_rows, axis=-1, keepdims=True)
    scaled = lax.rsqrt(jnp.mean(centred * centred, axis=-1, keepdims=True) + EPS)
    normed = centred * scaled
    return (normed * gain + shift, normed, scaled)


def normalize_back(grad, normed, scaled, gain):
    weighted = grad * gain
    inner = jnp.mean(weighted * normed, axis=-1, keepdims=True)
    return scaled * (weighted - jnp.mean(weighted, axis=-1, keepdims=True) - normed * inner)


SQRT_HALF = 0.7071067811865476
INV_SQRT_2PI = 0.3989422804014327
ERF_P = 0.3275911
ERF_A = (0.254829592, -0.284496736, 1.421413741, -1.453152027, 1.061405429)
TILE = 96
CUT = 2 * HEAD


def dot(a, b):
    return lax.dot_general(a, b, (((1,), (0,)), ((), ())), preferred_element_type=F32)


def dot_nt(a, b):
    return lax.dot_general(a, b, (((1,), (1,)), ((), ())), preferred_element_type=F32)


def gelu_parts(v):
    size = jnp.abs(v) * SQRT_HALF
    t = 1.0 / (1.0 + ERF_P * size)
    bell = jnp.exp(-0.5 * v * v)
    poly = ERF_A[4]
    for a in ERF_A[3::-1]:
        poly = poly * t + a
    tail = 0.5 * poly * t * bell
    phi = jnp.where(v < 0.0, tail, 1.0 - tail)
    return v * phi, phi + v * bell * INV_SQRT_2PI


def low_lanes():
    return lax.broadcasted_iota(jnp.int32, (1, CUT), 1) < HEAD


def half_rows():
    lane = lax.broadcasted_iota(jnp.int32, (1, CUT), 1)
    low = jnp.where(lane < HEAD, 1.0, 0.0)
    return low.astype(BF16), (1.0 - low).astype(BF16)


def swap(a):
    return pltpu.roll(a, HEAD, 1)


def sel_matrix(key, b):
    lane = lax.broadcasted_iota(jnp.int32, (128, key.shape[1]), 0) * (NZ * NY) + b
    return jnp.where(lane == key, 1.0, 0.0).astype(BF16)


def sel_keys(width):
    col = lax.broadcasted_iota(jnp.int32, (1, width), 1)
    nr = width // (NZ * NY)
    q = jnp.where(col < CUT, col, col - 3 * CUT)
    v = jnp.where(col < 3 * CUT, col - 2 * CUT, col - 4 * CUT)
    is_q = (col < CUT) | ((col >= 4 * CUT) & (col < 4 * CUT + HEAD))
    is_v = ((col >= 2 * CUT) & (col < 3 * CUT)) | ((col >= 5 * CUT) & (col < 5 * CUT + HEAD))
    head = jnp.where(is_q, q, jnp.where(is_v, v + 3 * HEAD, -1))
    return (col % nr) * (NZ * NY) + col // nr, col, head


def run_hooks(hooks, i):
    for k, step in hooks.items():
        pl.when(i == k)(step)


class Layer:
    def __init__(self, **refs):
        self.__dict__.update(refs)
        self.tiles = self.x.shape[0]
        self.width = self.x.shape[2]
        self.rows = self.tiles * TILE
        self.seqs = self.qkv.shape[2]
        self.length = self.qkv.shape[3]
        self.per = self.length // TILE

    def weight(self, p, t, lo, size):
        c, x = t // NX, t % NX
        return self.w[p, c, x, :, :, :, lo:lo + size].reshape(self.width, size)

    def put_weight(self, p, t, lo, value):
        c, x = t // NX, t % NX
        size = value.shape[1]
        nr = self.width // (NZ * NY)
        self.w[p, c, x, :, :, :, lo:lo + size] = value.astype(BF16).reshape(NZ, NY, nr, size)

    def all_rows(self, ref, *at):
        a = ref[at] if at else ref[...]
        return a.reshape(self.rows, a.shape[-1])

    def seq_rows(self, ref, s, *at):
        a = ref[at + (pl.ds(self.per * s, self.per),)]
        return a.reshape(self.length, a.shape[-1])

    def transposed(self, ref, out):
        a = self.all_rows(ref)
        out[0:self.width, :] = a.T
        out[self.width:, :] = jnp.ones((out.shape[0] - self.width, self.rows), BF16)

    def vectors(self):
        keys = sel_keys(self.width)
        self.vec[...] = jnp.zeros(self.vec.shape, F32)

        @pl.loop(0, NZ * NY)
        def _(b):
            z, y = b // NY, b % NY
            own = self.v[:, :, z, y].reshape(NC * NX * 8, 128).astype(BF16)
            for i, key in enumerate(keys):
                part = dot(own, sel_matrix(key, b)).reshape(NC * NX, 8, self.width)
                self.vec[i] = self.vec[i] + part

    def row(self, i):
        return self.vec[0, 0, i:i + 1, :]

    def projections(self):
        low = low_lanes()

        @pl.loop(0, NC)
        def _(u):
            third = []
            for d in range(NX):
                t = NX * u + d
                xv = self.all_rows(self.x)
                for n in range(3):
                    a = dot(xv, self.weight(0, t, 256 * n, 256)) + self.vec[2, t, 7:8, 256 * n:256 * n + 256]
                    if n == 2:
                        third.append(a)
                    else:
                        for h in range(2 if n == 0 else 1):
                            part = a[:, CUT * h:CUT * h + CUT].astype(BF16)
                            self.qkv[2 * n + h, t] = part.reshape(self.seqs, self.length, CUT)
            a, b = third
            q = jnp.where(low, a[:, :CUT], swap(b[:, :CUT]))
            k = jnp.where(low, swap(a[:, :CUT]), b[:, :CUT])
            v = jnp.where(low, a[:, CUT:], swap(b[:, CUT:]))
            for i, part in enumerate((q, k, v)):
                self.qkv[i, NC * NX + u] = part.astype(BF16).reshape(self.seqs, self.length, CUT)

    def heads(self, p, s):
        halves = half_rows()
        q, k, v = (self.qkv[i, p, s] for i in range(3))
        valid = lax.broadcasted_iota(jnp.int32, (1, self.length), 1) < self.lens[self.first + s]
        context = []
        for j in range(2):
            scores = jnp.where(valid, dot_nt(q * halves[j], k) * SCALE, MASKED)
            powers = jnp.exp(scores - jnp.max(scores, axis=1, keepdims=True))
            probs = (powers * (1.0 / jnp.sum(powers, axis=1, keepdims=True))).astype(BF16)
            self.probs[p, s, j] = probs
            context.append(dot(probs, v))
        return jnp.where(low_lanes(), *context)

    def put_context(self, t, s, lo, value):
        value = value.astype(BF16).reshape(self.per, TILE, CUT)
        self.ctx[t, pl.ds(self.per * s, self.per), :, lo:lo + CUT] = value

    def attention_first(self, hooks):
        @pl.loop(0, NC * NX * self.seqs)
        def _(i):
            run_hooks(hooks, i)
            t, s = i // self.seqs, i % self.seqs
            self.put_context(t, s, 0, self.heads(t, s))

    def attention_third(self, hooks):
        low = low_lanes()

        @pl.loop(0, NC * self.seqs)
        def _(i):
            run_hooks(hooks, i)
            u, s = i // self.seqs, i % self.seqs
            context = self.heads(NC * NX + u, s)
            self.put_context(NX * u, s, CUT, jnp.where(low, 0.0, swap(context)))
            self.put_context(NX * u + 1, s, CUT, jnp.where(low, 0.0, context))

    def mixer_weight(self, t):
        return jnp.concatenate([self.weight(0, t, 3 * CUT, CUT), self.weight(0, t, 5 * CUT, CUT)], axis=1)

    def put_rows(self, ref, s, value):
        ref[pl.ds(self.per * s, self.per)] = value.reshape(self.per, TILE, value.shape[1])

    def mix(self):
        @pl.loop(0, self.seqs)
        def _(s):
            total = None
            for t in range(NC * NX):
                part = dot_nt(self.seq_rows(self.ctx, s, t), self.mixer_weight(t))
                total = part if total is None else total + part
            self.put_rows(self.tmp, s, total)

    def norm_first(self):
        @pl.loop(0, self.tiles)
        def _(i):
            total = self.x[i].astype(F32) + self.tmp[i] + self.row(0)
            _, normed, scaled = normalize(total, 1.0, 0.0)
            self.norm[i] = normed
            self.scaled[i] = scaled
            self.hidden[i] = (normed * self.row(1) + self.row(2)).astype(BF16)

    def expand(self, hooks):
        @pl.loop(0, NC * NX)
        def _(t):
            run_hooks(hooks, t)
            hidden = self.all_rows(self.hidden)
            for n in range(3):
                cols = slice(256 * n, 256 * n + 256)
                before = dot(hidden, self.weight(1, t, 256 * n, 256)) + self.vec[1, t, 6:7, cols]
                act, slope = gelu_parts(before)
                self.act[t, :, :, cols] = act.astype(BF16).reshape(self.tiles, TILE, 256)
                self.slope[t, :, :, cols] = slope.astype(BF16).reshape(self.tiles, TILE, 256)

    def times_back(self, p, ref):
        @pl.loop(0, self.seqs)
        def _(s):
            total = None
            for t in range(NC * NX):
                part = dot_nt(self.seq_rows(ref, s, t), self.weight(p, t, 0, self.width))
                total = part if total is None else total + part
            self.put_rows(self.tmp, s, total)

    def add_sum(self, i, value):
        self.sums[i] = self.sums[i] + jnp.sum(value.reshape(TILE // 8, 8, self.width), axis=0)

    def clear_sums(self):
        self.sums[...] = jnp.zeros(self.sums.shape, F32)

    def norm_second(self):
        @pl.loop(0, self.tiles)
        def _(i):
            hidden = self.norm[i] * self.row(1) + self.row(2)
            _, normed, scaled = normalize(hidden + self.tmp[i] + self.row(3), 1.0, 0.0)
            self.out[i] = (normed * self.row(4) + self.row(5)).astype(BF16)
            up = self.cot[i].astype(F32)
            self.add_sum(4, up * normed)
            self.add_sum(5, up)
            after = normalize_back(up, normed, scaled, self.row(4))
            self.add_sum(3, after)
            self.grad[i] = after
            self.low[i] = after.astype(BF16)

    def act_back(self):
        @pl.loop(0, NC * NX)
        def _(t):
            low = self.all_rows(self.low)
            for n in range(3):
                cols = slice(256 * n, 256 * n + 256)
                up = dot(low, self.weight(2, t, 256 * n, 256)).reshape(self.tiles, TILE, 256)
                self.slope[t, :, :, cols] = (up * self.slope[t, :, :, cols].astype(F32)).astype(BF16)

    def contract_grad(self):
        @pl.loop(0, NC * NX)
        def _(t):
            left = self.left[0:self.width, :]
            for n in range(3):
                right = self.all_rows(self.act, t, slice(None), slice(None), slice(256 * n, 256 * n + 256))
                self.put_weight(2, t, 256 * n, dot(left, right))

    def expand_grad(self):
        @pl.loop(0, NC * NX)
        def _(t):
            for n in range(3):
                cols = slice(256 * n, 256 * n + 256)
                grad = dot(self.left[...], self.all_rows(self.slope, t, slice(None), slice(None), cols))
                self.put_weight(1, t, 256 * n, grad[:self.width])
                self.unit_sums[0, t, :, cols] = grad[self.width:self.width + 8]

    def norm_first_back(self):
        @pl.loop(0, self.tiles)
        def _(i):
            grad = self.grad[i] + self.tmp[i]
            normed = self.norm[i]
            self.add_sum(1, grad * normed)
            self.add_sum(2, grad)
            after = normalize_back(grad, normed, self.scaled[i], self.row(1))
            self.add_sum(0, after)
            self.grad[i] = after
            self.low[i] = after.astype(BF16)

    def context_back(self):
        low = low_lanes()

        @pl.loop(0, NC)
        def _(u):
            third = []
            for d in range(NX):
                t = NX * u + d
                grad = dot(self.all_rows(self.low), self.mixer_weight(t))
                self.cgrad[t] = grad[:, :CUT].astype(BF16).reshape(self.seqs, self.length, CUT)
                third.append(grad[:, CUT:])
            pair = jnp.where(low, swap(third[0]), third[1])
            self.cgrad[NC * NX + u] = pair.astype(BF16).reshape(self.seqs, self.length, CUT)

    def heads_back(self, p, s):
        halves = half_rows()
        q, k, v = (self.qkv[i, p, s] for i in range(3))
        up = self.cgrad[p, s]
        up_t = up.T
        q_t = q.T
        dq, dk, dv = [], [], []
        for j in range(2):
            probs = self.probs[p, s, j]
            dv.append(dot(up_t[HEAD * j:HEAD * j + HEAD], probs))
            weight = dot_nt(up * halves[j], v)
            wide = probs.astype(F32)
            grad = wide * (weight - jnp.sum(wide * weight, axis=1, keepdims=True))
            grad = grad.astype(BF16)
            dq.append(dot(grad, k))
            dk.append(dot(q_t[HEAD * j:HEAD * j + HEAD], grad))
        dq = jnp.where(low_lanes(), *dq) * SCALE
        dk = jnp.concatenate(dk, axis=0).T * SCALE
        dv = jnp.concatenate(dv, axis=0).T
        return dq, dk, dv

    def put_stream(self, t, s, lo, value):
        value = value.astype(BF16).reshape(self.per, TILE, CUT)
        self.act[t, pl.ds(self.per * s, self.per), :, lo:lo + CUT] = value

    def attention_back_first(self, hooks):
        @pl.loop(0, NC * NX * self.seqs)
        def _(i):
            run_hooks(hooks, i)
            t, s = i // self.seqs, i % self.seqs
            grads = self.heads_back(t, s)
            for j in range(3):
                self.put_stream(t, s, CUT * j, grads[j])
            self.put_stream(t, s, 3 * CUT, jnp.zeros((self.length, CUT), F32))

    def attention_back_third(self, hooks):
        low = low_lanes()

        @pl.loop(0, NC * self.seqs)
        def _(i):
            run_hooks(hooks, i)
            u, s = i // self.seqs, i % self.seqs
            dq, dk, dv = self.heads_back(NC * NX + u, s)
            self.put_stream(NX * u, s, 4 * CUT, jnp.where(low, dq, swap(dk)))
            self.put_stream(NX * u + 1, s, 4 * CUT, jnp.where(low, swap(dq), dk))
            self.put_stream(NX * u, s, 5 * CUT, jnp.where(low, dv, 0.0))
            self.put_stream(NX * u + 1, s, 5 * CUT, jnp.where(low, swap(dv), 0.0))

    def input_back(self):
        half = self.width // NX

        @pl.loop(0, self.tiles)
        def _(i):
            total = (self.grad[i] + self.tmp[i]).astype(BF16)
            for x in range(NX):
                self.igrad[x, i] = total[:, half * x:half * x + half]

    def attention_grad(self):
        @pl.loop(0, NC * NX)
        def _(t):
            mixer = dot(self.left2[0:self.width, :], self.all_rows(self.ctx, t))
            for n in range(3):
                cols = slice(256 * n, 256 * n + 256)
                grad = dot(self.left[...], self.all_rows(self.act, t, slice(None), slice(None), cols))
                self.unit_sums[1, t, :, cols] = grad[self.width:self.width + 8]
                grad = grad[:self.width]
                if n > 0:
                    part = mixer[:, CUT * (n - 1):CUT * n]
                    grad = jnp.concatenate([grad[:, :CUT], grad[:, CUT:] + part], axis=1)
                self.put_weight(0, t, 256 * n, grad)

    def vector_tiles(self):
        keys = sel_keys(self.width)
        rows = [jnp.sum(self.sums[i], axis=0, keepdims=True) for i in range(6)]
        rows.append(jnp.zeros((2, self.width), F32))
        parts = [jnp.concatenate(rows, axis=0)]
        for i in range(2):
            units = [self.unit_sums[i, t, 0:1, :] for t in range(NC * NX)]
            parts.append(jnp.concatenate(units + [jnp.zeros((4, self.width), F32)], axis=0))
        split = []
        for part in parts:
            high = part.astype(BF16)
            split.append(jnp.concatenate([high, (part - high.astype(F32)).astype(BF16)], axis=0))

        @pl.loop(0, NZ * NY)
        def _(b):
            z, y = b // NY, b % NY
            got = []
            for key, part in zip(keys, split):
                both = dot_nt(part, sel_matrix(key, b))
                got.append(both[:8] + both[8:])
            for t in range(NC * NX):
                self.vtiles[t // NX, t % NX, z, y] = jnp.concatenate(
                    [got[0][:6], got[1][t:t + 1], got[2][t:t + 1]], axis=0
                )


def layer_scratch(seqs, length, width):
    tiles = seqs * length // TILE
    blocks = NC * NX
    pairs = 3 * blocks // 2
    rows = seqs * length
    nr = width // (NZ * NY)
    return [
        pltpu.VMEM((3, NC, NX, NZ, NY, nr, width), BF16),
        pltpu.VMEM((tiles, TILE, width), BF16),
        pltpu.VMEM((tiles, TILE, width), BF16),
        pltpu.VMEM((3, pairs, seqs, length, CUT), BF16),
        pltpu.VMEM((pairs, seqs, 2, length, length), BF16),
        pltpu.VMEM((blocks, tiles, TILE, 2 * CUT), BF16),
        pltpu.VMEM((tiles, TILE, width), F32),
        pltpu.VMEM((tiles, TILE, width), F32),
        pltpu.VMEM((tiles, TILE, 1), F32),
        pltpu.VMEM((tiles, TILE, width), BF16),
        pltpu.VMEM((blocks, tiles, TILE, width), BF16),
        pltpu.VMEM((blocks, tiles, TILE, width), BF16),
        pltpu.VMEM((tiles, TILE, width), F32),
        pltpu.VMEM((tiles, TILE, width), BF16),
        pltpu.VMEM((pairs, seqs, length, CUT), BF16),
        pltpu.VMEM((width + 16, rows), BF16),
        pltpu.VMEM((width + 16, rows), BF16),
        pltpu.VMEM((3, blocks, 8, width), F32),
        pltpu.VMEM((6, 8, width), F32),
        pltpu.VMEM((2, blocks, 8, width), F32),
    ]


class Gather:
    def __init__(self, me, w, v, sems, vsems):
        self.me, self.w, self.v, self.sems, self.vsems = me, w, v, sems, vsems
        half = w.shape[-1] // 2
        self.lo, self.hi = pl.ds(0, half), pl.ds(half, half)

    def same(self, slot, index, peer, small=False):
        return remote(slot, slot, self.vsems if small else self.sems, index, peer)

    def along_z(self, p, s):
        me = self.me
        return self.same(self.w.at[p, me.c, me.x, me.z, me.y], 8 * p + s - 1, me.zp(s))

    def second(self, p):
        me = self.me
        return (
            self.same(self.w.at[p, me.c, me.x, :, me.y, :, self.lo], 8 * p + 3, me.xp()),
            self.same(self.w.at[p, me.c, me.x, :, me.y, :, self.hi], 8 * p + 4, me.yp()),
        )

    def third(self, p):
        me = self.me
        return (
            self.same(self.w.at[p, me.c, :, :, me.y, :, self.lo], 8 * p + 5, me.yp()),
            self.same(self.w.at[p, me.c, me.x, :, :, :, self.hi], 8 * p + 6, me.xp()),
        )

    def fourth(self, p):
        return self.same(self.w.at[p, self.me.c], 8 * p + 7, self.me.core())

    def all_z(self, p):
        return [self.along_z(p, s) for s in range(1, NZ)]

    def send_z(self, p):
        for copy in self.all_z(p):
            copy.start()

    def send_second(self, p):
        for copy in self.all_z(p):
            copy.wait_recv()
        for copy in self.second(p):
            copy.start()

    def send_third(self, p):
        for copy in self.second(p):
            copy.wait_recv()
        for copy in self.third(p):
            copy.start()

    def send_fourth(self, p):
        for copy in self.third(p):
            copy.wait_recv()
        self.fourth(p).start()

    def arrived(self, p):
        self.fourth(p).wait_recv()

    def left(self, p):
        for copy in self.all_z(p) + list(self.second(p)) + list(self.third(p)) + [self.fourth(p)]:
            copy.wait_send()

    def small(self):
        me, v = self.me, self.v
        return [
            [self.same(v.at[me.c, me.x, me.z, me.y], s - 1, me.zp(s), True) for s in range(1, NZ)],
            [self.same(v.at[me.c, me.x, :, me.y], 3, me.xp(), True)],
            [self.same(v.at[me.c, :, :, me.y], 4, me.yp(), True)],
            [self.same(v.at[me.c], 5, me.core(), True)],
        ]

    def small_step(self, i):
        steps = self.small()
        if i > 0:
            for copy in steps[i - 1]:
                copy.wait_recv()
        if i < len(steps):
            for copy in steps[i]:
                copy.start()

    def small_left(self):
        for copy in sum(self.small(), []):
            copy.wait_send()


YFIRST = 640


class Scatter:
    def __init__(self, me, g, v, bufs, sems, vsems, osems, out, outs, ig, igs):
        self.me, self.g, self.v = me, g, v
        self.rc, self.ry0, self.rx1, self.rx0, self.ry1, self.rz, self.vc, self.vy, self.vx, self.vz = bufs
        self.sems, self.vsems, self.osems = sems, vsems, osems
        self.out, self.outs, self.ig, self.igs = out, outs, ig, igs
        width = g.shape[-1]
        self.packs = g.shape[0]
        self.lo, self.hi = pl.ds(0, YFIRST), pl.ds(YFIRST, width - YFIRST)

    def core(self, p):
        me = self.me
        return remote(self.g.at[p, 1 - me.c], self.rc.at[p], self.sems, 6 * p, me.core())

    def first(self, p):
        me = self.me
        return (
            remote(self.g.at[p, me.c, :, :, 1 - me.y, :, self.lo], self.ry0.at[p], self.sems, 6 * p + 1, me.yp()),
            remote(self.g.at[p, me.c, 1 - me.x, :, :, :, self.hi], self.rx1.at[p], self.sems, 6 * p + 2, me.xp()),
        )

    def second(self, p):
        me = self.me
        return (
            remote(
                self.g.at[p, me.c, 1 - me.x, :, me.y, :, self.lo], self.rx0.at[p], self.sems, 6 * p + 3, me.xp()
            ),
            remote(
                self.g.at[p, me.c, me.x, :, 1 - me.y, :, self.hi], self.ry1.at[p], self.sems, 6 * p + 4, me.yp()
            ),
        )

    def third(self, p):
        me = self.me
        return [
            remote(
                self.g.at[p, me.c, me.x, (me.z + s) % NZ, me.y], self.rz.at[p, s - 1],
                self.sems, 6 * self.packs + 3 * p + s - 1, me.zp(s),
            )
            for s in range(1, NZ)
        ]

    def send_core(self, p):
        self.core(p).start()

    def send_first(self, p):
        c = self.me.c
        self.core(p).wait_recv()

        @pl.loop(0, NZ)
        def _(j):
            for i in range(NX):
                for k in range(NY):
                    self.g[p, c, i, j, k] = self.g[p, c, i, j, k] + self.rc[p, i, j, k]

        for copy in self.first(p):
            copy.start()

    def send_second(self, p):
        c, x, y = self.me.c, self.me.x, self.me.y
        lo, hi = self.lo, self.hi
        for copy in self.first(p):
            copy.wait_recv()

        @pl.loop(0, NZ)
        def _(j):
            for i in range(NX):
                self.g[p, c, i, j, y, :, lo] = self.g[p, c, i, j, y, :, lo] + self.ry0[p, i, j]
            for k in range(NY):
                self.g[p, c, x, j, k, :, hi] = self.g[p, c, x, j, k, :, hi] + self.rx1[p, j, k]

        for copy in self.second(p):
            copy.start()

    def send_third(self, p):
        c, x, y = self.me.c, self.me.x, self.me.y
        lo, hi = self.lo, self.hi
        for copy in self.second(p):
            copy.wait_recv()

        @pl.loop(0, NZ)
        def _(j):
            self.g[p, c, x, j, y, :, lo] = self.g[p, c, x, j, y, :, lo] + self.rx0[p, j]
            self.g[p, c, x, j, y, :, hi] = self.g[p, c, x, j, y, :, hi] + self.ry1[p, j]

        for copy in self.third(p):
            copy.start()

    def total(self, p):
        me = self.me
        for copy in self.third(p):
            copy.wait_recv()
        total = self.g[p, me.c, me.x, me.z, me.y].astype(F32)
        for s in range(1, NZ):
            total = total + self.rz[p, s - 1].astype(F32)
        return total

    def left(self, p):
        for copy in [self.core(p)] + list(self.first(p)) + list(self.second(p)) + self.third(p):
            copy.wait_send()

    def small(self, i):
        me, v, sems = self.me, self.v, self.vsems
        if i == 0:
            return [remote(v.at[1 - me.c], self.vc, sems, 0, me.core())]
        if i == 1:
            return [remote(v.at[me.c, :, :, 1 - me.y], self.vy, sems, 1, me.yp())]
        if i == 2:
            return [remote(v.at[me.c, 1 - me.x, :, me.y], self.vx, sems, 2, me.xp())]
        return [
            remote(v.at[me.c, me.x, (me.z + s) % NZ, me.y], self.vz.at[s - 1], sems, 2 + s, me.zp(s))
            for s in range(1, NZ)
        ]

    def small_step(self, i):
        me, v = self.me, self.v
        if i > 0:
            for copy in self.small(i - 1):
                copy.wait_recv()
        if i == 1:
            v[me.c] = v[me.c] + self.vc[...]
        elif i == 2:
            v[me.c, :, :, me.y] = v[me.c, :, :, me.y] + self.vy[...]
        elif i == 3:
            v[me.c, me.x, :, me.y] = v[me.c, me.x, :, me.y] + self.vx[...]
        elif i == 4:
            total = v[me.c, me.x, me.z, me.y]
            for s in range(1, NZ):
                total = total + self.vz[s - 1]
            return total
        for copy in self.small(i):
            copy.start()

    def small_left(self):
        for i in range(4):
            for copy in self.small(i):
                copy.wait_send()

    def outputs(self, local):
        me = self.me
        t = me.x * NC + me.c
        return [
            remote(self.out, self.outs.at[t], self.osems, 0, me.xp()),
            remote(self.out, self.outs.at[t], self.osems, 1, me.core()),
        ], pltpu.make_async_copy(self.out, self.outs.at[t], local)

    def output_forward(self):
        me = self.me
        t = (1 - me.x) * NC + me.c
        return remote(self.outs.at[t], self.outs.at[t], self.osems, 4, me.core())

    def grads(self, local):
        me = self.me
        t = me.x * NC + me.c
        return [
            remote(self.ig.at[1 - me.x], self.igs.at[t], self.osems, 2, me.xp()),
            remote(self.ig.at[me.x], self.igs.at[t], self.osems, 3, me.core()),
        ], pltpu.make_async_copy(self.ig.at[me.x], self.igs.at[t], local)

    def grad_forward(self):
        me = self.me
        t = (1 - me.x) * NC + me.c
        return remote(self.igs.at[t], self.igs.at[t], self.osems, 5, me.core())


def start_all(group):
    copies, local = group
    for copy in copies:
        copy.start()
    local.start()


def step_kernel(
    x_in, cot_in, lens, tw, mw, ew, cw, vec_in,
    outs, igs, triple_out, mixer_out, expand_out, contract_out, small_out,
    w, v, vtiles, out, ig,
    x, cot, qkv, probs, ctx, tmp, norm, scaled, hidden, act, slope, grad, low, cgrad, left, left2, vec, sums,
    unit_sums,
    rc, ry0, rx1, rx0, ry1, rz, vc, vy, vx, vz,
    gsems, gvsems, sems, vsems, osems, lsems,
):
    me = Place()
    t = lax.axis_index("tensor")
    seqs = qkv.shape[2]
    load_x = pltpu.make_async_copy(x_in.at[t], x, lsems.at[0])
    load_cot = pltpu.make_async_copy(cot_in.at[t], cot, lsems.at[1])
    own = [w.at[p, me.c, me.x, me.z, me.y] for p in range(3)]
    load_e = pltpu.make_async_copy(ew, own[1], lsems.at[2])
    load_v = pltpu.make_async_copy(vec_in, v.at[me.c, me.x, me.z, me.y], lsems.at[3])
    load_v.start()
    load_e.start()
    load_x.start()
    load_cot.start()
    pack_attention(tw, mw, own[0])
    gather = Gather(me, w, v, gsems, gvsems)
    layer = Layer(
        w=w, x=x, cot=cot, qkv=qkv, probs=probs, ctx=ctx, tmp=tmp, norm=norm, scaled=scaled, hidden=hidden, act=act,
        slope=slope, grad=grad, low=low, cgrad=cgrad, left=left, left2=left2, vec=vec, sums=sums, unit_sums=unit_sums,
        v=v, out=out, igrad=ig, vtiles=vtiles, lens=lens, first=t * seqs,
    )
    scatter = Scatter(
        me, w, vtiles, (rc, ry0, rx1, rx0, ry1, rz, vc, vy, vx, vz), sems, vsems, osems, out, outs, ig, igs
    )
    load_v.wait()
    me.greet()
    gather.send_z(0)
    gather.small_step(0)
    load_e.wait()
    gather.send_z(1)
    own[2][...] = cw[...].T
    gather.send_z(2)
    layer.clear_sums()
    load_x.wait()
    load_cot.wait()
    gather.small_step(1)
    gather.send_second(0)
    gather.small_step(2)
    gather.small_step(3)
    gather.small_step(4)
    layer.vectors()
    gather.send_third(0)
    gather.send_second(1)
    gather.send_fourth(0)
    gather.arrived(0)
    layer.projections()
    gather.send_third(1)
    gather.send_second(2)
    layer.attention_first({6: lambda: gather.send_fourth(1)})
    layer.attention_third({1: lambda: gather.send_third(2)})
    layer.mix()
    layer.norm_first()
    gather.arrived(1)
    layer.expand({2: lambda: gather.send_fourth(2)})
    gather.arrived(2)
    layer.times_back(2, act)
    layer.norm_second()
    start_all(scatter.outputs(lsems.at[4]))
    layer.transposed(low, left)
    layer.act_back()
    gather.left(2)
    layer.contract_grad()
    scatter.send_core(2)
    layer.times_back(1, slope)
    scatter.send_first(2)
    layer.transposed(hidden, left)
    gather.left(1)
    layer.expand_grad()
    scatter.send_core(1)
    layer.norm_first_back()
    layer.transposed(low, left2)
    layer.context_back()
    scatter.send_first(1)

    def forward_output():
        scatter.outputs(lsems.at[4])[0][0].wait_recv()
        scatter.output_forward().start()

    layer.attention_back_first({3: lambda: scatter.send_second(2), 5: forward_output})
    layer.attention_back_third({2: lambda: scatter.send_third(2)})
    layer.times_back(0, act)
    layer.input_back()
    start_all(scatter.grads(lsems.at[5]))
    layer.transposed(x, left)
    gather.left(0)
    layer.attention_grad()
    scatter.send_core(0)
    layer.vector_tiles()
    scatter.small_step(0)
    scatter.send_second(1)
    scatter.send_first(0)
    scatter.small_step(1)
    contract_out[...] = scatter.total(2).T
    scatter.small_step(2)
    scatter.send_third(1)
    scatter.small_step(3)
    scatter.grads(lsems.at[5])[0][0].wait_recv()
    scatter.grad_forward().start()
    scatter.send_second(0)
    expand_out[...] = scatter.total(1)
    small_out[...] = scatter.small_step(4)
    scatter.send_third(0)
    unpack_attention(scatter.total(0), triple_out, mixer_out)
    outputs, out_local = scatter.outputs(lsems.at[4])
    grads, ig_local = scatter.grads(lsems.at[5])
    outputs[1].wait_recv()
    grads[1].wait_recv()
    for copy in (scatter.output_forward(), scatter.grad_forward()):
        copy.wait_recv()
        copy.wait_send()
    for copy in outputs + grads:
        copy.wait_send()
    out_local.wait()
    ig_local.wait()
    gather.small_left()
    scatter.small_left()
    for p in range(3):
        scatter.left(p)


def pack_attention(tw, mw, slot):
    mixer = mw[...].T
    for i in range(3):
        slot[:, CUT * i:CUT * i + CUT] = tw[i, :, 0:CUT]
    slot[:, 3 * CUT:4 * CUT] = mixer[:, 0:CUT]
    slot[:, 4 * CUT:5 * CUT] = jnp.concatenate([tw[0, :, CUT:], tw[1, :, CUT:]], axis=1)
    slot[:, 5 * CUT:6 * CUT] = jnp.concatenate([tw[2, :, CUT:], mixer[:, CUT:]], axis=1)


def unpack_attention(total, triple_out, mixer_out):
    for i in range(3):
        triple_out[i, :, 0:CUT] = total[:, CUT * i:CUT * i + CUT]
        triple_out[i, :, CUT:] = total[:, 4 * CUT + HEAD * i:4 * CUT + HEAD * i + HEAD]
    mixer_out[0:CUT] = total[:, 3 * CUT:4 * CUT].T
    mixer_out[CUT:] = total[:, 5 * CUT + HEAD:].T


def step_call(x, cot, lengths, tw, mw, ew, cw, vec, seqs):
    pairs, length, width = x.shape
    tiles = seqs * length // TILE
    blocks = NX * NC
    nr, feat = width // (NZ * NY), width // blocks
    shape = (blocks, tiles, TILE, width)
    rest = width - YFIRST
    vmem = pl.BlockSpec(memory_space=pltpu.VMEM)
    hbm = pl.BlockSpec(memory_space=pl.ANY)
    layer = layer_scratch(seqs, length, width)
    small = (8, 128)
    return pl.pallas_call(
        step_kernel,
        out_shape=(
            jax.ShapeDtypeStruct(shape, BF16),
            jax.ShapeDtypeStruct((blocks, tiles, TILE, width // NX), BF16),
            jax.ShapeDtypeStruct((3, nr, feat), F32),
            jax.ShapeDtypeStruct((feat, nr), F32),
            jax.ShapeDtypeStruct((nr, width), F32),
            jax.ShapeDtypeStruct((width, nr), F32),
            jax.ShapeDtypeStruct(small, F32),
        ),
        in_specs=[hbm, hbm, pl.BlockSpec(memory_space=pltpu.SMEM), vmem, vmem, hbm, vmem, hbm],
        out_specs=(hbm, hbm, vmem, vmem, vmem, vmem, vmem),
        scratch_shapes=[
            layer[0],
            pltpu.VMEM((NC, NX, NZ, NY) + small, F32),
            pltpu.VMEM((NC, NX, NZ, NY) + small, F32),
            pltpu.VMEM((tiles, TILE, width), BF16),
            pltpu.VMEM((NX, tiles, TILE, width // NX), BF16),
        ] + layer[1:] + [
            pltpu.VMEM((3, NX, NZ, NY, nr, width), BF16),
            pltpu.VMEM((3, NX, NZ, nr, YFIRST), BF16),
            pltpu.VMEM((3, NZ, NY, nr, rest), BF16),
            pltpu.VMEM((3, NZ, nr, YFIRST), BF16),
            pltpu.VMEM((3, NZ, nr, rest), BF16),
            pltpu.VMEM((3, NZ - 1, nr, width), BF16),
            pltpu.VMEM((NX, NZ, NY) + small, F32),
            pltpu.VMEM((NX, NZ) + small, F32),
            pltpu.VMEM((NZ,) + small, F32),
            pltpu.VMEM((NZ - 1,) + small, F32),
            pltpu.SemaphoreType.DMA((2, 24)),
            pltpu.SemaphoreType.DMA((2, 6)),
            pltpu.SemaphoreType.DMA((2, 27)),
            pltpu.SemaphoreType.DMA((2, 6)),
            pltpu.SemaphoreType.DMA((2, 6)),
            pltpu.SemaphoreType.DMA((6,)),
        ],
        compiler_params=pltpu.CompilerParams(
            collective_id=0, has_side_effects=True, vmem_limit_bytes=67043328
        ),
    )(x.reshape(shape), cot.reshape(shape), lengths, tw, mw, ew, cw, vec)


def layer_step(x_seq, lengths, cot, w, d_vec, e_bias, p_bias):
    seqs, length, width = x_seq.shape
    rows = seqs * length
    blocks = w.shape[1]
    feat = width // blocks
    heads = feat // HEAD
    mixer_shift, gain_one, shift_one, contract_shift, gain_two, shift_two = d_vec
    x = x_seq.reshape(rows, width)
    att = w[0]
    cut = 2 * HEAD
    def columns(i):
        return jnp.concatenate(
            [att[:, :, i * cut:(i + 1) * cut], att[:, :, 4 * cut + i * HEAD:4 * cut + (i + 1) * HEAD]], axis=2
        )
    wq, wk, wv, wm = (columns(i) for i in range(4))
    def project(weight, bias):
        out = jnp.einsum("rd,tde->rte", x, weight, preferred_element_type=F32)
        if bias is not None:
            out = out + bias
        return out.astype(BF16).reshape(seqs, length, blocks * heads, HEAD)
    queries = project(wq, p_bias[0])
    keys = project(wk, None)
    values = project(wv, p_bias[1])
    valid = lax.broadcasted_iota(jnp.int32, (seqs, 1, 1, length), 3) < lengths[:, None, None, None]
    raw = jnp.einsum("sqhd,skhd->shqk", queries, keys, preferred_element_type=F32) * SCALE
    raw = jnp.where(valid, raw, MASKED)
    peak = jnp.max(raw, axis=-1, keepdims=True)
    powers = jnp.exp(raw - peak)
    probs = powers / jnp.sum(powers, axis=-1, keepdims=True)
    attention = probs.astype(BF16)
    context = jnp.einsum("shqk,skhd->sqhd", attention, values, preferred_element_type=F32)
    context = context.astype(BF16).reshape(rows, blocks, feat)
    mixed = jnp.einsum("rtc,tdc->rd", context, wm, preferred_element_type=F32)
    hidden, normed_one, scaled_one = normalize(x.astype(F32) + mixed + mixer_shift, gain_one, shift_one)
    hidden_low = hidden.astype(BF16)
    before = jnp.einsum("rd,tdf->rtf", hidden_low, w[1], preferred_element_type=F32) + e_bias
    activated = jax.nn.gelu(before, approximate=False).astype(BF16)
    branch = jnp.einsum("rtf,tdf->rd", activated, w[2], preferred_element_type=F32)
    result, normed_two, scaled_two = normalize(hidden + branch + contract_shift, gain_two, shift_two)
    outputs = result.astype(BF16)
    up = cot.reshape(rows, width).astype(F32)
    gain_two_grad = jnp.sum(up * normed_two, axis=0)
    shift_two_grad = jnp.sum(up, axis=0)
    after_two = normalize_back(up, normed_two, scaled_two, gain_two)
    contract_shift_grad = jnp.sum(after_two, axis=0)
    two_low = after_two.astype(BF16)
    contract_grad = jnp.einsum("rd,rtf->tdf", two_low, activated, preferred_element_type=F32)
    act_grad = jnp.einsum("rd,tdf->rtf", two_low, w[2], preferred_element_type=F32)
    _, gelu_back = jax.vjp(partial(jax.nn.gelu, approximate=False), before)
    before_grad = gelu_back(act_grad)[0].astype(BF16)
    expand_grad = jnp.einsum("rd,rtf->tdf", hidden_low, before_grad, preferred_element_type=F32)
    e_bias_grad = jnp.sum(before_grad, axis=0, dtype=F32)
    hidden_part = jnp.einsum("rtf,tdf->rd", before_grad, w[1], preferred_element_type=F32)
    hidden_grad = after_two + hidden_part
    after_one = normalize_back(hidden_grad, normed_one, scaled_one, gain_one)
    gain_one_grad = jnp.sum(hidden_grad * normed_one, axis=0)
    shift_one_grad = jnp.sum(hidden_grad, axis=0)
    mixer_shift_grad = jnp.sum(after_one, axis=0)
    one_low = after_one.astype(BF16)
    mixer_grad = jnp.einsum("rd,rtc->tdc", one_low, context, preferred_element_type=F32)
    context_grad = jnp.einsum("rd,tdc->rtc", one_low, wm, preferred_element_type=F32).astype(BF16)
    context_grad = context_grad.reshape(seqs, length, blocks * heads, HEAD)
    value_grad = jnp.einsum("shqk,sqhd->skhd", attention, context_grad, preferred_element_type=F32)
    weight_grad = jnp.einsum("sqhd,skhd->shqk", context_grad, values, preferred_element_type=F32)
    score_grad = probs * (weight_grad - jnp.sum(probs * weight_grad, axis=-1, keepdims=True))
    score_grad = score_grad.astype(BF16)
    query_grad = jnp.einsum("shqk,skhd->sqhd", score_grad, keys, preferred_element_type=F32) * SCALE
    key_grad = jnp.einsum("shqk,sqhd->skhd", score_grad, queries, preferred_element_type=F32) * SCALE
    streams = [g.astype(BF16).reshape(rows, blocks, feat) for g in (query_grad, key_grad, value_grad)]
    p_grad = [jnp.sum(streams[i], axis=0, dtype=F32) for i in (0, 2)]
    tgrads = [jnp.einsum("rd,rte->tde", x, s, preferred_element_type=F32) for s in streams] + [mixer_grad]
    att_grad = jnp.concatenate([g[:, :, :cut] for g in tgrads] + [g[:, :, cut:] for g in tgrads], axis=2)
    part = sum(
        jnp.einsum("rte,tde->rd", s, wt, preferred_element_type=F32) for s, wt in zip(streams, (wq, wk, wv))
    )
    input_grad = (after_one + part).astype(BF16)
    grads = jnp.stack([att_grad, expand_grad, contract_grad]).astype(BF16)
    vecs = jnp.stack(
        [mixer_shift_grad, gain_one_grad, shift_one_grad, contract_shift_grad, gain_two_grad, shift_two_grad]
    )
    return outputs, input_grad, grads, vecs, e_bias_grad, jnp.stack(p_grad)


def make_on_device(sizes):
    fast = sizes == {"batch": NZ * NY, "tensor": NX * NC}

    def on_device(
        inputs, lengths, triple_weight, pair_bias, mixer_weight, mixer_bias, first_gain, first_shift,
        expand_weight, expand_bias, contract_weight, contract_bias, second_gain, second_shift, cotangent,
    ):
        pairs, length, width = inputs.shape
        n_tensor, n_batch = sizes["tensor"], sizes["batch"]
        nr = width // n_batch
        own_pairs = pairs // n_tensor
        t = lax.axis_index("tensor")
        feat = width // n_tensor
        small = (mixer_bias, first_gain, first_shift, contract_bias, second_gain, second_shift, expand_bias, pair_bias)
        if fast:
            vec = jnp.concatenate([jnp.pad(v.reshape(-1).astype(F32), (0, 128 - v.size)) for v in small])
            outs, ig, triple_grad, mixer_grad, expand_grad, contract_grad, vred = step_call(
                inputs, cotangent, lengths, triple_weight, mixer_weight, expand_weight, contract_weight,
                vec.reshape(8, 128), own_pairs,
            )
            ig = lax.dynamic_slice_in_dim(ig, t % NC * feat, feat, 3)
            outs = outs.reshape(pairs, length, width)
            ig = ig.reshape(pairs, length, feat).astype(F32)
        else:
            cut = 2 * HEAD
            four = [triple_weight[0], triple_weight[1], triple_weight[2], mixer_weight.T]
            att = jnp.concatenate([m[:, :cut] for m in four] + [m[:, cut:] for m in four], axis=1)
            pack = jnp.stack([att, expand_weight, contract_weight.T])
            def row(v):
                return jnp.pad(v.reshape(1, -1), ((0, 0), (0, 128 - v.size)))
            vec = jnp.concatenate(
                [row(v) for v in (mixer_bias, first_gain, first_shift, contract_bias, second_gain, second_shift,
                                  expand_bias, pair_bias)] + [jnp.zeros((8, 128), BF16)], axis=0
            )
            w = lax.all_gather(lax.all_gather(pack, "batch", axis=1, tiled=True), "tensor", axis=1)
            v = lax.all_gather(lax.all_gather(vec, "batch"), "tensor")
            d_vec = v[0, :, :6, :nr].transpose(1, 0, 2).reshape(6, width).astype(F32)
            e_bias = v[:, :, 6, :nr].transpose(0, 2, 1).reshape(n_tensor, width).astype(F32)
            p_bias = v[:, :, 7, :2 * feat // n_batch].reshape(n_tensor, n_batch, 2, feat // n_batch)
            p_bias = p_bias.transpose(2, 0, 3, 1).reshape(2, n_tensor, feat).astype(F32)
            mine = partial(lax.dynamic_slice_in_dim, start_index=t * own_pairs, slice_size=own_pairs, axis=0)
            outputs, input_grad, grads, vecs, e_grad, p_grad = layer_step(
                mine(inputs), mine(lengths), mine(cotangent), w, d_vec, e_bias, p_bias
            )
            rows = own_pairs * length
            dv = jnp.broadcast_to(vecs.reshape(1, 6, n_batch, nr).transpose(0, 2, 1, 3), (n_tensor, n_batch, 6, nr))
            ev = e_grad.reshape(n_tensor, nr, n_batch).transpose(0, 2, 1)[:, :, None]
            pv = p_grad.reshape(2, n_tensor, feat // n_batch, n_batch).transpose(1, 3, 0, 2)
            pv = pv.reshape(n_tensor, n_batch, 1, 2 * feat // n_batch)
            lanes = lambda a: jnp.pad(a, ((0, 0), (0, 0), (0, 0), (0, 128 - a.shape[-1])))
            tiles = jnp.concatenate([lanes(dv), lanes(ev), lanes(pv)], axis=2)
            grads = lax.psum_scatter(grads.astype(F32), "tensor", scatter_dimension=1)
            red = lax.psum_scatter(grads, "batch", scatter_dimension=1, tiled=True)
            vred = lax.psum_scatter(lax.psum_scatter(tiles, "tensor"), "batch")
            outs = lax.all_gather(outputs, "tensor").reshape(pairs, length, width)
            ig = lax.all_to_all(
                input_grad.reshape(rows, n_tensor, feat), "tensor", split_axis=1, concat_axis=0, tiled=True
            )
            ig = ig.reshape(pairs, length, feat).astype(F32)
            att_g = red[0]
            four_g = [
                jnp.concatenate([att_g[:, i * cut:(i + 1) * cut], att_g[:, 4 * cut + i * HEAD:4 * cut + (i + 1) * HEAD]], axis=1)
                for i in range(4)
            ]
            triple_grad, mixer_grad = jnp.stack(four_g[:3]), four_g[3].T
            expand_grad, contract_grad = red[1], red[2].T
        return (
            outs,
            ig,
            triple_grad,
            vred[7, :2 * feat // n_batch].reshape(pair_bias.shape),
            mixer_grad,
            vred[0, :nr],
            vred[1, :nr],
            vred[2, :nr],
            expand_grad,
            vred[6, :nr].reshape(expand_bias.shape),
            contract_grad,
            vred[3, :nr],
            vred[4, :nr],
            vred[5, :nr],
        )

    return on_device


def solution(mesh):
    return jax.shard_map(
        make_on_device(dict(mesh.shape)),
        mesh=mesh,
        in_specs=(
            P("batch", None, None),
            P("batch"),
            P(None, "batch", "tensor"),
            P(None, "tensor", "batch"),
            P("tensor", "batch"),
            P("batch"),
            P("batch"),
            P("batch"),
            P("batch", "tensor"),
            P("tensor", "batch"),
            P("tensor", "batch"),
            P("batch"),
            P("batch"),
            P("batch"),
            P("batch", None, None),
        ),
        out_specs=(
            P("batch", None, None),
            P("batch", None, "tensor"),
            P(None, "batch", "tensor"),
            P(None, "tensor", "batch"),
            P("tensor", "batch"),
            P("batch"),
            P("batch"),
            P("batch"),
            P("batch", "tensor"),
            P("tensor", "batch"),
            P("tensor", "batch"),
            P("batch"),
            P("batch"),
            P("batch"),
        ),
        check_vma=False,
    )
```

```python
from functools import partial

import jax
import jax.numpy as jnp
from jax import lax
from jax.experimental import pallas as pl
from jax.experimental.pallas import tpu as pltpu
from jax.sharding import PartitionSpec as P

HEAD = 64
EPS = 1e-12
SCALE = 0.125
MASKED = -1e30
MESH = pl.DeviceIdType.MESH
F32 = jnp.float32
BF16 = jnp.bfloat16
NZ, NY, NX, NC = 4, 2, 2, 2


class Place:
    def __init__(self):
        b = lax.axis_index("batch")
        t = lax.axis_index("tensor")
        self.z, self.y = b // NY, b % NY
        self.x, self.c = t // NC, t % NC

    def at(self, z=None, y=None, x=None, c=None):
        z = self.z if z is None else z
        y = self.y if y is None else y
        x = self.x if x is None else x
        c = self.c if c is None else c
        return (z * NY + y, x * NC + c)

    def core(self):
        return self.at(c=1 - self.c)

    def xp(self):
        return self.at(x=1 - self.x)

    def yp(self):
        return self.at(y=1 - self.y)

    def zp(self, step):
        return self.at(z=(self.z + step) % NZ)

    def peers(self):
        return [self.core(), self.xp(), self.yp()] + [self.zp(s) for s in range(1, NZ)]

    def signal(self):
        barrier = pltpu.get_barrier_semaphore()
        for peer in self.peers():
            pl.semaphore_signal(barrier, inc=1, device_id=peer, device_id_type=MESH)

    def meet(self):
        pl.semaphore_wait(pltpu.get_barrier_semaphore(), len(self.peers()))

    def own(self, axis):
        return {"x": self.x, "y": self.y, "z": self.z}[axis]

    def others(self, axis):
        if axis == "z":
            return [(self.z + s) % NZ for s in range(1, NZ)]
        return [1 - self.own(axis)]

    def along(self, axis):
        if axis == "z":
            return [self.zp(s) for s in range(1, NZ)]
        return [self.xp() if axis == "x" else self.yp()]


def remote(src, dst, sems, index, peer):
    return pltpu.make_async_remote_copy(
        src_ref=src,
        dst_ref=dst,
        send_sem=sems.at[0, index],
        recv_sem=sems.at[1, index],
        device_id=peer,
        device_id_type=MESH,
    )


def normalize(value_rows, gain, shift):
    centred = value_rows - jnp.mean(value_rows, axis=-1, keepdims=True)
    scaled = lax.rsqrt(jnp.mean(centred * centred, axis=-1, keepdims=True) + EPS)
    normed = centred * scaled
    return (normed * gain + shift, normed, scaled)


def normalize_back(grad, normed, scaled, gain):
    weighted = grad * gain
    inner = jnp.mean(weighted * normed, axis=-1, keepdims=True)
    return scaled * (weighted - jnp.mean(weighted, axis=-1, keepdims=True) - normed * inner)


SQRT_HALF = 0.7071067811865476
INV_SQRT_2PI = 0.3989422804014327
ERF_P = 0.3275911
ERF_A = (0.254829592, -0.284496736, 1.421413741, -1.453152027, 1.061405429)
TILE = 96
CUT = 2 * HEAD


def dot(a, b):
    return lax.dot_general(a, b, (((1,), (0,)), ((), ())), preferred_element_type=F32)


def dot_nt(a, b):
    return lax.dot_general(a, b, (((1,), (1,)), ((), ())), preferred_element_type=F32)


def gelu_parts(v):
    size = jnp.abs(v) * SQRT_HALF
    t = 1.0 / (1.0 + ERF_P * size)
    bell = jnp.exp(-0.5 * v * v)
    poly = ERF_A[4]
    for a in ERF_A[3::-1]:
        poly = poly * t + a
    tail = 0.5 * poly * t * bell
    phi = jnp.where(v < 0.0, tail, 1.0 - tail)
    return v * phi, phi + v * bell * INV_SQRT_2PI


def low_lanes():
    return lax.broadcasted_iota(jnp.int32, (1, CUT), 1) < HEAD


def half_rows():
    lane = lax.broadcasted_iota(jnp.int32, (1, CUT), 1)
    low = jnp.where(lane < HEAD, 1.0, 0.0)
    return low.astype(BF16), (1.0 - low).astype(BF16)


def swap(a):
    return pltpu.roll(a, HEAD, 1)


def sel_matrix(key, b):
    lane = lax.broadcasted_iota(jnp.int32, (128, key.shape[1]), 0) * (NZ * NY) + b
    return jnp.where(lane == key, 1.0, 0.0).astype(BF16)


def sel_keys(width):
    col = lax.broadcasted_iota(jnp.int32, (1, width), 1)
    nr = width // (NZ * NY)
    q = jnp.where(col < CUT, col, col - 3 * CUT)
    v = jnp.where(col < 3 * CUT, col - 2 * CUT, col - 4 * CUT)
    is_q = (col < CUT) | ((col >= 4 * CUT) & (col < 4 * CUT + HEAD))
    is_v = ((col >= 2 * CUT) & (col < 3 * CUT)) | ((col >= 5 * CUT) & (col < 5 * CUT + HEAD))
    head = jnp.where(is_q, q, jnp.where(is_v, v + 3 * HEAD, -1))
    return (col % nr) * (NZ * NY) + col // nr, col, head


def run_hooks(hooks, i):
    for k, step in hooks.items():
        pl.when(i == k)(step)


class Layer:
    def __init__(self, **refs):
        self.__dict__.update(refs)
        self.tiles = self.x.shape[0]
        self.width = self.x.shape[2]
        self.rows = self.tiles * TILE
        self.seqs = self.qkv.shape[2]
        self.length = self.qkv.shape[3]
        self.per = self.length // TILE

    def weight(self, p, t, lo, size):
        c, x = t // NX, t % NX
        return self.w[p, c, x, :, :, :, lo:lo + size].reshape(self.width, size)

    def put_weight(self, p, t, lo, value):
        c, x = t // NX, t % NX
        size = value.shape[1]
        nr = self.width // (NZ * NY)
        self.w[p, c, x, :, :, :, lo:lo + size] = value.astype(BF16).reshape(NZ, NY, nr, size)

    def all_rows(self, ref, *at):
        a = ref[at] if at else ref[...]
        return a.reshape(self.rows, a.shape[-1])

    def seq_rows(self, ref, s, *at):
        a = ref[at + (pl.ds(self.per * s, self.per),)]
        return a.reshape(self.length, a.shape[-1])

    def transposed(self, ref, out):
        a = self.all_rows(ref)
        out[0:self.width, :] = a.T
        out[self.width:, :] = jnp.ones((out.shape[0] - self.width, self.rows), BF16)

    def vectors(self):
        keys = sel_keys(self.width)
        self.vec[...] = jnp.zeros(self.vec.shape, F32)

        @pl.loop(0, NZ * NY)
        def _(b):
            z, y = b // NY, b % NY
            own = self.v[:, :, z, y].reshape(NC * NX * 8, 128).astype(BF16)
            for i, key in enumerate(keys):
                part = dot(own, sel_matrix(key, b)).reshape(NC * NX, 8, self.width)
                self.vec[i] = self.vec[i] + part

    def row(self, i):
        return self.vec[0, 0, i:i + 1, :]

    def projected(self, t, n):
        bias = self.vec[2, t, 7:8, 256 * n:256 * n + 256]
        return dot(self.all_rows(self.x), self.weight(0, t, 256 * n, 256)) + bias

    def put_head(self, i, p, value):
        self.qkv[i, p] = value.astype(BF16).reshape(self.seqs, self.length, CUT)

    def projections_first(self):
        @pl.loop(0, NC * NX)
        def _(t):
            a = self.projected(t, 0)
            self.put_head(0, t, a[:, :CUT])
            self.put_head(1, t, a[:, CUT:])
            bias = self.vec[2, t, 7:8, 2 * CUT:3 * CUT]
            self.put_head(2, t, dot(self.all_rows(self.x), self.weight(0, t, 2 * CUT, CUT)) + bias)

    def projections_third(self):
        low = low_lanes()

        @pl.loop(0, NC)
        def _(u):
            a, b = self.projected(NX * u, 2), self.projected(NX * u + 1, 2)
            self.put_head(0, NC * NX + u, jnp.where(low, a[:, :CUT], swap(b[:, :CUT])))
            self.put_head(1, NC * NX + u, jnp.where(low, swap(a[:, :CUT]), b[:, :CUT]))
            self.put_head(2, NC * NX + u, jnp.where(low, a[:, CUT:], swap(b[:, CUT:])))

    def heads(self, p, s):
        halves = half_rows()
        q, k, v = (self.qkv[i, p, s] for i in range(3))
        valid = lax.broadcasted_iota(jnp.int32, (1, self.length), 1) < self.lens[self.first + s]
        context = []
        for j in range(2):
            scores = jnp.where(valid, dot_nt(q * halves[j], k) * SCALE, MASKED)
            powers = jnp.exp(scores - jnp.max(scores, axis=1, keepdims=True))
            probs = (powers * (1.0 / jnp.sum(powers, axis=1, keepdims=True))).astype(BF16)
            self.probs[p, s, j] = probs
            context.append(dot(probs, v))
        return jnp.where(low_lanes(), *context)

    def put_context(self, t, s, lo, value):
        value = value.astype(BF16).reshape(self.per, TILE, CUT)
        self.ctx[t, pl.ds(self.per * s, self.per), :, lo:lo + CUT] = value

    def attention_first(self, hooks):
        @pl.loop(0, NC * NX * self.seqs)
        def _(i):
            run_hooks(hooks, i)
            t, s = i // self.seqs, i % self.seqs
            self.put_context(t, s, 0, self.heads(t, s))

    def attention_third(self, hooks):
        low = low_lanes()

        @pl.loop(0, NC * self.seqs)
        def _(i):
            run_hooks(hooks, i)
            u, s = i // self.seqs, i % self.seqs
            context = self.heads(NC * NX + u, s)
            self.put_context(NX * u, s, CUT, jnp.where(low, 0.0, swap(context)))
            self.put_context(NX * u + 1, s, CUT, jnp.where(low, 0.0, context))

    def mixer_weight(self, t):
        return jnp.concatenate([self.weight(0, t, 3 * CUT, CUT), self.weight(0, t, 5 * CUT, CUT)], axis=1)

    def put_rows(self, ref, s, value):
        ref[pl.ds(self.per * s, self.per)] = value.reshape(self.per, TILE, value.shape[1])

    def mix(self):
        @pl.loop(0, self.seqs)
        def _(s):
            total = None
            for t in range(NC * NX):
                part = dot_nt(self.seq_rows(self.ctx, s, t), self.mixer_weight(t))
                total = part if total is None else total + part
            self.put_rows(self.tmp, s, total)

    def norm_first(self):
        @pl.loop(0, self.tiles)
        def _(i):
            total = self.x[i].astype(F32) + self.tmp[i] + self.row(0)
            _, normed, scaled = normalize(total, 1.0, 0.0)
            self.norm[i] = normed
            self.scaled[i] = scaled
            self.hidden[i] = (normed * self.row(1) + self.row(2)).astype(BF16)

    def expand(self, hooks):
        @pl.loop(0, NC * NX)
        def _(t):
            run_hooks(hooks, t)
            hidden = self.all_rows(self.hidden)
            for n in range(3):
                cols = slice(256 * n, 256 * n + 256)
                before = dot(hidden, self.weight(1, t, 256 * n, 256)) + self.vec[1, t, 6:7, cols]
                act, slope = gelu_parts(before)
                self.act[t, :, :, cols] = act.astype(BF16).reshape(self.tiles, TILE, 256)
                self.slope[t, :, :, cols] = slope.astype(BF16).reshape(self.tiles, TILE, 256)

    def times_back(self, p, ref, lo=0, size=None, more=False):
        size = self.width if size is None else size

        @pl.loop(0, self.seqs)
        def _(s):
            rows = pl.ds(self.per * s, self.per)
            total = self.tmp[rows].reshape(self.length, self.width) if more else None
            for t in range(NC * NX):
                left = ref[t, rows, :, lo:lo + size].reshape(self.length, size)
                part = dot_nt(left, self.weight(p, t, lo, size))
                total = part if total is None else total + part
            self.put_rows(self.tmp, s, total)

    def add_sum(self, i, value):
        self.sums[i] = self.sums[i] + jnp.sum(value.reshape(TILE // 8, 8, self.width), axis=0)

    def clear_sums(self):
        self.sums[...] = jnp.zeros(self.sums.shape, F32)

    def norm_second(self):
        @pl.loop(0, self.tiles)
        def _(i):
            hidden = self.norm[i] * self.row(1) + self.row(2)
            _, normed, scaled = normalize(hidden + self.tmp[i] + self.row(3), 1.0, 0.0)
            self.out[i] = (normed * self.row(4) + self.row(5)).astype(BF16)
            up = self.cot[i].astype(F32)
            self.add_sum(4, up * normed)
            self.add_sum(5, up)
            after = normalize_back(up, normed, scaled, self.row(4))
            self.add_sum(3, after)
            self.grad[i] = after
            self.low[i] = after.astype(BF16)

    def act_back(self):
        @pl.loop(0, NC * NX)
        def _(t):
            low = self.all_rows(self.low)
            for n in range(3):
                cols = slice(256 * n, 256 * n + 256)
                up = dot(low, self.weight(2, t, 256 * n, 256)).reshape(self.tiles, TILE, 256)
                self.slope[t, :, :, cols] = (up * self.slope[t, :, :, cols].astype(F32)).astype(BF16)

    def contract_grad(self):
        @pl.loop(0, NC * NX)
        def _(t):
            left = self.left[0:self.width, :]
            for n in range(3):
                right = self.all_rows(self.act, t, slice(None), slice(None), slice(256 * n, 256 * n + 256))
                self.put_weight(2, t, 256 * n, dot(left, right))

    def expand_grad(self):
        @pl.loop(0, NC * NX)
        def _(t):
            for n in range(3):
                cols = slice(256 * n, 256 * n + 256)
                grad = dot(self.left[...], self.all_rows(self.slope, t, slice(None), slice(None), cols))
                self.put_weight(1, t, 256 * n, grad[:self.width])
                self.unit_sums[0, t, :, cols] = grad[self.width:self.width + 8]

    def norm_first_back(self):
        @pl.loop(0, self.tiles)
        def _(i):
            grad = self.grad[i] + self.tmp[i]
            normed = self.norm[i]
            self.add_sum(1, grad * normed)
            self.add_sum(2, grad)
            after = normalize_back(grad, normed, self.scaled[i], self.row(1))
            self.add_sum(0, after)
            self.grad[i] = after
            self.low[i] = after.astype(BF16)

    def context_back(self):
        low = low_lanes()

        @pl.loop(0, NC)
        def _(u):
            third = []
            for d in range(NX):
                t = NX * u + d
                grad = dot(self.all_rows(self.low), self.mixer_weight(t))
                self.cgrad[t] = grad[:, :CUT].astype(BF16).reshape(self.seqs, self.length, CUT)
                third.append(grad[:, CUT:])
            pair = jnp.where(low, swap(third[0]), third[1])
            self.cgrad[NC * NX + u] = pair.astype(BF16).reshape(self.seqs, self.length, CUT)

    def heads_back(self, p, s):
        halves = half_rows()
        q, k, v = (self.qkv[i, p, s] for i in range(3))
        up = self.cgrad[p, s]
        up_t = up.T
        q_t = q.T
        dq, dk, dv = [], [], []
        for j in range(2):
            probs = self.probs[p, s, j]
            dv.append(dot(up_t[HEAD * j:HEAD * j + HEAD], probs))
            weight = dot_nt(up * halves[j], v)
            wide = probs.astype(F32)
            grad = wide * (weight - jnp.sum(wide * weight, axis=1, keepdims=True))
            grad = grad.astype(BF16)
            dq.append(dot(grad, k))
            dk.append(dot(q_t[HEAD * j:HEAD * j + HEAD], grad))
        dq = jnp.where(low_lanes(), *dq) * SCALE
        dk = jnp.concatenate(dk, axis=0).T * SCALE
        dv = jnp.concatenate(dv, axis=0).T
        return dq, dk, dv

    def put_stream(self, t, s, lo, value):
        value = value.astype(BF16).reshape(self.per, TILE, CUT)
        self.act[t, pl.ds(self.per * s, self.per), :, lo:lo + CUT] = value

    def attention_back_first(self, hooks):
        @pl.loop(0, NC * NX * self.seqs)
        def _(i):
            run_hooks(hooks, i)
            t, s = i // self.seqs, i % self.seqs
            grads = self.heads_back(t, s)
            for j in range(3):
                self.put_stream(t, s, CUT * j, grads[j])
            self.put_stream(t, s, 3 * CUT, jnp.zeros((self.length, CUT), F32))

    def attention_back_third(self, hooks):
        low = low_lanes()

        @pl.loop(0, NC * self.seqs)
        def _(i):
            run_hooks(hooks, i)
            u, s = i // self.seqs, i % self.seqs
            dq, dk, dv = self.heads_back(NC * NX + u, s)
            self.put_stream(NX * u, s, 4 * CUT, jnp.where(low, dq, swap(dk)))
            self.put_stream(NX * u + 1, s, 4 * CUT, jnp.where(low, swap(dq), dk))
            self.put_stream(NX * u, s, 5 * CUT, jnp.where(low, dv, 0.0))
            self.put_stream(NX * u + 1, s, 5 * CUT, jnp.where(low, swap(dv), 0.0))

    def input_back(self):
        half = self.width // NX

        @pl.loop(0, self.tiles)
        def _(i):
            total = (self.grad[i] + self.tmp[i]).astype(BF16)
            for x in range(NX):
                self.igrad[x, i] = total[:, half * x:half * x + half]

    def stream_grad(self, t, n):
        cols = slice(256 * n, 256 * n + 256)
        grad = dot(self.left[...], self.all_rows(self.act, t, slice(None), slice(None), cols))
        self.unit_sums[1, t, :, cols] = grad[self.width:self.width + 8]
        return grad[:self.width]

    def mixer_grad(self, t, h):
        cols = slice(CUT * h, CUT * h + CUT)
        return dot(self.left2[0:self.width, :], self.all_rows(self.ctx, t, slice(None), slice(None), cols))

    def attention_grad_first(self):
        @pl.loop(0, NC * NX)
        def _(t):
            self.put_weight(0, t, 0, self.stream_grad(t, 0))
            grad = self.stream_grad(t, 1)
            self.put_weight(0, t, 2 * CUT, grad[:, :CUT])
            self.put_weight(0, t, 3 * CUT, self.mixer_grad(t, 0))

    def attention_grad_third(self):
        @pl.loop(0, NC * NX)
        def _(t):
            grad = self.stream_grad(t, 2)
            self.put_weight(0, t, 4 * CUT, grad[:, :CUT])
            self.put_weight(0, t, 5 * CUT, grad[:, CUT:] + self.mixer_grad(t, 1))

    def vector_tiles(self):
        keys = sel_keys(self.width)
        rows = [jnp.sum(self.sums[i], axis=0, keepdims=True) for i in range(6)]
        rows.append(jnp.zeros((2, self.width), F32))
        parts = [jnp.concatenate(rows, axis=0)]
        for i in range(2):
            units = [self.unit_sums[i, t, 0:1, :] for t in range(NC * NX)]
            parts.append(jnp.concatenate(units + [jnp.zeros((4, self.width), F32)], axis=0))
        split = []
        for part in parts:
            high = part.astype(BF16)
            split.append(jnp.concatenate([high, (part - high.astype(F32)).astype(BF16)], axis=0))

        @pl.loop(0, NZ * NY)
        def _(b):
            z, y = b // NY, b % NY
            got = []
            for key, part in zip(keys, split):
                both = dot_nt(part, sel_matrix(key, b))
                got.append(both[:8] + both[8:])
            for t in range(NC * NX):
                self.vtiles[t // NX, t % NX, z, y] = jnp.concatenate(
                    [got[0][:6], got[1][t:t + 1], got[2][t:t + 1]], axis=0
                )


def layer_scratch(seqs, length, width):
    tiles = seqs * length // TILE
    blocks = NC * NX
    pairs = 3 * blocks // 2
    rows = seqs * length
    nr = width // (NZ * NY)
    return [
        pltpu.VMEM((3, NC, NX, NZ, NY, nr, width), BF16),
        pltpu.VMEM((tiles, TILE, width), BF16),
        pltpu.VMEM((tiles, TILE, width), BF16),
        pltpu.VMEM((3, pairs, seqs, length, CUT), BF16),
        pltpu.VMEM((pairs, seqs, 2, length, length), BF16),
        pltpu.VMEM((blocks, tiles, TILE, 2 * CUT), BF16),
        pltpu.VMEM((tiles, TILE, width), F32),
        pltpu.VMEM((tiles, TILE, width), F32),
        pltpu.VMEM((tiles, TILE, 1), F32),
        pltpu.VMEM((tiles, TILE, width), BF16),
        pltpu.VMEM((blocks, tiles, TILE, width), BF16),
        pltpu.VMEM((blocks, tiles, TILE, width), BF16),
        pltpu.VMEM((tiles, TILE, width), F32),
        pltpu.VMEM((tiles, TILE, width), BF16),
        pltpu.VMEM((pairs, seqs, length, CUT), BF16),
        pltpu.VMEM((width + 16, rows), BF16),
        pltpu.VMEM((width + 16, rows), BF16),
        pltpu.VMEM((3, blocks, 8, width), F32),
        pltpu.VMEM((6, 8, width), F32),
        pltpu.VMEM((2, blocks, 8, width), F32),
    ]


class Gather:
    def __init__(self, me, w, v, sems, vsems):
        self.me, self.w, self.v, self.sems, self.vsems = me, w, v, sems, vsems

    def hop(self, k, i):
        p, lo, size, route = GATHER_PARTS[k]
        me = self.me
        at = {axis: slice(None) if axis in route[:i] else me.own(axis) for axis in "xyz"}
        slot = self.w.at[p, me.c, at["x"], at["z"], at["y"], :, pl.ds(lo, size)]
        first = {"z": 0, "x": NZ - 1, "y": NZ}[route[i]]
        return [
            remote(slot, slot, self.sems, 5 * k + first + j, peer) for j, peer in enumerate(me.along(route[i]))
        ]

    def start(self, k, i):
        if i > 0:
            for copy in self.hop(k, i - 1):
                copy.wait_recv()
        for copy in self.hop(k, i):
            copy.start()

    def core(self, group):
        p, lo, size, parts = GATHER_GROUPS[group]
        slot = self.w.at[p, self.me.c, :, :, :, :, pl.ds(lo, size)]
        return remote(slot, slot, self.sems, 5 * len(GATHER_PARTS) + group, self.me.core())

    def start_core(self, group):
        for k in GATHER_GROUPS[group][3]:
            for copy in self.hop(k, 2):
                copy.wait_recv()
        self.core(group).start()

    def arrived(self, group):
        self.core(group).wait_recv()

    def left(self, group):
        for k in GATHER_GROUPS[group][3]:
            for i in range(3):
                for copy in self.hop(k, i):
                    copy.wait_send()
        self.core(group).wait_send()

    def small(self):
        me, v = self.me, self.v
        def same(slot, index, peer):
            return remote(slot, slot, self.vsems, index, peer)
        return [
            [same(v.at[me.c, me.x, me.z, me.y], s, peer) for s, peer in enumerate(me.along("z"))],
            [same(v.at[me.c, me.x, :, me.y], 3, me.xp())],
            [same(v.at[me.c, :, :, me.y], 4, me.yp())],
            [same(v.at[me.c], 5, me.core())],
        ]

    def small_step(self, i):
        steps = self.small()
        if i > 0:
            for copy in steps[i - 1]:
                copy.wait_recv()
        if i < len(steps):
            for copy in steps[i]:
                copy.start()

    def small_left(self):
        for copy in sum(self.small(), []):
            copy.wait_send()


GATHER_PARTS = (
    (0, 0, 256, "zxy"), (0, 256, 256, "zyx"),
    (0, 512, 128, "zxy"), (0, 640, 128, "zyx"),
    (1, 0, 256, "zxy"), (1, 256, 384, "zyx"), (1, 640, 128, "yxz"),
    (2, 0, 384, "zxy"), (2, 384, 256, "zyx"), (2, 640, 128, "xyz"),
)
GATHER_GROUPS = ((0, 0, 512, (0, 1)), (0, 512, 256, (2, 3)), (1, 0, 768, (4, 5, 6)), (2, 0, 768, (7, 8, 9)))
SCATTER_PARTS = (
    (2, 0, 512, "yxz"), (2, 512, 128, "xyz"), (2, 640, 128, "zyx"),
    (1, 0, 512, "yxz"), (1, 512, 128, "xyz"), (1, 640, 128, "zyx"),
    (0, 0, 384, "yxz"), (0, 384, 128, "xyz"),
    (0, 512, 128, "yxz"), (0, 640, 128, "xyz"),
)
SCATTER_GROUPS = ((2, 0, 768, (0, 1, 2)), (1, 0, 768, (3, 4, 5)), (0, 0, 512, (6, 7)), (0, 512, 256, (8, 9)))


class Scatter:
    def __init__(self, me, g, v, bufs, sems, vsems, osems, out, outs, ig, igs):
        self.me, self.g, self.v = me, g, v
        self.rc, self.rb, self.vc, self.vy, self.vx, self.vz = bufs
        self.sems, self.vsems, self.osems = sems, vsems, osems
        self.out, self.outs, self.ig, self.igs = out, outs, ig, igs

    def core(self, group):
        p, lo, size, _ = SCATTER_GROUPS[group]
        me, cols = self.me, pl.ds(lo, size)
        return remote(
            self.g.at[p, 1 - me.c, :, :, :, :, cols], self.rc.at[p, :, :, :, :, cols],
            self.sems, 9 * len(SCATTER_PARTS) + group, me.core(),
        )

    def start_core(self, group):
        self.core(group).start()

    def add_core(self, group):
        p, lo, size, _ = SCATTER_GROUPS[group]
        c, cols = self.me.c, slice(lo, lo + size)
        self.core(group).wait_recv()

        @pl.loop(0, NZ)
        def _(j):
            for i in range(NX):
                for k in range(NY):
                    self.g[p, c, i, j, k, :, cols] = self.g[p, c, i, j, k, :, cols] + self.rc[p, i, j, k, :, cols]

    def plan(self, k, i):
        p, lo, size, route = SCATTER_PARTS[k]
        me = self.me
        axis = route[i]
        done = {a: me.own(a) for a in route[:i]}
        firsts = (0, 8, 12) if route[2] == "z" else (0, 12, 14)
        every = slice(None)
        moves = []
        at = firsts[i]
        for peer, other in zip(me.along(axis), me.others(axis)):
            spare = [a for a in "xyz" if a != axis and a not in done]
            inner = "z" if "z" in spare else (spare[-1] if spare else None)
            outer = [a for a in spare if a != inner]
            for o in range(2 if outer else 1):
                send = dict(done)
                if outer:
                    send[outer[0]] = o
                if inner:
                    send[inner] = every
                keep = dict(send)
                send[axis], keep[axis] = other, me.own(axis)
                count = None if inner is None else (NZ if inner == "z" else 2)
                moves.append((send, keep, at, count, peer))
                at += 1 if count is None else count
        return p, lo, size, moves

    def hop(self, k, i):
        p, lo, size, moves = self.plan(k, i)
        me, cols = self.me, pl.ds(lo, size)
        base = 9 * k + (0, 6, 8)[i] if SCATTER_PARTS[k][3][0] == "z" else 9 * k + (0, 2, 3)[i]
        copies = []
        for j, (send, _, at, count, peer) in enumerate(moves):
            src = self.g.at[p, me.c, send["x"], send["z"], send["y"], :, cols]
            dst = self.rb.at[p, at, :, cols] if count is None else self.rb.at[p, pl.ds(at, count), :, cols]
            copies.append(remote(src, dst, self.sems, base + j, peer))
        return copies

    def start(self, k, i):
        if i > 0:
            self.add(k, i - 1)
        for copy in self.hop(k, i):
            copy.start()

    def add(self, k, i):
        p, lo, size, moves = self.plan(k, i)
        c, cols = self.me.c, slice(lo, lo + size)
        for copy in self.hop(k, i):
            copy.wait_recv()
        terms = {}
        for _, keep, at, count, _ in moves:
            inner = [a for a in "xyz" if isinstance(keep[a], slice)]
            for n in range(1 if count is None else count):
                spot = dict(keep)
                if inner:
                    spot[inner[0]] = n
                name = tuple(spot[a] if isinstance(spot[a], int) else a for a in "xyz")
                terms.setdefault(name, (spot, []))[1].append(at + n)
        for spot, places in terms.values():
            ref = self.g.at[p, c, spot["x"], spot["z"], spot["y"], :, cols]
            if len(places) == 1:
                ref[...] = ref[...] + self.rb[p, places[0], :, cols]
            else:
                total = ref[...].astype(F32)
                for n in places:
                    total = total + self.rb[p, n, :, cols].astype(F32)
                ref[...] = total.astype(BF16)

    def total(self, k):
        p, lo, size, moves = self.plan(k, 2)
        me, cols = self.me, slice(lo, lo + size)
        for copy in self.hop(k, 2):
            copy.wait_recv()
        total = self.g[p, me.c, me.x, me.z, me.y, :, cols].astype(F32)
        for _, _, at, _, _ in moves:
            total = total + self.rb[p, at, :, cols].astype(F32)
        return total

    def left(self, group):
        self.core(group).wait_send()
        for k in SCATTER_GROUPS[group][3]:
            for i in range(3):
                for copy in self.hop(k, i):
                    copy.wait_send()

    def small(self, i):
        me, v, sems = self.me, self.v, self.vsems
        if i == 0:
            return [remote(v.at[1 - me.c], self.vc, sems, 0, me.core())]
        if i == 1:
            return [remote(v.at[me.c, :, :, 1 - me.y], self.vy, sems, 1, me.yp())]
        if i == 2:
            return [remote(v.at[me.c, 1 - me.x, :, me.y], self.vx, sems, 2, me.xp())]
        return [
            remote(v.at[me.c, me.x, (me.z + s) % NZ, me.y], self.vz.at[s - 1], sems, 2 + s, me.zp(s))
            for s in range(1, NZ)
        ]

    def small_step(self, i):
        me, v = self.me, self.v
        if i > 0:
            for copy in self.small(i - 1):
                copy.wait_recv()
        if i == 1:
            v[me.c] = v[me.c] + self.vc[...]
        elif i == 2:
            v[me.c, :, :, me.y] = v[me.c, :, :, me.y] + self.vy[...]
        elif i == 3:
            v[me.c, me.x, :, me.y] = v[me.c, me.x, :, me.y] + self.vx[...]
        elif i == 4:
            total = v[me.c, me.x, me.z, me.y]
            for s in range(1, NZ):
                total = total + self.vz[s - 1]
            return total
        for copy in self.small(i):
            copy.start()

    def small_left(self):
        for i in range(4):
            for copy in self.small(i):
                copy.wait_send()

    def outputs(self):
        me = self.me
        t = me.x * NC + me.c
        return [remote(self.out, self.outs.at[t], self.osems, i, peer) for i, peer in enumerate((me.xp(), me.core()))]

    def output_local(self, sem):
        return pltpu.make_async_copy(self.out, self.outs.at[self.me.x * NC + self.me.c], sem)

    def output_forward(self):
        me = self.me
        t = (1 - me.x) * NC + me.c
        return remote(self.outs.at[t], self.outs.at[t], self.osems, 4, me.core())

    def grads(self):
        me = self.me
        t = me.x * NC + me.c
        return [
            remote(self.ig.at[1 - me.x], self.igs.at[t], self.osems, 2, me.xp()),
            remote(self.ig.at[me.x], self.igs.at[t], self.osems, 3, me.core()),
        ]

    def grad_local(self, sem):
        return pltpu.make_async_copy(self.ig.at[self.me.x], self.igs.at[self.me.x * NC + self.me.c], sem)

    def grad_forward(self):
        me = self.me
        t = (1 - me.x) * NC + me.c
        return remote(self.igs.at[t], self.igs.at[t], self.osems, 5, me.core())


def step_kernel(
    x_in, cot_in, lens, tw, mw, ew, cw, vec_in,
    outs, igs, triple_out, mixer_out, expand_out, contract_out, small_out,
    w, v, vtiles, out, ig,
    x, cot, qkv, probs, ctx, tmp, norm, scaled, hidden, act, slope, grad, low, cgrad, left, left2, vec, sums,
    unit_sums,
    rc, rb, vc, vy, vx, vz,
    gsems, gvsems, sems, vsems, osems, lsems,
):
    me = Place()
    t = lax.axis_index("tensor")
    seqs = qkv.shape[2]
    own = [w.at[p, me.c, me.x, me.z, me.y] for p in range(3)]
    load_v = pltpu.make_async_copy(vec_in, v.at[me.c, me.x, me.z, me.y], lsems.at[3])
    load_e = pltpu.make_async_copy(ew, own[1], lsems.at[2])
    load_c = pltpu.make_async_copy(cw, own[2], lsems.at[6])
    load_x = pltpu.make_async_copy(x_in.at[t], x, lsems.at[0])
    load_cot = pltpu.make_async_copy(cot_in.at[t], cot, lsems.at[1])
    me.signal()
    for copy in (load_v, load_e, load_c, load_x, load_cot):
        copy.start()
    pack_attention(tw, mw, own[0])
    gather = Gather(me, w, v, gsems, gvsems)
    layer = Layer(
        w=w, x=x, cot=cot, qkv=qkv, probs=probs, ctx=ctx, tmp=tmp, norm=norm, scaled=scaled, hidden=hidden, act=act,
        slope=slope, grad=grad, low=low, cgrad=cgrad, left=left, left2=left2, vec=vec, sums=sums, unit_sums=unit_sums,
        v=v, out=out, igrad=ig, vtiles=vtiles, lens=lens, first=t * seqs,
    )
    scatter = Scatter(me, w, vtiles, (rc, rb, vc, vy, vx, vz), sems, vsems, osems, out, outs, ig, igs)
    me.meet()
    for k in range(4):
        gather.start(k, 0)
    load_v.wait()
    gather.small_step(0)
    load_e.wait()
    load_c.wait()
    for k in range(4, 10):
        gather.start(k, 0)
    layer.clear_sums()
    load_x.wait()
    load_cot.wait()
    gather.small_step(1)
    gather.start(6, 1)
    gather.start(9, 1)
    gather.start(0, 1)
    gather.start(1, 1)
    gather.small_step(2)
    gather.start(2, 1)
    gather.start(3, 1)
    gather.small_step(3)
    gather.start(6, 2)
    gather.start(9, 2)
    gather.start(0, 2)
    gather.start(1, 2)
    gather.start(2, 2)
    gather.start(3, 2)
    gather.small_step(4)
    layer.vectors()
    gather.start_core(0)
    gather.arrived(0)
    layer.projections_first()
    gather.start(4, 1)
    gather.start(5, 1)
    gather.start_core(1)

    def attention_a():
        gather.start(4, 2)
        gather.start(5, 2)

    def attention_b():
        gather.start(7, 1)
        gather.start(8, 1)

    layer.attention_first({6: attention_a, 7: attention_b})
    gather.arrived(1)
    layer.projections_third()
    layer.attention_third({})
    layer.mix()
    gather.start_core(2)
    layer.norm_first()
    gather.start(7, 2)
    gather.start(8, 2)
    gather.arrived(2)
    layer.expand({})
    gather.start_core(3)
    gather.arrived(3)
    layer.times_back(2, act)
    layer.norm_second()
    for copy in scatter.outputs():
        copy.start()
    scatter.output_local(lsems.at[4]).start()
    layer.transposed(low, left)
    layer.act_back()
    gather.left(3)
    layer.contract_grad()
    scatter.start_core(0)
    layer.times_back(1, slope)
    scatter.add_core(0)
    for k in range(3):
        scatter.start(k, 0)
    layer.transposed(hidden, left)
    gather.left(2)
    layer.expand_grad()
    scatter.start_core(1)
    layer.norm_first_back()
    layer.transposed(low, left2)
    layer.context_back()
    scatter.add_core(1)
    for k in range(3, 6):
        scatter.start(k, 0)

    def back_a():
        scatter.start(1, 1)
        scatter.start(2, 1)

    def back_b():
        scatter.start(0, 1)

    def back_c():
        scatter.outputs()[0].wait_recv()
        scatter.output_forward().start()

    layer.attention_back_first({2: back_a, 4: back_c, 6: back_b})
    layer.times_back(0, act, 0, 3 * CUT)
    layer.transposed(x, left)
    gather.left(0)
    layer.attention_grad_first()
    scatter.start_core(2)
    layer.attention_back_third({})
    scatter.add_core(2)
    scatter.start(6, 0)
    scatter.start(7, 0)
    layer.times_back(0, act, 4 * CUT, 2 * CUT, True)
    gather.left(1)
    layer.attention_grad_third()
    scatter.start_core(3)
    layer.input_back()
    for copy in scatter.grads():
        copy.start()
    scatter.grad_local(lsems.at[5]).start()
    scatter.add_core(3)
    scatter.start(8, 0)
    scatter.start(9, 0)
    scatter.start(4, 1)
    scatter.start(5, 1)
    layer.vector_tiles()
    scatter.small_step(0)
    scatter.start(1, 2)
    scatter.start(2, 2)
    scatter.start(0, 2)
    scatter.start(3, 1)
    scatter.small_step(1)
    scatter.start(7, 1)
    scatter.start(4, 2)
    scatter.start(5, 2)
    scatter.small_step(2)
    scatter.start(9, 1)
    scatter.start(6, 1)
    scatter.small_step(3)
    scatter.start(8, 1)
    for k in range(3):
        scatter_out(scatter, k, contract_out)
    scatter.start(3, 2)
    scatter.start(7, 2)
    scatter.grads()[0].wait_recv()
    scatter.grad_forward().start()
    scatter.start(9, 2)
    scatter.start(6, 2)
    scatter.start(8, 2)
    for k in range(3, 6):
        scatter_out(scatter, k, expand_out)
    small_out[...] = scatter.small_step(4)
    for k in (7, 9, 6, 8):
        scatter_out(scatter, k, tmp.at[0])
    unpack_attention(tmp[0], triple_out, mixer_out)
    scatter.outputs()[1].wait_recv()
    scatter.grads()[1].wait_recv()
    for copy in (scatter.output_forward(), scatter.grad_forward()):
        copy.wait()
    for copy in scatter.outputs() + scatter.grads():
        copy.wait_send()
    scatter.output_local(lsems.at[4]).wait()
    scatter.grad_local(lsems.at[5]).wait()
    gather.small_left()
    scatter.small_left()
    for group in range(4):
        scatter.left(group)


def scatter_out(scatter, k, ref):
    _, lo, size, _ = SCATTER_PARTS[k]
    ref[:, lo:lo + size] = scatter.total(k)


def pack_attention(tw, mw, slot):
    mixer = mw[...].T
    for i in range(3):
        slot[:, CUT * i:CUT * i + CUT] = tw[i, :, 0:CUT]
    slot[:, 3 * CUT:4 * CUT] = mixer[:, 0:CUT]
    slot[:, 4 * CUT:5 * CUT] = jnp.concatenate([tw[0, :, CUT:], tw[1, :, CUT:]], axis=1)
    slot[:, 5 * CUT:6 * CUT] = jnp.concatenate([tw[2, :, CUT:], mixer[:, CUT:]], axis=1)


def unpack_attention(total, triple_out, mixer_out):
    for i in range(3):
        triple_out[i, :, 0:CUT] = total[:, CUT * i:CUT * i + CUT]
        triple_out[i, :, CUT:] = total[:, 4 * CUT + HEAD * i:4 * CUT + HEAD * i + HEAD]
    mixer_out[0:CUT] = total[:, 3 * CUT:4 * CUT].T
    mixer_out[CUT:] = total[:, 5 * CUT + HEAD:].T


def step_call(x, cot, lengths, tw, mw, ew, cw, vec, seqs):
    pairs, length, width = x.shape
    tiles = seqs * length // TILE
    blocks = NX * NC
    nr, feat = width // (NZ * NY), width // blocks
    shape = (blocks, tiles, TILE, width)
    vmem = pl.BlockSpec(memory_space=pltpu.VMEM)
    hbm = pl.BlockSpec(memory_space=pl.ANY)
    layer = layer_scratch(seqs, length, width)
    small = (8, 128)
    return pl.pallas_call(
        step_kernel,
        out_shape=(
            jax.ShapeDtypeStruct(shape, BF16),
            jax.ShapeDtypeStruct((blocks, tiles, TILE, width // NX), BF16),
            jax.ShapeDtypeStruct((3, nr, feat), F32),
            jax.ShapeDtypeStruct((feat, nr), F32),
            jax.ShapeDtypeStruct((nr, width), F32),
            jax.ShapeDtypeStruct((nr, width), F32),
            jax.ShapeDtypeStruct(small, F32),
        ),
        in_specs=[hbm, hbm, pl.BlockSpec(memory_space=pltpu.SMEM), vmem, vmem, hbm, hbm, hbm],
        out_specs=(hbm, hbm, vmem, vmem, vmem, vmem, vmem),
        scratch_shapes=[
            layer[0],
            pltpu.VMEM((NC, NX, NZ, NY) + small, F32),
            pltpu.VMEM((NC, NX, NZ, NY) + small, F32),
            pltpu.VMEM((tiles, TILE, width), BF16),
            pltpu.VMEM((NX, tiles, TILE, width // NX), BF16),
        ] + layer[1:] + [
            pltpu.VMEM((3, NX, NZ, NY, nr, width), BF16),
            pltpu.VMEM((3, 15, nr, width), BF16),
            pltpu.VMEM((NX, NZ, NY) + small, F32),
            pltpu.VMEM((NX, NZ) + small, F32),
            pltpu.VMEM((NZ,) + small, F32),
            pltpu.VMEM((NZ - 1,) + small, F32),
            pltpu.SemaphoreType.DMA((2, 5 * len(GATHER_PARTS) + len(GATHER_GROUPS))),
            pltpu.SemaphoreType.DMA((2, 6)),
            pltpu.SemaphoreType.DMA((2, 9 * len(SCATTER_PARTS) + len(SCATTER_GROUPS))),
            pltpu.SemaphoreType.DMA((2, 6)),
            pltpu.SemaphoreType.DMA((2, 6)),
            pltpu.SemaphoreType.DMA((7,)),
        ],
        compiler_params=pltpu.CompilerParams(
            collective_id=0, has_side_effects=True, vmem_limit_bytes=67043328
        ),
    )(x.reshape(shape), cot.reshape(shape), lengths, tw, mw, ew, cw, vec)


def layer_step(x_seq, lengths, cot, w, d_vec, e_bias, p_bias):
    seqs, length, width = x_seq.shape
    rows = seqs * length
    blocks = w.shape[1]
    feat = width // blocks
    heads = feat // HEAD
    mixer_shift, gain_one, shift_one, contract_shift, gain_two, shift_two = d_vec
    x = x_seq.reshape(rows, width)
    att = w[0]
    cut = 2 * HEAD
    def columns(i):
        return jnp.concatenate(
            [att[:, :, i * cut:(i + 1) * cut], att[:, :, 4 * cut + i * HEAD:4 * cut + (i + 1) * HEAD]], axis=2
        )
    wq, wk, wv, wm = (columns(i) for i in range(4))
    def project(weight, bias):
        out = jnp.einsum("rd,tde->rte", x, weight, preferred_element_type=F32)
        if bias is not None:
            out = out + bias
        return out.astype(BF16).reshape(seqs, length, blocks * heads, HEAD)
    queries = project(wq, p_bias[0])
    keys = project(wk, None)
    values = project(wv, p_bias[1])
    valid = lax.broadcasted_iota(jnp.int32, (seqs, 1, 1, length), 3) < lengths[:, None, None, None]
    raw = jnp.einsum("sqhd,skhd->shqk", queries, keys, preferred_element_type=F32) * SCALE
    raw = jnp.where(valid, raw, MASKED)
    peak = jnp.max(raw, axis=-1, keepdims=True)
    powers = jnp.exp(raw - peak)
    probs = powers / jnp.sum(powers, axis=-1, keepdims=True)
    attention = probs.astype(BF16)
    context = jnp.einsum("shqk,skhd->sqhd", attention, values, preferred_element_type=F32)
    context = context.astype(BF16).reshape(rows, blocks, feat)
    mixed = jnp.einsum("rtc,tdc->rd", context, wm, preferred_element_type=F32)
    hidden, normed_one, scaled_one = normalize(x.astype(F32) + mixed + mixer_shift, gain_one, shift_one)
    hidden_low = hidden.astype(BF16)
    before = jnp.einsum("rd,tdf->rtf", hidden_low, w[1], preferred_element_type=F32) + e_bias
    activated = jax.nn.gelu(before, approximate=False).astype(BF16)
    branch = jnp.einsum("rtf,tdf->rd", activated, w[2], preferred_element_type=F32)
    result, normed_two, scaled_two = normalize(hidden + branch + contract_shift, gain_two, shift_two)
    outputs = result.astype(BF16)
    up = cot.reshape(rows, width).astype(F32)
    gain_two_grad = jnp.sum(up * normed_two, axis=0)
    shift_two_grad = jnp.sum(up, axis=0)
    after_two = normalize_back(up, normed_two, scaled_two, gain_two)
    contract_shift_grad = jnp.sum(after_two, axis=0)
    two_low = after_two.astype(BF16)
    contract_grad = jnp.einsum("rd,rtf->tdf", two_low, activated, preferred_element_type=F32)
    act_grad = jnp.einsum("rd,tdf->rtf", two_low, w[2], preferred_element_type=F32)
    _, gelu_back = jax.vjp(partial(jax.nn.gelu, approximate=False), before)
    before_grad = gelu_back(act_grad)[0].astype(BF16)
    expand_grad = jnp.einsum("rd,rtf->tdf", hidden_low, before_grad, preferred_element_type=F32)
    e_bias_grad = jnp.sum(before_grad, axis=0, dtype=F32)
    hidden_part = jnp.einsum("rtf,tdf->rd", before_grad, w[1], preferred_element_type=F32)
    hidden_grad = after_two + hidden_part
    after_one = normalize_back(hidden_grad, normed_one, scaled_one, gain_one)
    gain_one_grad = jnp.sum(hidden_grad * normed_one, axis=0)
    shift_one_grad = jnp.sum(hidden_grad, axis=0)
    mixer_shift_grad = jnp.sum(after_one, axis=0)
    one_low = after_one.astype(BF16)
    mixer_grad = jnp.einsum("rd,rtc->tdc", one_low, context, preferred_element_type=F32)
    context_grad = jnp.einsum("rd,tdc->rtc", one_low, wm, preferred_element_type=F32).astype(BF16)
    context_grad = context_grad.reshape(seqs, length, blocks * heads, HEAD)
    value_grad = jnp.einsum("shqk,sqhd->skhd", attention, context_grad, preferred_element_type=F32)
    weight_grad = jnp.einsum("sqhd,skhd->shqk", context_grad, values, preferred_element_type=F32)
    score_grad = probs * (weight_grad - jnp.sum(probs * weight_grad, axis=-1, keepdims=True))
    score_grad = score_grad.astype(BF16)
    query_grad = jnp.einsum("shqk,skhd->sqhd", score_grad, keys, preferred_element_type=F32) * SCALE
    key_grad = jnp.einsum("shqk,sqhd->skhd", score_grad, queries, preferred_element_type=F32) * SCALE
    streams = [g.astype(BF16).reshape(rows, blocks, feat) for g in (query_grad, key_grad, value_grad)]
    p_grad = [jnp.sum(streams[i], axis=0, dtype=F32) for i in (0, 2)]
    tgrads = [jnp.einsum("rd,rte->tde", x, s, preferred_element_type=F32) for s in streams] + [mixer_grad]
    att_grad = jnp.concatenate([g[:, :, :cut] for g in tgrads] + [g[:, :, cut:] for g in tgrads], axis=2)
    part = sum(
        jnp.einsum("rte,tde->rd", s, wt, preferred_element_type=F32) for s, wt in zip(streams, (wq, wk, wv))
    )
    input_grad = (after_one + part).astype(BF16)
    grads = jnp.stack([att_grad, expand_grad, contract_grad]).astype(BF16)
    vecs = jnp.stack(
        [mixer_shift_grad, gain_one_grad, shift_one_grad, contract_shift_grad, gain_two_grad, shift_two_grad]
    )
    return outputs, input_grad, grads, vecs, e_bias_grad, jnp.stack(p_grad)


def make_on_device(sizes):
    fast = sizes == {"batch": NZ * NY, "tensor": NX * NC}

    def on_device(
        inputs, lengths, triple_weight, pair_bias, mixer_weight, mixer_bias, first_gain, first_shift,
        expand_weight, expand_bias, contract_weight, contract_bias, second_gain, second_shift, cotangent,
    ):
        pairs, length, width = inputs.shape
        n_tensor, n_batch = sizes["tensor"], sizes["batch"]
        nr = width // n_batch
        own_pairs = pairs // n_tensor
        t = lax.axis_index("tensor")
        feat = width // n_tensor
        if fast:
            def lay(v, lo=0):
                return jnp.pad(v.reshape(-1).astype(F32), (lo, 128 - lo - v.size))
            small = [mixer_bias, first_gain, first_shift, contract_bias, second_gain, second_shift, expand_bias]
            half = pair_bias.shape[1]
            small = [lay(v) for v in small] + [lay(pair_bias[0]) + lay(pair_bias[1], half)]
            place = lax.broadcasted_iota(jnp.int32, (8, 128), 0)
            vec = jnp.zeros((8, 128), F32)
            for i, v in enumerate(small):
                vec = jnp.where(place == i, v[None, :], vec)
            outs, ig, triple_grad, mixer_grad, expand_grad, contract_grad, vred = step_call(
                inputs, cotangent, lengths, triple_weight, mixer_weight, expand_weight, contract_weight.T,
                vec, own_pairs,
            )
            ig = lax.dynamic_slice_in_dim(ig, t % NC * feat, feat, 3)
            outs = outs.reshape(pairs, length, width)
            ig = ig.reshape(pairs, length, feat).astype(F32)
            contract_grad = contract_grad.T
        else:
            cut = 2 * HEAD
            four = [triple_weight[0], triple_weight[1], triple_weight[2], mixer_weight.T]
            att = jnp.concatenate([m[:, :cut] for m in four] + [m[:, cut:] for m in four], axis=1)
            pack = jnp.stack([att, expand_weight, contract_weight.T])
            def row(v):
                return jnp.pad(v.reshape(1, -1), ((0, 0), (0, 128 - v.size)))
            vec = jnp.concatenate(
                [row(v) for v in (mixer_bias, first_gain, first_shift, contract_bias, second_gain, second_shift,
                                  expand_bias, pair_bias)] + [jnp.zeros((8, 128), BF16)], axis=0
            )
            w = lax.all_gather(lax.all_gather(pack, "batch", axis=1, tiled=True), "tensor", axis=1)
            v = lax.all_gather(lax.all_gather(vec, "batch"), "tensor")
            d_vec = v[0, :, :6, :nr].transpose(1, 0, 2).reshape(6, width).astype(F32)
            e_bias = v[:, :, 6, :nr].transpose(0, 2, 1).reshape(n_tensor, width).astype(F32)
            p_bias = v[:, :, 7, :2 * feat // n_batch].reshape(n_tensor, n_batch, 2, feat // n_batch)
            p_bias = p_bias.transpose(2, 0, 3, 1).reshape(2, n_tensor, feat).astype(F32)
            mine = partial(lax.dynamic_slice_in_dim, start_index=t * own_pairs, slice_size=own_pairs, axis=0)
            outputs, input_grad, grads, vecs, e_grad, p_grad = layer_step(
                mine(inputs), mine(lengths), mine(cotangent), w, d_vec, e_bias, p_bias
            )
            rows = own_pairs * length
            dv = jnp.broadcast_to(vecs.reshape(1, 6, n_batch, nr).transpose(0, 2, 1, 3), (n_tensor, n_batch, 6, nr))
            ev = e_grad.reshape(n_tensor, nr, n_batch).transpose(0, 2, 1)[:, :, None]
            pv = p_grad.reshape(2, n_tensor, feat // n_batch, n_batch).transpose(1, 3, 0, 2)
            pv = pv.reshape(n_tensor, n_batch, 1, 2 * feat // n_batch)
            lanes = lambda a: jnp.pad(a, ((0, 0), (0, 0), (0, 0), (0, 128 - a.shape[-1])))
            tiles = jnp.concatenate([lanes(dv), lanes(ev), lanes(pv)], axis=2)
            grads = lax.psum_scatter(grads.astype(F32), "tensor", scatter_dimension=1)
            red = lax.psum_scatter(grads, "batch", scatter_dimension=1, tiled=True)
            vred = lax.psum_scatter(lax.psum_scatter(tiles, "tensor"), "batch")
            outs = lax.all_gather(outputs, "tensor").reshape(pairs, length, width)
            ig = lax.all_to_all(
                input_grad.reshape(rows, n_tensor, feat), "tensor", split_axis=1, concat_axis=0, tiled=True
            )
            ig = ig.reshape(pairs, length, feat).astype(F32)
            att_g = red[0]
            four_g = [
                jnp.concatenate([att_g[:, i * cut:(i + 1) * cut], att_g[:, 4 * cut + i * HEAD:4 * cut + (i + 1) * HEAD]], axis=1)
                for i in range(4)
            ]
            triple_grad, mixer_grad = jnp.stack(four_g[:3]), four_g[3].T
            expand_grad, contract_grad = red[1], red[2].T
        return (
            outs,
            ig,
            triple_grad,
            vred[7, :2 * feat // n_batch].reshape(pair_bias.shape),
            mixer_grad,
            vred[0, :nr],
            vred[1, :nr],
            vred[2, :nr],
            expand_grad,
            vred[6, :nr].reshape(expand_bias.shape),
            contract_grad,
            vred[3, :nr],
            vred[4, :nr],
            vred[5, :nr],
        )

    return on_device


def solution(mesh):
    return jax.shard_map(
        make_on_device(dict(mesh.shape)),
        mesh=mesh,
        in_specs=(
            P("batch", None, None),
            P("batch"),
            P(None, "batch", "tensor"),
            P(None, "tensor", "batch"),
            P("tensor", "batch"),
            P("batch"),
            P("batch"),
            P("batch"),
            P("batch", "tensor"),
            P("tensor", "batch"),
            P("tensor", "batch"),
            P("batch"),
            P("batch"),
            P("batch"),
            P("batch", None, None),
        ),
        out_specs=(
            P("batch", None, None),
            P("batch", None, "tensor"),
            P(None, "batch", "tensor"),
            P(None, "tensor", "batch"),
            P("tensor", "batch"),
            P("batch"),
            P("batch"),
            P("batch"),
            P("batch", "tensor"),
            P("tensor", "batch"),
            P("tensor", "batch"),
            P("batch"),
            P("batch"),
            P("batch"),
        ),
        check_vma=False,
    )
```

```python
from functools import partial

import jax
import jax.numpy as jnp
from jax import lax
from jax.experimental import pallas as pl
from jax.experimental.pallas import tpu as pltpu
from jax.sharding import PartitionSpec as P

HEAD = 64
EPS = 1e-12
SCALE = 0.125
MASKED = -1e30
MESH = pl.DeviceIdType.MESH
F32 = jnp.float32
BF16 = jnp.bfloat16
NZ, NY, NX, NC = 4, 2, 2, 2


class Place:
    def __init__(self):
        b = lax.axis_index("batch")
        t = lax.axis_index("tensor")
        self.z, self.y = b // NY, b % NY
        self.x, self.c = t // NC, t % NC

    def at(self, z=None, y=None, x=None, c=None):
        z = self.z if z is None else z
        y = self.y if y is None else y
        x = self.x if x is None else x
        c = self.c if c is None else c
        return (z * NY + y, x * NC + c)

    def core(self):
        return self.at(c=1 - self.c)

    def xp(self):
        return self.at(x=1 - self.x)

    def yp(self):
        return self.at(y=1 - self.y)

    def zp(self, step):
        return self.at(z=(self.z + step) % NZ)

    def peers(self):
        return [self.core(), self.xp(), self.yp()] + [self.zp(s) for s in range(1, NZ)]

    def signal(self):
        barrier = pltpu.get_barrier_semaphore()
        for peer in self.peers():
            pl.semaphore_signal(barrier, inc=1, device_id=peer, device_id_type=MESH)

    def meet(self):
        pl.semaphore_wait(pltpu.get_barrier_semaphore(), len(self.peers()))

    def own(self, axis):
        return {"x": self.x, "y": self.y, "z": self.z}[axis]

    def others(self, axis):
        if axis == "z":
            return [(self.z + s) % NZ for s in range(1, NZ)]
        return [1 - self.own(axis)]

    def along(self, axis):
        if axis == "z":
            return [self.zp(s) for s in range(1, NZ)]
        return [self.xp() if axis == "x" else self.yp()]


def remote(src, dst, sems, index, peer):
    return pltpu.make_async_remote_copy(
        src_ref=src,
        dst_ref=dst,
        send_sem=sems.at[0, index],
        recv_sem=sems.at[1, index],
        device_id=peer,
        device_id_type=MESH,
    )


def normalize(value_rows, gain, shift):
    centred = value_rows - jnp.mean(value_rows, axis=-1, keepdims=True)
    scaled = lax.rsqrt(jnp.mean(centred * centred, axis=-1, keepdims=True) + EPS)
    normed = centred * scaled
    return (normed * gain + shift, normed, scaled)


def normalize_back(grad, normed, scaled, gain):
    weighted = grad * gain
    inner = jnp.mean(weighted * normed, axis=-1, keepdims=True)
    return scaled * (weighted - jnp.mean(weighted, axis=-1, keepdims=True) - normed * inner)


SQRT_HALF = 0.7071067811865476
INV_SQRT_2PI = 0.3989422804014327
ERF_P = 0.3275911
ERF_A = (0.254829592, -0.284496736, 1.421413741, -1.453152027, 1.061405429)
TILE = 96
CUT = 2 * HEAD


def dot(a, b):
    return lax.dot_general(a, b, (((1,), (0,)), ((), ())), preferred_element_type=F32)


def dot_nt(a, b):
    return lax.dot_general(a, b, (((1,), (1,)), ((), ())), preferred_element_type=F32)


def gelu_parts(v):
    size = jnp.abs(v) * SQRT_HALF
    t = 1.0 / (1.0 + ERF_P * size)
    bell = jnp.exp(-0.5 * v * v)
    poly = ERF_A[4]
    for a in ERF_A[3::-1]:
        poly = poly * t + a
    tail = 0.5 * poly * t * bell
    phi = jnp.where(v < 0.0, tail, 1.0 - tail)
    return v * phi, phi + v * bell * INV_SQRT_2PI


def low_lanes():
    return lax.broadcasted_iota(jnp.int32, (1, CUT), 1) < HEAD


def half_rows():
    lane = lax.broadcasted_iota(jnp.int32, (1, CUT), 1)
    low = jnp.where(lane < HEAD, 1.0, 0.0)
    return low.astype(BF16), (1.0 - low).astype(BF16)


def swap(a):
    return pltpu.roll(a, HEAD, 1)


def sel_matrix(key, b):
    lane = lax.broadcasted_iota(jnp.int32, (128, key.shape[1]), 0) * (NZ * NY) + b
    return jnp.where(lane == key, 1.0, 0.0).astype(BF16)


def sel_keys(width):
    col = lax.broadcasted_iota(jnp.int32, (1, width), 1)
    nr = width // (NZ * NY)
    q = jnp.where(col < CUT, col, col - 3 * CUT)
    v = jnp.where(col < 3 * CUT, col - 2 * CUT, col - 4 * CUT)
    is_q = (col < CUT) | ((col >= 4 * CUT) & (col < 4 * CUT + HEAD))
    is_v = ((col >= 2 * CUT) & (col < 3 * CUT)) | ((col >= 5 * CUT) & (col < 5 * CUT + HEAD))
    head = jnp.where(is_q, q, jnp.where(is_v, v + 3 * HEAD, -1))
    return (col % nr) * (NZ * NY) + col // nr, col, head


def run_hooks(hooks, i):
    for k, step in (hooks or {}).items():
        pl.when(i == k)(step)


class Layer:
    def __init__(self, **refs):
        self.__dict__.update(refs)
        self.tiles = self.x.shape[0]
        self.width = self.x.shape[2]
        self.rows = self.tiles * TILE
        self.seqs = self.qkv.shape[2]
        self.length = self.qkv.shape[3]
        self.per = self.length // TILE

    def weight(self, p, t, lo, size):
        c, x = t // NX, t % NX
        return self.w[p, c, x, :, :, :, lo:lo + size].reshape(self.width, size)

    def put_weight(self, p, t, lo, value):
        c, x = t // NX, t % NX
        size = value.shape[1]
        nr = self.width // (NZ * NY)
        self.w[p, c, x, :, :, :, lo:lo + size] = value.astype(BF16).reshape(NZ, NY, nr, size)

    def all_rows(self, ref, *at):
        a = ref[at] if at else ref[...]
        return a.reshape(self.rows, a.shape[-1])

    def seq_rows(self, ref, s, *at):
        a = ref[at + (pl.ds(self.per * s, self.per),)]
        return a.reshape(self.length, a.shape[-1])

    def transposed(self, ref, out):
        a = self.all_rows(ref)
        out[0:self.width, :] = a.T
        out[self.width:, :] = jnp.ones((out.shape[0] - self.width, self.rows), BF16)

    def vectors(self):
        keys = sel_keys(self.width)
        self.vec[...] = jnp.zeros(self.vec.shape, F32)

        @pl.loop(0, NZ * NY)
        def _(b):
            z, y = b // NY, b % NY
            own = self.v[:, :, z, y].reshape(NC * NX * 8, 128).astype(BF16)
            for i, key in enumerate(keys):
                part = dot(own, sel_matrix(key, b)).reshape(NC * NX, 8, self.width)
                self.vec[i] = self.vec[i] + part

    def row(self, i):
        return self.vec[0, 0, i:i + 1, :]

    def projected(self, t, n):
        bias = self.vec[2, t, 7:8, 256 * n:256 * n + 256]
        return dot(self.all_rows(self.x), self.weight(0, t, 256 * n, 256)) + bias

    def put_head(self, i, p, value):
        self.qkv[i, p] = value.astype(BF16).reshape(self.seqs, self.length, CUT)

    def projections_first(self):
        @pl.loop(0, NC * NX)
        def _(t):
            a = self.projected(t, 0)
            self.put_head(0, t, a[:, :CUT])
            self.put_head(1, t, a[:, CUT:])
            bias = self.vec[2, t, 7:8, 2 * CUT:3 * CUT]
            self.put_head(2, t, dot(self.all_rows(self.x), self.weight(0, t, 2 * CUT, CUT)) + bias)

    def projections_third(self):
        low = low_lanes()

        @pl.loop(0, NC)
        def _(u):
            a, b = self.projected(NX * u, 2), self.projected(NX * u + 1, 2)
            self.put_head(0, NC * NX + u, jnp.where(low, a[:, :CUT], swap(b[:, :CUT])))
            self.put_head(1, NC * NX + u, jnp.where(low, swap(a[:, :CUT]), b[:, :CUT]))
            self.put_head(2, NC * NX + u, jnp.where(low, a[:, CUT:], swap(b[:, CUT:])))

    def heads(self, p, s):
        halves = half_rows()
        q, k, v = (self.qkv[i, p, s] for i in range(3))
        valid = lax.broadcasted_iota(jnp.int32, (1, self.length), 1) < self.lens[self.first + s]
        context = []
        for j in range(2):
            scores = jnp.where(valid, dot_nt(q * halves[j], k) * SCALE, MASKED)
            powers = jnp.exp(scores - jnp.max(scores, axis=1, keepdims=True))
            probs = (powers * (1.0 / jnp.sum(powers, axis=1, keepdims=True))).astype(BF16)
            self.probs[p, s, j] = probs
            context.append(dot(probs, v))
        return jnp.where(low_lanes(), *context)

    def put_context(self, t, s, lo, value):
        value = value.astype(BF16).reshape(self.per, TILE, CUT)
        self.ctx[t, pl.ds(self.per * s, self.per), :, lo:lo + CUT] = value

    def attention_first(self, hooks=None):
        @pl.loop(0, NC * NX * self.seqs)
        def _(i):
            run_hooks(hooks, i)
            t, s = i // self.seqs, i % self.seqs
            self.put_context(t, s, 0, self.heads(t, s))

    def attention_third(self, hooks=None):
        low = low_lanes()

        @pl.loop(0, NC * self.seqs)
        def _(i):
            run_hooks(hooks, i)
            u, s = i // self.seqs, i % self.seqs
            context = self.heads(NC * NX + u, s)
            self.put_context(NX * u, s, CUT, jnp.where(low, 0.0, swap(context)))
            self.put_context(NX * u + 1, s, CUT, jnp.where(low, 0.0, context))

    def mixer_weight(self, t):
        return jnp.concatenate([self.weight(0, t, 3 * CUT, CUT), self.weight(0, t, 5 * CUT, CUT)], axis=1)

    def put_rows(self, ref, s, value):
        ref[pl.ds(self.per * s, self.per)] = value.reshape(self.per, TILE, value.shape[1])

    def mix(self):
        @pl.loop(0, self.seqs)
        def _(s):
            total = None
            for t in range(NC * NX):
                part = dot_nt(self.seq_rows(self.ctx, s, t), self.mixer_weight(t))
                total = part if total is None else total + part
            self.put_rows(self.tmp, s, total)

    def norm_first(self, hooks=None):
        @pl.loop(0, self.tiles)
        def _(i):
            run_hooks(hooks, i)
            total = self.x[i].astype(F32) + self.tmp[i] + self.row(0)
            _, normed, scaled = normalize(total, 1.0, 0.0)
            self.norm[i] = normed
            self.scaled[i] = scaled
            self.hidden[i] = (normed * self.row(1) + self.row(2)).astype(BF16)

    def expand(self, hooks, chunks):
        @pl.loop(0, NC * NX)
        def _(t):
            run_hooks(hooks, t)
            hidden = self.all_rows(self.hidden)
            for n in chunks:
                cols = slice(256 * n, 256 * n + 256)
                before = dot(hidden, self.weight(1, t, 256 * n, 256)) + self.vec[1, t, 6:7, cols]
                act, slope = gelu_parts(before)
                self.act[t, :, :, cols] = act.astype(BF16).reshape(self.tiles, TILE, 256)
                self.slope[t, :, :, cols] = slope.astype(BF16).reshape(self.tiles, TILE, 256)

    def times_back(self, p, ref, lo=0, size=None, more=False, hooks=None):
        size = self.width if size is None else size

        @pl.loop(0, self.seqs)
        def _(s):
            run_hooks(hooks, s)
            rows = pl.ds(self.per * s, self.per)
            total = self.tmp[rows].reshape(self.length, self.width) if more else None
            for t in range(NC * NX):
                left = ref[t, rows, :, lo:lo + size].reshape(self.length, size)
                part = dot_nt(left, self.weight(p, t, lo, size))
                total = part if total is None else total + part
            self.put_rows(self.tmp, s, total)

    def add_sum(self, i, value):
        self.sums[i] = self.sums[i] + jnp.sum(value.reshape(TILE // 8, 8, self.width), axis=0)

    def clear_sums(self):
        self.sums[...] = jnp.zeros(self.sums.shape, F32)

    def norm_second(self, hooks=None):
        @pl.loop(0, self.tiles)
        def _(i):
            run_hooks(hooks, i)
            hidden = self.norm[i] * self.row(1) + self.row(2)
            _, normed, scaled = normalize(hidden + self.tmp[i] + self.row(3), 1.0, 0.0)
            self.out[i] = (normed * self.row(4) + self.row(5)).astype(BF16)
            up = self.cot[i].astype(F32)
            self.add_sum(4, up * normed)
            self.add_sum(5, up)
            after = normalize_back(up, normed, scaled, self.row(4))
            self.add_sum(3, after)
            self.grad[i] = after
            self.low[i] = after.astype(BF16)

    def act_back(self, hooks=None):
        @pl.loop(0, NC * NX)
        def _(t):
            run_hooks(hooks, t)
            low = self.all_rows(self.low)
            for n in range(3):
                cols = slice(256 * n, 256 * n + 256)
                up = dot(low, self.weight(2, t, 256 * n, 256)).reshape(self.tiles, TILE, 256)
                self.slope[t, :, :, cols] = (up * self.slope[t, :, :, cols].astype(F32)).astype(BF16)

    def contract_grad(self, hooks=None):
        @pl.loop(0, NC * NX)
        def _(t):
            run_hooks(hooks, t)
            left = self.left[0:self.width, :]
            for n in range(3):
                right = self.all_rows(self.act, t, slice(None), slice(None), slice(256 * n, 256 * n + 256))
                self.put_weight(2, t, 256 * n, dot(left, right))

    def expand_grad(self, hooks=None):
        @pl.loop(0, NC * NX)
        def _(t):
            run_hooks(hooks, t)
            for n in range(3):
                cols = slice(256 * n, 256 * n + 256)
                grad = dot(self.left[...], self.all_rows(self.slope, t, slice(None), slice(None), cols))
                self.put_weight(1, t, 256 * n, grad[:self.width])
                self.unit_sums[0, t, :, cols] = grad[self.width:self.width + 8]

    def norm_first_back(self, hooks=None):
        @pl.loop(0, self.tiles)
        def _(i):
            run_hooks(hooks, i)
            grad = self.grad[i] + self.tmp[i]
            normed = self.norm[i]
            self.add_sum(1, grad * normed)
            self.add_sum(2, grad)
            after = normalize_back(grad, normed, self.scaled[i], self.row(1))
            self.add_sum(0, after)
            self.grad[i] = after
            self.low[i] = after.astype(BF16)

    def context_back(self):
        low = low_lanes()

        @pl.loop(0, NC)
        def _(u):
            third = []
            for d in range(NX):
                t = NX * u + d
                grad = dot(self.all_rows(self.low), self.mixer_weight(t))
                self.cgrad[t] = grad[:, :CUT].astype(BF16).reshape(self.seqs, self.length, CUT)
                third.append(grad[:, CUT:])
            pair = jnp.where(low, swap(third[0]), third[1])
            self.cgrad[NC * NX + u] = pair.astype(BF16).reshape(self.seqs, self.length, CUT)

    def heads_back(self, p, s):
        halves = half_rows()
        q, k, v = (self.qkv[i, p, s] for i in range(3))
        up = self.cgrad[p, s]
        up_t = up.T
        q_t = q.T
        dq, dk, dv = [], [], []
        for j in range(2):
            probs = self.probs[p, s, j]
            dv.append(dot(up_t[HEAD * j:HEAD * j + HEAD], probs))
            weight = dot_nt(up * halves[j], v)
            wide = probs.astype(F32)
            grad = wide * (weight - jnp.sum(wide * weight, axis=1, keepdims=True))
            grad = grad.astype(BF16)
            dq.append(dot(grad, k))
            dk.append(dot(q_t[HEAD * j:HEAD * j + HEAD], grad))
        dq = jnp.where(low_lanes(), *dq) * SCALE
        dk = jnp.concatenate(dk, axis=0).T * SCALE
        dv = jnp.concatenate(dv, axis=0).T
        return dq, dk, dv

    def put_stream(self, t, s, lo, value):
        value = value.astype(BF16).reshape(self.per, TILE, CUT)
        self.act[t, pl.ds(self.per * s, self.per), :, lo:lo + CUT] = value

    def attention_back_first(self, hooks=None):
        @pl.loop(0, NC * NX * self.seqs)
        def _(i):
            run_hooks(hooks, i)
            t, s = i // self.seqs, i % self.seqs
            grads = self.heads_back(t, s)
            for j in range(3):
                self.put_stream(t, s, CUT * j, grads[j])
            self.put_stream(t, s, 3 * CUT, jnp.zeros((self.length, CUT), F32))

    def attention_back_third(self, hooks=None):
        low = low_lanes()

        @pl.loop(0, NC * self.seqs)
        def _(i):
            run_hooks(hooks, i)
            u, s = i // self.seqs, i % self.seqs
            dq, dk, dv = self.heads_back(NC * NX + u, s)
            self.put_stream(NX * u, s, 4 * CUT, jnp.where(low, dq, swap(dk)))
            self.put_stream(NX * u + 1, s, 4 * CUT, jnp.where(low, swap(dq), dk))
            self.put_stream(NX * u, s, 5 * CUT, jnp.where(low, dv, 0.0))
            self.put_stream(NX * u + 1, s, 5 * CUT, jnp.where(low, swap(dv), 0.0))

    def input_back(self):
        half = self.width // NX

        @pl.loop(0, self.tiles)
        def _(i):
            total = (self.grad[i] + self.tmp[i]).astype(BF16)
            for x in range(NX):
                self.igrad[x, i] = total[:, half * x:half * x + half]

    def stream_grad(self, t, n):
        cols = slice(256 * n, 256 * n + 256)
        grad = dot(self.left[...], self.all_rows(self.act, t, slice(None), slice(None), cols))
        self.unit_sums[1, t, :, cols] = grad[self.width:self.width + 8]
        return grad[:self.width]

    def mixer_grad(self, t, h):
        cols = slice(CUT * h, CUT * h + CUT)
        return dot(self.left2[0:self.width, :], self.all_rows(self.ctx, t, slice(None), slice(None), cols))

    def attention_grad_first(self, hooks=None):
        @pl.loop(0, NC * NX)
        def _(t):
            run_hooks(hooks, t)
            self.put_weight(0, t, 0, self.stream_grad(t, 0))
            grad = self.stream_grad(t, 1)
            self.put_weight(0, t, 2 * CUT, grad[:, :CUT])
            self.put_weight(0, t, 3 * CUT, self.mixer_grad(t, 0))

    def attention_grad_third(self, hooks=None):
        @pl.loop(0, NC * NX)
        def _(t):
            run_hooks(hooks, t)
            grad = self.stream_grad(t, 2)
            self.put_weight(0, t, 4 * CUT, grad[:, :CUT])
            self.put_weight(0, t, 5 * CUT, grad[:, CUT:] + self.mixer_grad(t, 1))

    def vector_tiles(self):
        keys = sel_keys(self.width)
        rows = [jnp.sum(self.sums[i], axis=0, keepdims=True) for i in range(6)]
        rows.append(jnp.zeros((2, self.width), F32))
        parts = [jnp.concatenate(rows, axis=0)]
        for i in range(2):
            units = [self.unit_sums[i, t, 0:1, :] for t in range(NC * NX)]
            parts.append(jnp.concatenate(units + [jnp.zeros((4, self.width), F32)], axis=0))
        split = []
        for part in parts:
            high = part.astype(BF16)
            split.append(jnp.concatenate([high, (part - high.astype(F32)).astype(BF16)], axis=0))

        @pl.loop(0, NZ * NY)
        def _(b):
            z, y = b // NY, b % NY
            got = []
            for key, part in zip(keys, split):
                both = dot_nt(part, sel_matrix(key, b))
                got.append(both[:8] + both[8:])
            for t in range(NC * NX):
                self.vtiles[t // NX, t % NX, z, y] = jnp.concatenate(
                    [got[0][:6], got[1][t:t + 1], got[2][t:t + 1]], axis=0
                )


def layer_scratch(seqs, length, width):
    tiles = seqs * length // TILE
    blocks = NC * NX
    pairs = 3 * blocks // 2
    rows = seqs * length
    nr = width // (NZ * NY)
    return [
        pltpu.VMEM((3, NC, NX, NZ, NY, nr, width), BF16),
        pltpu.VMEM((tiles, TILE, width), BF16),
        pltpu.VMEM((tiles, TILE, width), BF16),
        pltpu.VMEM((3, pairs, seqs, length, CUT), BF16),
        pltpu.VMEM((pairs, seqs, 2, length, length), BF16),
        pltpu.VMEM((blocks, tiles, TILE, 2 * CUT), BF16),
        pltpu.VMEM((tiles, TILE, width), F32),
        pltpu.VMEM((tiles, TILE, width), F32),
        pltpu.VMEM((tiles, TILE, 1), F32),
        pltpu.VMEM((tiles, TILE, width), BF16),
        pltpu.VMEM((blocks, tiles, TILE, width), BF16),
        pltpu.VMEM((blocks, tiles, TILE, width), BF16),
        pltpu.VMEM((tiles, TILE, width), F32),
        pltpu.VMEM((tiles, TILE, width), BF16),
        pltpu.VMEM((pairs, seqs, length, CUT), BF16),
        pltpu.VMEM((width + 16, rows), BF16),
        pltpu.VMEM((width + 16, rows), BF16),
        pltpu.VMEM((3, blocks, 8, width), F32),
        pltpu.VMEM((6, 8, width), F32),
        pltpu.VMEM((2, blocks, 8, width), F32),
    ]


class Gather:
    def __init__(self, me, w, v, sems, vsems):
        self.me, self.w, self.v, self.sems, self.vsems = me, w, v, sems, vsems

    def hop(self, k, i):
        p, lo, size, route = GATHER_PARTS[k]
        me = self.me
        at = {axis: slice(None) if axis in route[:i] else me.own(axis) for axis in "xyz"}
        slot = self.w.at[p, me.c, at["x"], at["z"], at["y"], :, pl.ds(lo, size)]
        first = {"z": 0, "x": NZ - 1, "y": NZ}[route[i]]
        return [
            remote(slot, slot, self.sems, 5 * k + first + j, peer) for j, peer in enumerate(me.along(route[i]))
        ]

    def start(self, k, i):
        if i > 0:
            for copy in self.hop(k, i - 1):
                copy.wait_recv()
        for copy in self.hop(k, i):
            copy.start()

    def core(self, group):
        p, lo, size, parts = GATHER_GROUPS[group]
        slot = self.w.at[p, self.me.c, :, :, :, :, pl.ds(lo, size)]
        return remote(slot, slot, self.sems, 5 * len(GATHER_PARTS) + group, self.me.core())

    def start_core(self, group):
        for k in GATHER_GROUPS[group][3]:
            for copy in self.hop(k, 2):
                copy.wait_recv()
        self.core(group).start()

    def arrived(self, group):
        self.core(group).wait_recv()

    def left(self, group):
        for k in GATHER_GROUPS[group][3]:
            for i in range(3):
                for copy in self.hop(k, i):
                    copy.wait_send()
        self.core(group).wait_send()

    def small(self):
        me, v = self.me, self.v
        def same(slot, index, peer):
            return remote(slot, slot, self.vsems, index, peer)
        return [
            [same(v.at[me.c, me.x, me.z, me.y], s, peer) for s, peer in enumerate(me.along("z"))],
            [same(v.at[me.c, me.x, :, me.y], 3, me.xp())],
            [same(v.at[me.c, :, :, me.y], 4, me.yp())],
            [same(v.at[me.c], 5, me.core())],
        ]

    def small_step(self, i):
        steps = self.small()
        if i > 0:
            for copy in steps[i - 1]:
                copy.wait_recv()
        if i < len(steps):
            for copy in steps[i]:
                copy.start()

    def small_left(self):
        for copy in sum(self.small(), []):
            copy.wait_send()


GATHER_PARTS = (
    (0, 0, 256, "zxy"),
    (0, 256, 256, "zyx"),
    (0, 512, 128, "zxy"),
    (0, 640, 128, "yxz"),
    (1, 0, 256, "zxy"),
    (1, 256, 384, "zyx"),
    (1, 640, 128, "xzy"),
    (2, 0, 256, "zyx"),
    (2, 384, 256, "zxy"),
    (2, 640, 128, "yxz"),
    (2, 256, 128, "xyz"),
)
GATHER_GROUPS = (
    (0, 0, 512, (0, 1)), (0, 512, 256, (2, 3)), (1, 0, 256, (4,)), (1, 256, 512, (5, 6)),
    (2, 0, 384, (7, 10)), (2, 384, 384, (8, 9)),
)
SCATTER_PARTS = (
    (2, 0, 512, "yxz"),
    (2, 512, 128, "zxy"),
    (2, 640, 128, "xzy"),
    (1, 0, 384, "yxz"),
    (1, 384, 128, "xzy"),
    (1, 512, 256, "zxy"),
    (0, 0, 384, "yxz"),
    (0, 384, 128, "xyz"),
    (0, 512, 128, "xyz"),
    (0, 640, 128, "yxz"),
)
SCATTER_GROUPS = ((2, 0, 768, (0, 1, 2)), (1, 0, 768, (3, 4, 5)), (0, 0, 512, (6, 7)), (0, 512, 256, (8, 9)))
AXIS = {"x": NX, "y": NY, "z": NZ}


class Scatter:
    def __init__(self, me, g, v, bufs, sems, vsems, osems, out, outs, ig, igs):
        self.me, self.g, self.v = me, g, v
        self.rc, self.rb, self.vc, self.vy, self.vx, self.vz = bufs
        self.sems, self.vsems, self.osems = sems, vsems, osems
        self.out, self.outs, self.ig, self.igs = out, outs, ig, igs

    def core(self, group):
        p, lo, size, _ = SCATTER_GROUPS[group]
        me, cols = self.me, pl.ds(lo, size)
        return remote(
            self.g.at[p, 1 - me.c, :, :, :, :, cols], self.rc.at[p, :, :, :, :, cols],
            self.sems, 9 * len(SCATTER_PARTS) + group, me.core(),
        )

    def start_core(self, group):
        self.core(group).start()

    def add_core(self, group):
        p, lo, size, _ = SCATTER_GROUPS[group]
        c, cols = self.me.c, slice(lo, lo + size)
        self.core(group).wait_recv()

        @pl.loop(0, NZ)
        def _(j):
            for i in range(NX):
                for k in range(NY):
                    self.g[p, c, i, j, k, :, cols] = self.g[p, c, i, j, k, :, cols] + self.rc[p, i, j, k, :, cols]

    def plan(self, k, i):
        p, lo, size, route = SCATTER_PARTS[k]
        me = self.me
        axis = route[i]
        done = {a: me.own(a) for a in route[:i]}
        every = slice(None)
        moves = []
        sizes = [AXIS[a] for a in route]
        at = sum((sizes[n] - 1) * sizes[n + 1] * (sizes[2] if n == 0 else 1) for n in range(i))
        for peer, other in zip(me.along(axis), me.others(axis)):
            spare = [a for a in "xyz" if a != axis and a not in done]
            inner = "z" if "z" in spare else (spare[-1] if spare else None)
            outer = [a for a in spare if a != inner]
            for o in range(2 if outer else 1):
                send = dict(done)
                if outer:
                    send[outer[0]] = o
                if inner:
                    send[inner] = every
                keep = dict(send)
                send[axis], keep[axis] = other, me.own(axis)
                count = None if inner is None else (NZ if inner == "z" else 2)
                moves.append((send, keep, at, count, peer))
                at += 1 if count is None else count
        return p, lo, size, moves

    def hop(self, k, i):
        p, lo, size, moves = self.plan(k, i)
        me, cols = self.me, pl.ds(lo, size)
        base = 9 * k + sum(len(self.plan(k, n)[3]) for n in range(i))
        copies = []
        for j, (send, _, at, count, peer) in enumerate(moves):
            src = self.g.at[p, me.c, send["x"], send["z"], send["y"], :, cols]
            dst = self.rb.at[p, at, :, cols] if count is None else self.rb.at[p, pl.ds(at, count), :, cols]
            copies.append(remote(src, dst, self.sems, base + j, peer))
        return copies

    def start(self, k, i):
        if i > 0:
            self.add(k, i - 1)
        for copy in self.hop(k, i):
            copy.start()

    def add(self, k, i):
        p, lo, size, moves = self.plan(k, i)
        c, cols = self.me.c, slice(lo, lo + size)
        for copy in self.hop(k, i):
            copy.wait_recv()
        terms = {}
        for _, keep, at, count, _ in moves:
            inner = [a for a in "xyz" if isinstance(keep[a], slice)]
            for n in range(1 if count is None else count):
                spot = dict(keep)
                if inner:
                    spot[inner[0]] = n
                name = tuple(spot[a] if isinstance(spot[a], int) else a for a in "xyz")
                terms.setdefault(name, (spot, []))[1].append(at + n)
        for spot, places in terms.values():
            ref = self.g.at[p, c, spot["x"], spot["z"], spot["y"], :, cols]
            if len(places) == 1:
                ref[...] = ref[...] + self.rb[p, places[0], :, cols]
            else:
                total = ref[...].astype(F32)
                for n in places:
                    total = total + self.rb[p, n, :, cols].astype(F32)
                ref[...] = total.astype(BF16)

    def total(self, k):
        p, lo, size, moves = self.plan(k, 2)
        me, cols = self.me, slice(lo, lo + size)
        for copy in self.hop(k, 2):
            copy.wait_recv()
        total = self.g[p, me.c, me.x, me.z, me.y, :, cols].astype(F32)
        for _, _, at, _, _ in moves:
            total = total + self.rb[p, at, :, cols].astype(F32)
        return total

    def left(self, group):
        self.core(group).wait_send()
        for k in SCATTER_GROUPS[group][3]:
            for i in range(3):
                for copy in self.hop(k, i):
                    copy.wait_send()

    def small(self, i):
        me, v, sems = self.me, self.v, self.vsems
        if i == 0:
            return [remote(v.at[1 - me.c], self.vc, sems, 0, me.core())]
        if i == 1:
            return [remote(v.at[me.c, :, :, 1 - me.y], self.vy, sems, 1, me.yp())]
        if i == 2:
            return [remote(v.at[me.c, 1 - me.x, :, me.y], self.vx, sems, 2, me.xp())]
        return [
            remote(v.at[me.c, me.x, (me.z + s) % NZ, me.y], self.vz.at[s - 1], sems, 2 + s, me.zp(s))
            for s in range(1, NZ)
        ]

    def small_step(self, i):
        me, v = self.me, self.v
        if i > 0:
            for copy in self.small(i - 1):
                copy.wait_recv()
        if i == 1:
            v[me.c] = v[me.c] + self.vc[...]
        elif i == 2:
            v[me.c, :, :, me.y] = v[me.c, :, :, me.y] + self.vy[...]
        elif i == 3:
            v[me.c, me.x, :, me.y] = v[me.c, me.x, :, me.y] + self.vx[...]
        elif i == 4:
            total = v[me.c, me.x, me.z, me.y]
            for s in range(1, NZ):
                total = total + self.vz[s - 1]
            return total
        for copy in self.small(i):
            copy.start()

    def small_left(self):
        for i in range(4):
            for copy in self.small(i):
                copy.wait_send()

    def outputs(self):
        me = self.me
        t = me.x * NC + me.c
        return [remote(self.out, self.outs.at[t], self.osems, i, peer) for i, peer in enumerate((me.xp(), me.core()))]

    def output_local(self, sem):
        return pltpu.make_async_copy(self.out, self.outs.at[self.me.x * NC + self.me.c], sem)

    def output_forward(self):
        me = self.me
        t = (1 - me.x) * NC + me.c
        return remote(self.outs.at[t], self.outs.at[t], self.osems, 4, me.core())

    def grads(self):
        me = self.me
        t = me.x * NC + me.c
        return [
            remote(self.ig.at[1 - me.x], self.igs.at[t], self.osems, 2, me.xp()),
            remote(self.ig.at[me.x], self.igs.at[t], self.osems, 3, me.core()),
        ]

    def grad_local(self, sem):
        return pltpu.make_async_copy(self.ig.at[self.me.x], self.igs.at[self.me.x * NC + self.me.c], sem)

    def grad_forward(self):
        me = self.me
        t = (1 - me.x) * NC + me.c
        return remote(self.igs.at[t], self.igs.at[t], self.osems, 5, me.core())


def step_kernel(
    x_in, cot_in, lens, tw, mw, ew, cw, vec_in,
    outs, igs, triple_out, mixer_out, expand_out, contract_out, small_out,
    w, v, vtiles, out, ig,
    x, cot, qkv, probs, ctx, tmp, norm, scaled, hidden, act, slope, grad, low, cgrad, left, left2, vec, sums,
    unit_sums,
    rc, rb, vc, vy, vx, vz,
    gsems, gvsems, sems, vsems, osems, lsems,
):
    me = Place()
    t = lax.axis_index("tensor")
    seqs = qkv.shape[2]
    own = [w.at[p, me.c, me.x, me.z, me.y] for p in range(3)]
    load_v = pltpu.make_async_copy(vec_in, v.at[me.c, me.x, me.z, me.y], lsems.at[3])
    load_e = pltpu.make_async_copy(ew, own[1], lsems.at[2])
    load_c = pltpu.make_async_copy(cw, own[2], lsems.at[6])
    load_x = pltpu.make_async_copy(x_in.at[t], x, lsems.at[0])
    load_cot = pltpu.make_async_copy(cot_in.at[t], cot, lsems.at[1])
    me.signal()
    for copy in (load_v, load_e, load_c, load_x, load_cot):
        copy.start()
    pack_attention(tw, mw, own[0])
    gather = Gather(me, w, v, gsems, gvsems)
    layer = Layer(
        w=w, x=x, cot=cot, qkv=qkv, probs=probs, ctx=ctx, tmp=tmp, norm=norm, scaled=scaled, hidden=hidden, act=act,
        slope=slope, grad=grad, low=low, cgrad=cgrad, left=left, left2=left2, vec=vec, sums=sums, unit_sums=unit_sums,
        v=v, out=out, igrad=ig, vtiles=vtiles, lens=lens, first=t * seqs,
    )
    scatter = Scatter(me, w, vtiles, (rc, rb, vc, vy, vx, vz), sems, vsems, osems, out, outs, ig, igs)
    me.meet()
    load_e.wait()
    load_c.wait()
    load_v.wait()
    gather.small_step(0)
    gather.start(10, 0)
    gather.start(2, 0)
    gather.start(1, 0)
    gather.start(9, 0)
    gather.small_step(1)
    gather.start(2, 1)
    gather.start(0, 0)
    gather.small_step(2)
    gather.start(5, 0)
    gather.start(4, 0)
    gather.start(3, 0)
    gather.start(7, 0)
    gather.start(3, 1)
    gather.start(2, 2)
    gather.start(1, 1)
    gather.start(8, 0)
    layer.clear_sums()
    gather.start(10, 1)
    gather.start(3, 2)
    gather.start(9, 1)
    gather.small_step(3)
    gather.small_step(4)
    gather.start(6, 0)
    gather.start(0, 1)
    gather.start(1, 2)
    gather.start(0, 2)
    gather.start(5, 1)
    gather.start(6, 1)
    layer.vectors()
    gather.start(4, 1)
    gather.start_core(0)
    gather.start(8, 1)
    load_x.wait()
    load_cot.wait()
    gather.arrived(0)
    layer.projections_first()
    gather.start(7, 1)
    def at_3_1():
        gather.start(10, 2)

    def at_3_2():
        gather.start(5, 2)

    def at_3_4():
        gather.start(4, 2)

    def at_3_6():
        gather.start(7, 2)
        gather.start_core(1)

    layer.attention_first(hooks={1: at_3_1, 2: at_3_2, 4: at_3_4, 6: at_3_6})
    gather.arrived(1)
    layer.projections_third()
    def at_5_2():
        gather.start(6, 2)

    layer.attention_third(hooks={2: at_5_2})
    layer.mix()
    gather.start(8, 2)
    def at_7_1():
        gather.start_core(2)

    def at_7_2():
        gather.start(9, 2)
        gather.start_core(3)

    def at_7_3():
        gather.arrived(2)

    layer.norm_first(hooks={1: at_7_1, 2: at_7_2, 3: at_7_3})
    layer.expand({}, (0,))
    gather.arrived(3)
    def at_9_2():
        gather.start_core(4)

    def at_9_3():
        gather.start_core(5)

    layer.expand({2: at_9_2, 3: at_9_3}, (1, 2))
    gather.arrived(4)
    layer.times_back(2, act, 0, 384, hooks={})
    gather.arrived(5)
    layer.times_back(2, act, 384, 384, True, hooks={})
    layer.norm_second(hooks={})
    layer.transposed(low, left)
    def at_14_1():
        for copy in scatter.outputs():
            copy.start()
        scatter.output_local(lsems.at[4]).start()

    layer.act_back(hooks={1: at_14_1})
    gather.left(4)
    gather.left(5)
    layer.contract_grad(hooks={})
    scatter.start_core(0)
    layer.times_back(1, slope, hooks={})
    layer.transposed(hidden, left)
    scatter.add_core(0)
    scatter.start(2, 0)
    scatter.start(1, 0)
    gather.left(2)
    gather.left(3)
    scatter.start(0, 0)
    layer.expand_grad(hooks={})
    scatter.start_core(1)
    layer.norm_first_back(hooks={})
    layer.transposed(low, left2)
    layer.context_back()
    def at_24_1():
        scatter.add_core(1)
        scatter.start(3, 0)
        scatter.start(5, 0)

    def at_24_2():
        scatter.start(4, 0)

    def at_24_3():
        scatter.start(1, 1)

    layer.attention_back_first(hooks={1: at_24_1, 2: at_24_2, 3: at_24_3})
    layer.times_back(0, act, 0, 3 * CUT, hooks={})
    scatter.start(0, 1)
    scatter.start(2, 1)
    layer.transposed(x, left)
    gather.left(0)
    layer.attention_grad_first(hooks={})
    scatter.start_core(2)
    scatter.add_core(2)
    scatter.start(7, 0)
    scatter.start(6, 0)
    def at_29_3():
        scatter.start(5, 1)
        scatter.start(0, 2)

    layer.attention_back_third(hooks={3: at_29_3})
    def at_30_1():
        scatter.start(7, 1)
        scatter.start(3, 1)
        scatter.start(4, 1)

    layer.times_back(0, act, 4 * CUT, 2 * CUT, True, hooks={1: at_30_1})
    layer.input_back()
    gather.left(1)
    layer.attention_grad_third(hooks={})
    scatter.start_core(3)
    layer.vector_tiles()
    scatter.small_step(0)
    scatter.add_core(3)
    scatter.start(8, 0)
    scatter.start(3, 2)
    scatter.start(6, 1)
    scatter.small_step(1)
    scatter.start(9, 0)
    scatter.start(2, 2)
    scatter.start(8, 1)
    scatter.small_step(2)
    scatter.outputs()[0].wait_recv()
    scatter.output_forward().start()
    scatter.start(7, 2)
    scatter.start(9, 1)
    scatter_out(scatter, 0, contract_out)
    scatter.start(4, 2)
    scatter.start(6, 2)
    for copy in scatter.grads():
        copy.start()
    scatter.grad_local(lsems.at[5]).start()
    scatter_out(scatter, 2, contract_out)
    scatter.start(5, 2)
    scatter.start(8, 2)
    scatter_out(scatter, 7, tmp.at[0])
    scatter_out(scatter, 3, expand_out)
    scatter.start(9, 2)
    scatter.start(1, 2)
    scatter_out(scatter, 1, contract_out)
    scatter_out(scatter, 6, tmp.at[0])
    scatter.small_step(3)
    scatter.grads()[0].wait_recv()
    scatter.grad_forward().start()
    scatter_out(scatter, 5, expand_out)
    scatter_out(scatter, 9, tmp.at[0])
    scatter_out(scatter, 4, expand_out)
    scatter_out(scatter, 8, tmp.at[0])
    small_out[...] = scatter.small_step(4)
    unpack_attention(tmp[0], triple_out, mixer_out)
    scatter.outputs()[1].wait_recv()
    scatter.grads()[1].wait_recv()
    for copy in (scatter.output_forward(), scatter.grad_forward()):
        copy.wait()
    for copy in scatter.outputs() + scatter.grads():
        copy.wait_send()
    scatter.output_local(lsems.at[4]).wait()
    scatter.grad_local(lsems.at[5]).wait()
    gather.small_left()
    scatter.small_left()
    for group in range(4):
        scatter.left(group)


def scatter_out(scatter, k, ref):
    _, lo, size, _ = SCATTER_PARTS[k]
    ref[:, lo:lo + size] = scatter.total(k)


def pack_attention(tw, mw, slot):
    mixer = mw[...].T
    for i in range(3):
        slot[:, CUT * i:CUT * i + CUT] = tw[i, :, 0:CUT]
    slot[:, 3 * CUT:4 * CUT] = mixer[:, 0:CUT]
    slot[:, 4 * CUT:5 * CUT] = jnp.concatenate([tw[0, :, CUT:], tw[1, :, CUT:]], axis=1)
    slot[:, 5 * CUT:6 * CUT] = jnp.concatenate([tw[2, :, CUT:], mixer[:, CUT:]], axis=1)


def unpack_attention(total, triple_out, mixer_out):
    for i in range(3):
        triple_out[i, :, 0:CUT] = total[:, CUT * i:CUT * i + CUT]
        triple_out[i, :, CUT:] = total[:, 4 * CUT + HEAD * i:4 * CUT + HEAD * i + HEAD]
    mixer_out[0:CUT] = total[:, 3 * CUT:4 * CUT].T
    mixer_out[CUT:] = total[:, 5 * CUT + HEAD:].T


def step_call(x, cot, lengths, tw, mw, ew, cw, vec, seqs):
    pairs, length, width = x.shape
    tiles = seqs * length // TILE
    blocks = NX * NC
    nr, feat = width // (NZ * NY), width // blocks
    shape = (blocks, tiles, TILE, width)
    vmem = pl.BlockSpec(memory_space=pltpu.VMEM)
    hbm = pl.BlockSpec(memory_space=pl.ANY)
    layer = layer_scratch(seqs, length, width)
    small = (8, 128)
    return pl.pallas_call(
        step_kernel,
        out_shape=(
            jax.ShapeDtypeStruct(shape, BF16),
            jax.ShapeDtypeStruct((blocks, tiles, TILE, width // NX), BF16),
            jax.ShapeDtypeStruct((3, nr, feat), F32),
            jax.ShapeDtypeStruct((feat, nr), F32),
            jax.ShapeDtypeStruct((nr, width), F32),
            jax.ShapeDtypeStruct((nr, width), F32),
            jax.ShapeDtypeStruct(small, F32),
        ),
        in_specs=[hbm, hbm, pl.BlockSpec(memory_space=pltpu.SMEM), vmem, vmem, hbm, hbm, hbm],
        out_specs=(hbm, hbm, vmem, vmem, vmem, vmem, vmem),
        scratch_shapes=[
            layer[0],
            pltpu.VMEM((NC, NX, NZ, NY) + small, F32),
            pltpu.VMEM((NC, NX, NZ, NY) + small, F32),
            pltpu.VMEM((tiles, TILE, width), BF16),
            pltpu.VMEM((NX, tiles, TILE, width // NX), BF16),
        ] + layer[1:] + [
            pltpu.VMEM((3, NX, NZ, NY, nr, width), BF16),
            pltpu.VMEM((3, 15, nr, width), BF16),
            pltpu.VMEM((NX, NZ, NY) + small, F32),
            pltpu.VMEM((NX, NZ) + small, F32),
            pltpu.VMEM((NZ,) + small, F32),
            pltpu.VMEM((NZ - 1,) + small, F32),
            pltpu.SemaphoreType.DMA((2, 5 * len(GATHER_PARTS) + len(GATHER_GROUPS))),
            pltpu.SemaphoreType.DMA((2, 6)),
            pltpu.SemaphoreType.DMA((2, 9 * len(SCATTER_PARTS) + len(SCATTER_GROUPS))),
            pltpu.SemaphoreType.DMA((2, 6)),
            pltpu.SemaphoreType.DMA((2, 6)),
            pltpu.SemaphoreType.DMA((7,)),
        ],
        compiler_params=pltpu.CompilerParams(
            collective_id=0, has_side_effects=True, vmem_limit_bytes=67043328
        ),
    )(x.reshape(shape), cot.reshape(shape), lengths, tw, mw, ew, cw, vec)


def layer_step(x_seq, lengths, cot, w, d_vec, e_bias, p_bias):
    seqs, length, width = x_seq.shape
    rows = seqs * length
    blocks = w.shape[1]
    feat = width // blocks
    heads = feat // HEAD
    mixer_shift, gain_one, shift_one, contract_shift, gain_two, shift_two = d_vec
    x = x_seq.reshape(rows, width)
    att = w[0]
    cut = 2 * HEAD
    def columns(i):
        return jnp.concatenate(
            [att[:, :, i * cut:(i + 1) * cut], att[:, :, 4 * cut + i * HEAD:4 * cut + (i + 1) * HEAD]], axis=2
        )
    wq, wk, wv, wm = (columns(i) for i in range(4))
    def project(weight, bias):
        out = jnp.einsum("rd,tde->rte", x, weight, preferred_element_type=F32)
        if bias is not None:
            out = out + bias
        return out.astype(BF16).reshape(seqs, length, blocks * heads, HEAD)
    queries = project(wq, p_bias[0])
    keys = project(wk, None)
    values = project(wv, p_bias[1])
    valid = lax.broadcasted_iota(jnp.int32, (seqs, 1, 1, length), 3) < lengths[:, None, None, None]
    raw = jnp.einsum("sqhd,skhd->shqk", queries, keys, preferred_element_type=F32) * SCALE
    raw = jnp.where(valid, raw, MASKED)
    peak = jnp.max(raw, axis=-1, keepdims=True)
    powers = jnp.exp(raw - peak)
    probs = powers / jnp.sum(powers, axis=-1, keepdims=True)
    attention = probs.astype(BF16)
    context = jnp.einsum("shqk,skhd->sqhd", attention, values, preferred_element_type=F32)
    context = context.astype(BF16).reshape(rows, blocks, feat)
    mixed = jnp.einsum("rtc,tdc->rd", context, wm, preferred_element_type=F32)
    hidden, normed_one, scaled_one = normalize(x.astype(F32) + mixed + mixer_shift, gain_one, shift_one)
    hidden_low = hidden.astype(BF16)
    before = jnp.einsum("rd,tdf->rtf", hidden_low, w[1], preferred_element_type=F32) + e_bias
    activated = jax.nn.gelu(before, approximate=False).astype(BF16)
    branch = jnp.einsum("rtf,tdf->rd", activated, w[2], preferred_element_type=F32)
    result, normed_two, scaled_two = normalize(hidden + branch + contract_shift, gain_two, shift_two)
    outputs = result.astype(BF16)
    up = cot.reshape(rows, width).astype(F32)
    gain_two_grad = jnp.sum(up * normed_two, axis=0)
    shift_two_grad = jnp.sum(up, axis=0)
    after_two = normalize_back(up, normed_two, scaled_two, gain_two)
    contract_shift_grad = jnp.sum(after_two, axis=0)
    two_low = after_two.astype(BF16)
    contract_grad = jnp.einsum("rd,rtf->tdf", two_low, activated, preferred_element_type=F32)
    act_grad = jnp.einsum("rd,tdf->rtf", two_low, w[2], preferred_element_type=F32)
    _, gelu_back = jax.vjp(partial(jax.nn.gelu, approximate=False), before)
    before_grad = gelu_back(act_grad)[0].astype(BF16)
    expand_grad = jnp.einsum("rd,rtf->tdf", hidden_low, before_grad, preferred_element_type=F32)
    e_bias_grad = jnp.sum(before_grad, axis=0, dtype=F32)
    hidden_part = jnp.einsum("rtf,tdf->rd", before_grad, w[1], preferred_element_type=F32)
    hidden_grad = after_two + hidden_part
    after_one = normalize_back(hidden_grad, normed_one, scaled_one, gain_one)
    gain_one_grad = jnp.sum(hidden_grad * normed_one, axis=0)
    shift_one_grad = jnp.sum(hidden_grad, axis=0)
    mixer_shift_grad = jnp.sum(after_one, axis=0)
    one_low = after_one.astype(BF16)
    mixer_grad = jnp.einsum("rd,rtc->tdc", one_low, context, preferred_element_type=F32)
    context_grad = jnp.einsum("rd,tdc->rtc", one_low, wm, preferred_element_type=F32).astype(BF16)
    context_grad = context_grad.reshape(seqs, length, blocks * heads, HEAD)
    value_grad = jnp.einsum("shqk,sqhd->skhd", attention, context_grad, preferred_element_type=F32)
    weight_grad = jnp.einsum("sqhd,skhd->shqk", context_grad, values, preferred_element_type=F32)
    score_grad = probs * (weight_grad - jnp.sum(probs * weight_grad, axis=-1, keepdims=True))
    score_grad = score_grad.astype(BF16)
    query_grad = jnp.einsum("shqk,skhd->sqhd", score_grad, keys, preferred_element_type=F32) * SCALE
    key_grad = jnp.einsum("shqk,sqhd->skhd", score_grad, queries, preferred_element_type=F32) * SCALE
    streams = [g.astype(BF16).reshape(rows, blocks, feat) for g in (query_grad, key_grad, value_grad)]
    p_grad = [jnp.sum(streams[i], axis=0, dtype=F32) for i in (0, 2)]
    tgrads = [jnp.einsum("rd,rte->tde", x, s, preferred_element_type=F32) for s in streams] + [mixer_grad]
    att_grad = jnp.concatenate([g[:, :, :cut] for g in tgrads] + [g[:, :, cut:] for g in tgrads], axis=2)
    part = sum(
        jnp.einsum("rte,tde->rd", s, wt, preferred_element_type=F32) for s, wt in zip(streams, (wq, wk, wv))
    )
    input_grad = (after_one + part).astype(BF16)
    grads = jnp.stack([att_grad, expand_grad, contract_grad]).astype(BF16)
    vecs = jnp.stack(
        [mixer_shift_grad, gain_one_grad, shift_one_grad, contract_shift_grad, gain_two_grad, shift_two_grad]
    )
    return outputs, input_grad, grads, vecs, e_bias_grad, jnp.stack(p_grad)


def make_on_device(sizes):
    fast = sizes == {"batch": NZ * NY, "tensor": NX * NC}

    def on_device(
        inputs, lengths, triple_weight, pair_bias, mixer_weight, mixer_bias, first_gain, first_shift,
        expand_weight, expand_bias, contract_weight, contract_bias, second_gain, second_shift, cotangent,
    ):
        pairs, length, width = inputs.shape
        n_tensor, n_batch = sizes["tensor"], sizes["batch"]
        nr = width // n_batch
        own_pairs = pairs // n_tensor
        t = lax.axis_index("tensor")
        feat = width // n_tensor
        if fast:
            def lay(v, lo=0):
                return jnp.pad(v.reshape(-1).astype(F32), (lo, 128 - lo - v.size))
            small = [mixer_bias, first_gain, first_shift, contract_bias, second_gain, second_shift, expand_bias]
            half = pair_bias.shape[1]
            small = [lay(v) for v in small] + [lay(pair_bias[0]) + lay(pair_bias[1], half)]
            place = lax.broadcasted_iota(jnp.int32, (8, 128), 0)
            vec = jnp.zeros((8, 128), F32)
            for i, v in enumerate(small):
                vec = jnp.where(place == i, v[None, :], vec)
            outs, ig, triple_grad, mixer_grad, expand_grad, contract_grad, vred = step_call(
                inputs, cotangent, lengths, triple_weight, mixer_weight, expand_weight, contract_weight.T,
                vec, own_pairs,
            )
            ig = lax.dynamic_slice_in_dim(ig, t % NC * feat, feat, 3)
            outs = outs.reshape(pairs, length, width)
            ig = ig.reshape(pairs, length, feat).astype(F32)
            contract_grad = contract_grad.T
        else:
            cut = 2 * HEAD
            four = [triple_weight[0], triple_weight[1], triple_weight[2], mixer_weight.T]
            att = jnp.concatenate([m[:, :cut] for m in four] + [m[:, cut:] for m in four], axis=1)
            pack = jnp.stack([att, expand_weight, contract_weight.T])
            def row(v):
                return jnp.pad(v.reshape(1, -1), ((0, 0), (0, 128 - v.size)))
            vec = jnp.concatenate(
                [row(v) for v in (mixer_bias, first_gain, first_shift, contract_bias, second_gain, second_shift,
                                  expand_bias, pair_bias)] + [jnp.zeros((8, 128), BF16)], axis=0
            )
            w = lax.all_gather(lax.all_gather(pack, "batch", axis=1, tiled=True), "tensor", axis=1)
            v = lax.all_gather(lax.all_gather(vec, "batch"), "tensor")
            d_vec = v[0, :, :6, :nr].transpose(1, 0, 2).reshape(6, width).astype(F32)
            e_bias = v[:, :, 6, :nr].transpose(0, 2, 1).reshape(n_tensor, width).astype(F32)
            p_bias = v[:, :, 7, :2 * feat // n_batch].reshape(n_tensor, n_batch, 2, feat // n_batch)
            p_bias = p_bias.transpose(2, 0, 3, 1).reshape(2, n_tensor, feat).astype(F32)
            mine = partial(lax.dynamic_slice_in_dim, start_index=t * own_pairs, slice_size=own_pairs, axis=0)
            outputs, input_grad, grads, vecs, e_grad, p_grad = layer_step(
                mine(inputs), mine(lengths), mine(cotangent), w, d_vec, e_bias, p_bias
            )
            rows = own_pairs * length
            dv = jnp.broadcast_to(vecs.reshape(1, 6, n_batch, nr).transpose(0, 2, 1, 3), (n_tensor, n_batch, 6, nr))
            ev = e_grad.reshape(n_tensor, nr, n_batch).transpose(0, 2, 1)[:, :, None]
            pv = p_grad.reshape(2, n_tensor, feat // n_batch, n_batch).transpose(1, 3, 0, 2)
            pv = pv.reshape(n_tensor, n_batch, 1, 2 * feat // n_batch)
            lanes = lambda a: jnp.pad(a, ((0, 0), (0, 0), (0, 0), (0, 128 - a.shape[-1])))
            tiles = jnp.concatenate([lanes(dv), lanes(ev), lanes(pv)], axis=2)
            grads = lax.psum_scatter(grads.astype(F32), "tensor", scatter_dimension=1)
            red = lax.psum_scatter(grads, "batch", scatter_dimension=1, tiled=True)
            vred = lax.psum_scatter(lax.psum_scatter(tiles, "tensor"), "batch")
            outs = lax.all_gather(outputs, "tensor").reshape(pairs, length, width)
            ig = lax.all_to_all(
                input_grad.reshape(rows, n_tensor, feat), "tensor", split_axis=1, concat_axis=0, tiled=True
            )
            ig = ig.reshape(pairs, length, feat).astype(F32)
            att_g = red[0]
            four_g = [
                jnp.concatenate([att_g[:, i * cut:(i + 1) * cut], att_g[:, 4 * cut + i * HEAD:4 * cut + (i + 1) * HEAD]], axis=1)
                for i in range(4)
            ]
            triple_grad, mixer_grad = jnp.stack(four_g[:3]), four_g[3].T
            expand_grad, contract_grad = red[1], red[2].T
        return (
            outs,
            ig,
            triple_grad,
            vred[7, :2 * feat // n_batch].reshape(pair_bias.shape),
            mixer_grad,
            vred[0, :nr],
            vred[1, :nr],
            vred[2, :nr],
            expand_grad,
            vred[6, :nr].reshape(expand_bias.shape),
            contract_grad,
            vred[3, :nr],
            vred[4, :nr],
            vred[5, :nr],
        )

    return on_device


def solution(mesh):
    return jax.shard_map(
        make_on_device(dict(mesh.shape)),
        mesh=mesh,
        in_specs=(
            P("batch", None, None),
            P("batch"),
            P(None, "batch", "tensor"),
            P(None, "tensor", "batch"),
            P("tensor", "batch"),
            P("batch"),
            P("batch"),
            P("batch"),
            P("batch", "tensor"),
            P("tensor", "batch"),
            P("tensor", "batch"),
            P("batch"),
            P("batch"),
            P("batch"),
            P("batch", None, None),
        ),
        out_specs=(
            P("batch", None, None),
            P("batch", None, "tensor"),
            P(None, "batch", "tensor"),
            P(None, "tensor", "batch"),
            P("tensor", "batch"),
            P("batch"),
            P("batch"),
            P("batch"),
            P("batch", "tensor"),
            P("tensor", "batch"),
            P("tensor", "batch"),
            P("batch"),
            P("batch"),
            P("batch"),
        ),
        check_vma=False,
    )
```

```python
from functools import partial

import jax
import jax.numpy as jnp
from jax import lax
from jax.experimental import pallas as pl
from jax.experimental.pallas import tpu as pltpu
from jax.sharding import PartitionSpec as P

HEAD = 64
EPS = 1e-12
SCALE = 0.125
MASKED = -1e30
MESH = pl.DeviceIdType.MESH
F32 = jnp.float32
BF16 = jnp.bfloat16
NZ, NY, NX, NC = 4, 2, 2, 2


class Place:
    def __init__(self):
        b = lax.axis_index("batch")
        t = lax.axis_index("tensor")
        self.z, self.y = b // NY, b % NY
        self.x, self.c = t // NC, t % NC

    def at(self, z=None, y=None, x=None, c=None):
        z = self.z if z is None else z
        y = self.y if y is None else y
        x = self.x if x is None else x
        c = self.c if c is None else c
        return (z * NY + y, x * NC + c)

    def core(self):
        return self.at(c=1 - self.c)

    def xp(self):
        return self.at(x=1 - self.x)

    def yp(self):
        return self.at(y=1 - self.y)

    def zp(self, step):
        return self.at(z=(self.z + step) % NZ)

    def peers(self):
        return [self.core(), self.xp(), self.yp()] + [self.zp(s) for s in range(1, NZ)]

    def signal(self):
        barrier = pltpu.get_barrier_semaphore()
        for peer in self.peers():
            pl.semaphore_signal(barrier, inc=1, device_id=peer, device_id_type=MESH)

    def meet(self):
        pl.semaphore_wait(pltpu.get_barrier_semaphore(), len(self.peers()))

    def own(self, axis):
        return {"x": self.x, "y": self.y, "z": self.z}[axis]

    def others(self, axis):
        if axis == "z":
            return [(self.z + s) % NZ for s in range(1, NZ)]
        return [1 - self.own(axis)]

    def along(self, axis):
        if axis == "z":
            return [self.zp(s) for s in range(1, NZ)]
        return [self.xp() if axis == "x" else self.yp()]


def remote(src, dst, sems, index, peer):
    return pltpu.make_async_remote_copy(
        src_ref=src,
        dst_ref=dst,
        send_sem=sems.at[0, index],
        recv_sem=sems.at[1, index],
        device_id=peer,
        device_id_type=MESH,
    )


def normalize(value_rows, gain, shift):
    centred = value_rows - jnp.mean(value_rows, axis=-1, keepdims=True)
    scaled = lax.rsqrt(jnp.mean(centred * centred, axis=-1, keepdims=True) + EPS)
    normed = centred * scaled
    return (normed * gain + shift, normed, scaled)


def normalize_back(grad, normed, scaled, gain):
    weighted = grad * gain
    inner = jnp.mean(weighted * normed, axis=-1, keepdims=True)
    return scaled * (weighted - jnp.mean(weighted, axis=-1, keepdims=True) - normed * inner)


SQRT_HALF = 0.7071067811865476
INV_SQRT_2PI = 0.3989422804014327
LOG2_E = 1.4426950408889634
ERF_P = 0.3275911
ERF_A = (0.254829592, -0.284496736, 1.421413741, -1.453152027, 1.061405429)
TILE = 96
CUT = 2 * HEAD


def dot(a, b):
    return lax.dot_general(a, b, (((1,), (0,)), ((), ())), preferred_element_type=F32)


def dot_nt(a, b):
    return lax.dot_general(a, b, (((1,), (1,)), ((), ())), preferred_element_type=F32)


def gelu_parts(v):
    t = 1.0 / (1.0 + (ERF_P * SQRT_HALF) * jnp.abs(v))
    bell = jnp.exp2((-0.5 * LOG2_E) * (v * v))
    poly = 0.5 * ERF_A[4]
    for a in ERF_A[3::-1]:
        poly = poly * t + 0.5 * a
    tail = poly * t * bell
    phi = jnp.where(v < 0.0, tail, 1.0 - tail)
    return v * phi, phi + v * bell * INV_SQRT_2PI


def low_lanes():
    return lax.broadcasted_iota(jnp.int32, (1, CUT), 1) < HEAD


def half_rows():
    lane = lax.broadcasted_iota(jnp.int32, (1, CUT), 1)
    low = jnp.where(lane < HEAD, 1.0, 0.0)
    return low.astype(BF16), (1.0 - low).astype(BF16)


def swap(a):
    return pltpu.roll(a, HEAD, 1)


def sel_matrix(key, b):
    lane = lax.broadcasted_iota(jnp.int32, (128, key.shape[1]), 0) * (NZ * NY) + b
    return jnp.where(lane == key, 1.0, 0.0).astype(BF16)


def sel_keys(width):
    col = lax.broadcasted_iota(jnp.int32, (1, width), 1)
    nr = width // (NZ * NY)
    q = jnp.where(col < CUT, col, col - 3 * CUT)
    v = jnp.where(col < 3 * CUT, col - 2 * CUT, col - 4 * CUT)
    is_q = (col < CUT) | ((col >= 4 * CUT) & (col < 4 * CUT + HEAD))
    is_v = ((col >= 2 * CUT) & (col < 3 * CUT)) | ((col >= 5 * CUT) & (col < 5 * CUT + HEAD))
    head = jnp.where(is_q, q, jnp.where(is_v, v + 3 * HEAD, -1))
    return (col % nr) * (NZ * NY) + col // nr, col, head


def run_hooks(hooks, i):
    for k, step in (hooks or {}).items():
        pl.when(i == k)(step)


class Layer:
    def __init__(self, **refs):
        self.__dict__.update(refs)
        self.tiles = self.x.shape[0]
        self.width = self.x.shape[2]
        self.rows = self.tiles * TILE
        self.seqs = self.qkv.shape[2]
        self.length = self.qkv.shape[3]
        self.per = self.length // TILE

    def weight(self, p, t, lo, size):
        c, x = t // NX, t % NX
        return self.w[p, c, x, :, :, :, lo:lo + size].reshape(self.width, size)

    def put_weight(self, p, t, lo, value):
        c, x = t // NX, t % NX
        size = value.shape[1]
        nr = self.width // (NZ * NY)
        self.w[p, c, x, :, :, :, lo:lo + size] = value.astype(BF16).reshape(NZ, NY, nr, size)

    def all_rows(self, ref, *at):
        a = ref[at] if at else ref[...]
        return a.reshape(self.rows, a.shape[-1])

    def seq_rows(self, ref, s, *at):
        a = ref[at + (pl.ds(self.per * s, self.per),)]
        return a.reshape(self.length, a.shape[-1])

    def transposed(self, ref, out):
        a = self.all_rows(ref)
        out[0:self.width, :] = a.T
        out[self.width:, :] = jnp.ones((out.shape[0] - self.width, self.rows), BF16)

    def vectors(self):
        keys = sel_keys(self.width)
        self.vec[...] = jnp.zeros(self.vec.shape, F32)

        @pl.loop(0, NZ * NY)
        def _(b):
            z, y = b // NY, b % NY
            own = self.v[:, :, z, y].reshape(NC * NX * 8, 128).astype(BF16)
            for i, key in enumerate(keys):
                part = dot(own, sel_matrix(key, b)).reshape(NC * NX, 8, self.width)
                self.vec[i] = self.vec[i] + part

    def row(self, i):
        return self.vec[0, 0, i:i + 1, :]

    def projected(self, t, n):
        bias = self.vec[2, t, 7:8, 256 * n:256 * n + 256]
        return dot(self.all_rows(self.x), self.weight(0, t, 256 * n, 256)) + bias

    def put_head(self, i, p, value):
        self.qkv[i, p] = value.astype(BF16).reshape(self.seqs, self.length, CUT)

    def projections_first(self):
        @pl.loop(0, NC * NX)
        def _(t):
            a = self.projected(t, 0)
            self.put_head(0, t, a[:, :CUT])
            self.put_head(1, t, a[:, CUT:])
            bias = self.vec[2, t, 7:8, 2 * CUT:3 * CUT]
            self.put_head(2, t, dot(self.all_rows(self.x), self.weight(0, t, 2 * CUT, CUT)) + bias)

    def projections_third(self):
        low = low_lanes()

        @pl.loop(0, NC)
        def _(u):
            a, b = self.projected(NX * u, 2), self.projected(NX * u + 1, 2)
            self.put_head(0, NC * NX + u, jnp.where(low, a[:, :CUT], swap(b[:, :CUT])))
            self.put_head(1, NC * NX + u, jnp.where(low, swap(a[:, :CUT]), b[:, :CUT]))
            self.put_head(2, NC * NX + u, jnp.where(low, a[:, CUT:], swap(b[:, CUT:])))

    def heads(self, p, s):
        halves = half_rows()
        q, k, v = (self.qkv[i, p, s] for i in range(3))
        valid = lax.broadcasted_iota(jnp.int32, (1, self.length), 1) < self.lens[self.first + s]
        context = []
        for j in range(2):
            scores = jnp.where(valid, dot_nt(q * halves[j], k) * SCALE, MASKED)
            powers = jnp.exp(scores - jnp.max(scores, axis=1, keepdims=True))
            probs = (powers * (1.0 / jnp.sum(powers, axis=1, keepdims=True))).astype(BF16)
            self.probs[p, s, j] = probs
            context.append(dot(probs, v))
        return jnp.where(low_lanes(), *context)

    def put_context(self, t, s, lo, value):
        value = value.astype(BF16).reshape(self.per, TILE, CUT)
        self.ctx[t, pl.ds(self.per * s, self.per), :, lo:lo + CUT] = value

    def attention_first(self, hooks=None):
        @pl.loop(0, NC * NX * self.seqs)
        def _(i):
            run_hooks(hooks, i)
            t, s = i // self.seqs, i % self.seqs
            self.put_context(t, s, 0, self.heads(t, s))

    def attention_third(self, hooks=None):
        low = low_lanes()

        @pl.loop(0, NC * self.seqs)
        def _(i):
            run_hooks(hooks, i)
            u, s = i // self.seqs, i % self.seqs
            context = self.heads(NC * NX + u, s)
            self.put_context(NX * u, s, CUT, jnp.where(low, 0.0, swap(context)))
            self.put_context(NX * u + 1, s, CUT, jnp.where(low, 0.0, context))

    def mixer_weight(self, t):
        return jnp.concatenate([self.weight(0, t, 3 * CUT, CUT), self.weight(0, t, 5 * CUT, CUT)], axis=1)

    def put_rows(self, ref, s, value):
        ref[pl.ds(self.per * s, self.per)] = value.reshape(self.per, TILE, value.shape[1])

    def mix(self):
        @pl.loop(0, self.seqs)
        def _(s):
            total = None
            for t in range(NC * NX):
                part = dot_nt(self.seq_rows(self.ctx, s, t), self.mixer_weight(t))
                total = part if total is None else total + part
            self.put_rows(self.tmp, s, total)

    def norm_first(self, hooks=None):
        @pl.loop(0, self.tiles)
        def _(i):
            run_hooks(hooks, i)
            total = self.x[i].astype(F32) + self.tmp[i] + self.row(0)
            _, normed, scaled = normalize(total, 1.0, 0.0)
            self.norm[i] = normed
            self.scaled[i] = scaled
            self.hidden[i] = (normed * self.row(1) + self.row(2)).astype(BF16)

    def expand(self, hooks, chunks):
        @pl.loop(0, NC * NX)
        def _(t):
            run_hooks(hooks, t)
            hidden = self.all_rows(self.hidden)
            for n in chunks:
                cols = slice(256 * n, 256 * n + 256)
                before = dot(hidden, self.weight(1, t, 256 * n, 256)) + self.vec[1, t, 6:7, cols]
                act, slope = gelu_parts(before)
                self.act[t, :, :, cols] = act.astype(BF16).reshape(self.tiles, TILE, 256)
                self.slope[t, :, :, cols] = slope.astype(BF16).reshape(self.tiles, TILE, 256)

    def times_back(self, p, ref, lo=0, size=None, more=False, hooks=None):
        size = self.width if size is None else size

        @pl.loop(0, self.seqs)
        def _(s):
            run_hooks(hooks, s)
            rows = pl.ds(self.per * s, self.per)
            total = self.tmp[rows].reshape(self.length, self.width) if more else None
            for t in range(NC * NX):
                left = ref[t, rows, :, lo:lo + size].reshape(self.length, size)
                part = dot_nt(left, self.weight(p, t, lo, size))
                total = part if total is None else total + part
            self.put_rows(self.tmp, s, total)

    def add_sum(self, i, value):
        self.sums[i] = self.sums[i] + jnp.sum(value.reshape(TILE // 8, 8, self.width), axis=0)

    def clear_sums(self):
        self.sums[...] = jnp.zeros(self.sums.shape, F32)

    def norm_second(self, hooks=None):
        @pl.loop(0, self.tiles)
        def _(i):
            run_hooks(hooks, i)
            hidden = self.norm[i] * self.row(1) + self.row(2)
            _, normed, scaled = normalize(hidden + self.tmp[i] + self.row(3), 1.0, 0.0)
            self.out[i] = (normed * self.row(4) + self.row(5)).astype(BF16)
            up = self.cot[i].astype(F32)
            self.add_sum(4, up * normed)
            self.add_sum(5, up)
            after = normalize_back(up, normed, scaled, self.row(4))
            self.add_sum(3, after)
            self.grad[i] = after
            self.low[i] = after.astype(BF16)

    def act_back(self, chunks, hooks=None):
        @pl.loop(0, NC * NX)
        def _(t):
            run_hooks(hooks, t)
            low = self.all_rows(self.low)
            for n in chunks:
                cols = slice(256 * n, 256 * n + 256)
                up = dot(low, self.weight(2, t, 256 * n, 256)).reshape(self.tiles, TILE, 256)
                self.slope[t, :, :, cols] = (up * self.slope[t, :, :, cols].astype(F32)).astype(BF16)

    def contract_grad(self, chunks, hooks=None):
        @pl.loop(0, NC * NX)
        def _(t):
            run_hooks(hooks, t)
            left = self.left[0:self.width, :]
            for n in chunks:
                right = self.all_rows(self.act, t, slice(None), slice(None), slice(256 * n, 256 * n + 256))
                self.put_weight(2, t, 256 * n, dot(left, right))

    def expand_grad(self, chunks, hooks=None):
        @pl.loop(0, NC * NX)
        def _(t):
            run_hooks(hooks, t)
            for n in chunks:
                cols = slice(256 * n, 256 * n + 256)
                grad = dot(self.left[...], self.all_rows(self.slope, t, slice(None), slice(None), cols))
                self.put_weight(1, t, 256 * n, grad[:self.width])
                self.unit_sums[0, t, :, cols] = grad[self.width:self.width + 8]

    def norm_first_back(self, hooks=None):
        @pl.loop(0, self.tiles)
        def _(i):
            run_hooks(hooks, i)
            grad = self.grad[i] + self.tmp[i]
            normed = self.norm[i]
            self.add_sum(1, grad * normed)
            self.add_sum(2, grad)
            after = normalize_back(grad, normed, self.scaled[i], self.row(1))
            self.add_sum(0, after)
            self.grad[i] = after
            self.low[i] = after.astype(BF16)

    def context_back(self):
        low = low_lanes()

        @pl.loop(0, NC)
        def _(u):
            third = []
            for d in range(NX):
                t = NX * u + d
                grad = dot(self.all_rows(self.low), self.mixer_weight(t))
                self.cgrad[t] = grad[:, :CUT].astype(BF16).reshape(self.seqs, self.length, CUT)
                third.append(grad[:, CUT:])
            pair = jnp.where(low, swap(third[0]), third[1])
            self.cgrad[NC * NX + u] = pair.astype(BF16).reshape(self.seqs, self.length, CUT)

    def heads_back(self, p, s):
        halves = half_rows()
        q, k, v = (self.qkv[i, p, s] for i in range(3))
        up = self.cgrad[p, s]
        up_t = up.T
        q_t = q.T
        dq, dk, dv = [], [], []
        for j in range(2):
            probs = self.probs[p, s, j]
            dv.append(dot(up_t[HEAD * j:HEAD * j + HEAD], probs))
            weight = dot_nt(up * halves[j], v)
            wide = probs.astype(F32)
            grad = wide * (weight - jnp.sum(wide * weight, axis=1, keepdims=True))
            grad = grad.astype(BF16)
            dq.append(dot(grad, k))
            dk.append(dot(q_t[HEAD * j:HEAD * j + HEAD], grad))
        dq = jnp.where(low_lanes(), *dq) * SCALE
        dk = jnp.concatenate(dk, axis=0).T * SCALE
        dv = jnp.concatenate(dv, axis=0).T
        return dq, dk, dv

    def put_stream(self, t, s, lo, value):
        value = value.astype(BF16).reshape(self.per, TILE, CUT)
        self.act[t, pl.ds(self.per * s, self.per), :, lo:lo + CUT] = value

    def attention_back_first(self, hooks=None):
        @pl.loop(0, NC * NX * self.seqs)
        def _(i):
            run_hooks(hooks, i)
            t, s = i // self.seqs, i % self.seqs
            grads = self.heads_back(t, s)
            for j in range(3):
                self.put_stream(t, s, CUT * j, grads[j])
            self.put_stream(t, s, 3 * CUT, jnp.zeros((self.length, CUT), F32))

    def attention_back_third(self, hooks=None):
        low = low_lanes()

        @pl.loop(0, NC * self.seqs)
        def _(i):
            run_hooks(hooks, i)
            u, s = i // self.seqs, i % self.seqs
            dq, dk, dv = self.heads_back(NC * NX + u, s)
            self.put_stream(NX * u, s, 4 * CUT, jnp.where(low, dq, swap(dk)))
            self.put_stream(NX * u + 1, s, 4 * CUT, jnp.where(low, swap(dq), dk))
            self.put_stream(NX * u, s, 5 * CUT, jnp.where(low, dv, 0.0))
            self.put_stream(NX * u + 1, s, 5 * CUT, jnp.where(low, swap(dv), 0.0))

    def input_back(self):
        half = self.width // NX

        @pl.loop(0, self.tiles)
        def _(i):
            total = (self.grad[i] + self.tmp[i]).astype(BF16)
            for x in range(NX):
                self.igrad[x, i] = total[:, half * x:half * x + half]

    def stream_grad(self, t, n):
        cols = slice(256 * n, 256 * n + 256)
        grad = dot(self.left[...], self.all_rows(self.act, t, slice(None), slice(None), cols))
        self.unit_sums[1, t, :, cols] = grad[self.width:self.width + 8]
        return grad[:self.width]

    def mixer_grad(self, t, h):
        cols = slice(CUT * h, CUT * h + CUT)
        return dot(self.left2[0:self.width, :], self.all_rows(self.ctx, t, slice(None), slice(None), cols))

    def attention_grad_first(self, hooks=None):
        @pl.loop(0, NC * NX)
        def _(t):
            run_hooks(hooks, t)
            self.put_weight(0, t, 0, self.stream_grad(t, 0))
            grad = self.stream_grad(t, 1)
            self.put_weight(0, t, 2 * CUT, grad[:, :CUT])
            self.put_weight(0, t, 3 * CUT, self.mixer_grad(t, 0))

    def attention_grad_third(self, hooks=None):
        @pl.loop(0, NC * NX)
        def _(t):
            run_hooks(hooks, t)
            grad = self.stream_grad(t, 2)
            self.put_weight(0, t, 4 * CUT, grad[:, :CUT])
            self.put_weight(0, t, 5 * CUT, grad[:, CUT:] + self.mixer_grad(t, 1))

    def vector_tiles(self):
        keys = sel_keys(self.width)
        rows = [jnp.sum(self.sums[i], axis=0, keepdims=True) for i in range(6)]
        rows.append(jnp.zeros((2, self.width), F32))
        parts = [jnp.concatenate(rows, axis=0)]
        for i in range(2):
            units = [self.unit_sums[i, t, 0:1, :] for t in range(NC * NX)]
            parts.append(jnp.concatenate(units + [jnp.zeros((4, self.width), F32)], axis=0))
        split = []
        for part in parts:
            high = part.astype(BF16)
            split.append(jnp.concatenate([high, (part - high.astype(F32)).astype(BF16)], axis=0))

        @pl.loop(0, NZ * NY)
        def _(b):
            z, y = b // NY, b % NY
            got = []
            for key, part in zip(keys, split):
                both = dot_nt(part, sel_matrix(key, b))
                got.append(both[:8] + both[8:])
            for t in range(NC * NX):
                self.vtiles[t // NX, t % NX, z, y] = jnp.concatenate(
                    [got[0][:6], got[1][t:t + 1], got[2][t:t + 1]], axis=0
                )


def layer_scratch(seqs, length, width):
    tiles = seqs * length // TILE
    blocks = NC * NX
    pairs = 3 * blocks // 2
    rows = seqs * length
    nr = width // (NZ * NY)
    return [
        pltpu.VMEM((3, NC, NX, NZ, NY, nr, width), BF16),
        pltpu.VMEM((tiles, TILE, width), BF16),
        pltpu.VMEM((tiles, TILE, width), BF16),
        pltpu.VMEM((3, pairs, seqs, length, CUT), BF16),
        pltpu.VMEM((pairs, seqs, 2, length, length), BF16),
        pltpu.VMEM((blocks, tiles, TILE, 2 * CUT), BF16),
        pltpu.VMEM((tiles, TILE, width), F32),
        pltpu.VMEM((tiles, TILE, width), F32),
        pltpu.VMEM((tiles, TILE, 1), F32),
        pltpu.VMEM((tiles, TILE, width), BF16),
        pltpu.VMEM((blocks, tiles, TILE, width), BF16),
        pltpu.VMEM((blocks, tiles, TILE, width), BF16),
        pltpu.VMEM((tiles, TILE, width), F32),
        pltpu.VMEM((tiles, TILE, width), BF16),
        pltpu.VMEM((pairs, seqs, length, CUT), BF16),
        pltpu.VMEM((width + 16, rows), BF16),
        pltpu.VMEM((width + 16, rows), BF16),
        pltpu.VMEM((3, blocks, 8, width), F32),
        pltpu.VMEM((6, 8, width), F32),
        pltpu.VMEM((2, blocks, 8, width), F32),
    ]


class Gather:
    def __init__(self, me, w, v, sems, vsems):
        self.me, self.w, self.v, self.sems, self.vsems = me, w, v, sems, vsems

    def hop(self, k, i):
        p, lo, size, route = GATHER_PARTS[k]
        me = self.me
        at = {axis: slice(None) if axis in route[:i] else me.own(axis) for axis in "xyz"}
        slot = self.w.at[p, me.c, at["x"], at["z"], at["y"], :, pl.ds(lo, size)]
        first = {"z": 0, "x": NZ - 1, "y": NZ}[route[i]]
        return [
            remote(slot, slot, self.sems, 5 * k + first + j, peer) for j, peer in enumerate(me.along(route[i]))
        ]

    def start(self, k, i):
        if i > 0:
            for copy in self.hop(k, i - 1):
                copy.wait_recv()
        for copy in self.hop(k, i):
            copy.start()

    def core(self, group):
        p, lo, size, parts = GATHER_GROUPS[group]
        slot = self.w.at[p, self.me.c, :, :, :, :, pl.ds(lo, size)]
        return remote(slot, slot, self.sems, 5 * len(GATHER_PARTS) + group, self.me.core())

    def start_core(self, group):
        for k in GATHER_GROUPS[group][3]:
            for copy in self.hop(k, 2):
                copy.wait_recv()
        self.core(group).start()

    def arrived(self, group):
        self.core(group).wait_recv()

    def left(self, group):
        for k in GATHER_GROUPS[group][3]:
            for i in range(3):
                for copy in self.hop(k, i):
                    copy.wait_send()
        self.core(group).wait_send()

    def small(self):
        me, v = self.me, self.v
        def same(slot, index, peer):
            return remote(slot, slot, self.vsems, index, peer)
        return [
            [same(v.at[me.c, me.x, me.z, me.y], s, peer) for s, peer in enumerate(me.along("z"))],
            [same(v.at[me.c, me.x, :, me.y], 3, me.xp())],
            [same(v.at[me.c, :, :, me.y], 4, me.yp())],
            [same(v.at[me.c], 5, me.core())],
        ]

    def small_step(self, i):
        steps = self.small()
        if i > 0:
            for copy in steps[i - 1]:
                copy.wait_recv()
        if i < len(steps):
            for copy in steps[i]:
                copy.start()

    def small_left(self):
        for copy in sum(self.small(), []):
            copy.wait_send()


GATHER_PARTS = (
    (0, 0, 128, "zyx"),
    (0, 128, 128, "zxy"),
    (0, 256, 128, "zyx"),
    (0, 384, 128, "zyx"),
    (0, 512, 128, "zxy"),
    (0, 640, 128, "zxy"),
    (1, 0, 256, "zyx"),
    (1, 256, 256, "zxy"),
    (1, 512, 128, "zyx"),
    (1, 640, 128, "zxy"),
    (2, 0, 256, "yzx"),
    (2, 256, 128, "zxy"),
    (2, 384, 256, "yxz"),
    (2, 640, 128, "xzy"),
)
GATHER_GROUPS = (
    (0, 0, 512, (0, 1, 2, 3)), (0, 512, 256, (4, 5)), (1, 0, 256, (6,)), (1, 256, 512, (7, 8, 9)),
    (2, 0, 384, (10, 11)), (2, 384, 384, (12, 13)),
)
SCATTER_PARTS = (
    (2, 0, 256, "yxz"),
    (2, 256, 128, "zxy"),
    (2, 384, 128, "xzy"),
    (2, 512, 128, "yzx"),
    (2, 640, 128, "zyx"),
    (1, 0, 256, "yxz"),
    (1, 256, 128, "yzx"),
    (1, 384, 128, "xyz"),
    (1, 512, 256, "yxz"),
    (0, 0, 256, "xyz"),
    (0, 256, 128, "yxz"),
    (0, 384, 128, "yzx"),
    (0, 512, 128, "xyz"),
    (0, 640, 128, "yzx"),
)
SCATTER_GROUPS = (
    (2, 0, 256, (0,)), (2, 256, 256, (1, 2)), (2, 512, 256, (3, 4)), (1, 0, 256, (5,)), (1, 256, 512, (6, 7, 8)),
    (0, 0, 512, (9, 10, 11)), (0, 512, 256, (12, 13)),
)
AXIS = {"x": NX, "y": NY, "z": NZ}


class Scatter:
    def __init__(self, me, g, v, bufs, sems, vsems, osems, out, outs, ig, igs):
        self.me, self.g, self.v = me, g, v
        self.rc, self.rb, self.vc, self.vy, self.vx, self.vz = bufs
        self.sems, self.vsems, self.osems = sems, vsems, osems
        self.out, self.outs, self.ig, self.igs = out, outs, ig, igs

    def core(self, group):
        p, lo, size, _ = SCATTER_GROUPS[group]
        me, cols = self.me, pl.ds(lo, size)
        return remote(
            self.g.at[p, 1 - me.c, :, :, :, :, cols], self.rc.at[p, :, :, :, :, cols],
            self.sems, 9 * len(SCATTER_PARTS) + group, me.core(),
        )

    def start_core(self, group):
        self.core(group).start()

    def add_core(self, group):
        p, lo, size, _ = SCATTER_GROUPS[group]
        c, cols = self.me.c, slice(lo, lo + size)
        self.core(group).wait_recv()

        @pl.loop(0, NZ)
        def _(j):
            for i in range(NX):
                for k in range(NY):
                    self.g[p, c, i, j, k, :, cols] = self.g[p, c, i, j, k, :, cols] + self.rc[p, i, j, k, :, cols]

    def plan(self, k, i):
        p, lo, size, route = SCATTER_PARTS[k]
        me = self.me
        axis = route[i]
        done = {a: me.own(a) for a in route[:i]}
        every = slice(None)
        moves = []
        sizes = [AXIS[a] for a in route]
        at = sum((sizes[n] - 1) * sizes[n + 1] * (sizes[2] if n == 0 else 1) for n in range(i))
        for peer, other in zip(me.along(axis), me.others(axis)):
            spare = [a for a in "xyz" if a != axis and a not in done]
            inner = "z" if "z" in spare else (spare[-1] if spare else None)
            outer = [a for a in spare if a != inner]
            for o in range(2 if outer else 1):
                send = dict(done)
                if outer:
                    send[outer[0]] = o
                if inner:
                    send[inner] = every
                keep = dict(send)
                send[axis], keep[axis] = other, me.own(axis)
                count = None if inner is None else (NZ if inner == "z" else 2)
                moves.append((send, keep, at, count, peer))
                at += 1 if count is None else count
        return p, lo, size, moves

    def hop(self, k, i):
        p, lo, size, moves = self.plan(k, i)
        me, cols = self.me, pl.ds(lo, size)
        base = 9 * k + sum(len(self.plan(k, n)[3]) for n in range(i))
        copies = []
        for j, (send, _, at, count, peer) in enumerate(moves):
            src = self.g.at[p, me.c, send["x"], send["z"], send["y"], :, cols]
            dst = self.rb.at[p, at, :, cols] if count is None else self.rb.at[p, pl.ds(at, count), :, cols]
            copies.append(remote(src, dst, self.sems, base + j, peer))
        return copies

    def start(self, k, i):
        if i > 0:
            self.add(k, i - 1)
        for copy in self.hop(k, i):
            copy.start()

    def add(self, k, i):
        p, lo, size, moves = self.plan(k, i)
        c, cols = self.me.c, slice(lo, lo + size)
        for copy in self.hop(k, i):
            copy.wait_recv()
        terms = {}
        for _, keep, at, count, _ in moves:
            inner = [a for a in "xyz" if isinstance(keep[a], slice)]
            for n in range(1 if count is None else count):
                spot = dict(keep)
                if inner:
                    spot[inner[0]] = n
                name = tuple(spot[a] if isinstance(spot[a], int) else a for a in "xyz")
                terms.setdefault(name, (spot, []))[1].append(at + n)
        for spot, places in terms.values():
            ref = self.g.at[p, c, spot["x"], spot["z"], spot["y"], :, cols]
            if len(places) == 1:
                ref[...] = ref[...] + self.rb[p, places[0], :, cols]
            else:
                total = ref[...].astype(F32)
                for n in places:
                    total = total + self.rb[p, n, :, cols].astype(F32)
                ref[...] = total.astype(BF16)

    def total(self, k):
        p, lo, size, moves = self.plan(k, 2)
        me, cols = self.me, slice(lo, lo + size)
        for copy in self.hop(k, 2):
            copy.wait_recv()
        total = self.g[p, me.c, me.x, me.z, me.y, :, cols].astype(F32)
        for _, _, at, _, _ in moves:
            total = total + self.rb[p, at, :, cols].astype(F32)
        return total

    def left(self, group):
        self.core(group).wait_send()
        for k in SCATTER_GROUPS[group][3]:
            for i in range(3):
                for copy in self.hop(k, i):
                    copy.wait_send()

    def small(self, i):
        me, v, sems = self.me, self.v, self.vsems
        if i == 0:
            return [remote(v.at[1 - me.c], self.vc, sems, 0, me.core())]
        if i == 1:
            return [remote(v.at[me.c, :, :, 1 - me.y], self.vy, sems, 1, me.yp())]
        if i == 2:
            return [remote(v.at[me.c, 1 - me.x, :, me.y], self.vx, sems, 2, me.xp())]
        return [
            remote(v.at[me.c, me.x, (me.z + s) % NZ, me.y], self.vz.at[s - 1], sems, 2 + s, me.zp(s))
            for s in range(1, NZ)
        ]

    def small_step(self, i):
        me, v = self.me, self.v
        if i > 0:
            for copy in self.small(i - 1):
                copy.wait_recv()
        if i == 1:
            v[me.c] = v[me.c] + self.vc[...]
        elif i == 2:
            v[me.c, :, :, me.y] = v[me.c, :, :, me.y] + self.vy[...]
        elif i == 3:
            v[me.c, me.x, :, me.y] = v[me.c, me.x, :, me.y] + self.vx[...]
        elif i == 4:
            total = v[me.c, me.x, me.z, me.y]
            for s in range(1, NZ):
                total = total + self.vz[s - 1]
            return total
        for copy in self.small(i):
            copy.start()

    def small_left(self):
        for i in range(4):
            for copy in self.small(i):
                copy.wait_send()

    def outputs(self):
        me = self.me
        t = me.x * NC + me.c
        return [remote(self.out, self.outs.at[t], self.osems, i, peer) for i, peer in enumerate((me.xp(), me.core()))]

    def output_local(self, sem):
        return pltpu.make_async_copy(self.out, self.outs.at[self.me.x * NC + self.me.c], sem)

    def output_forward(self):
        me = self.me
        t = (1 - me.x) * NC + me.c
        return remote(self.outs.at[t], self.outs.at[t], self.osems, 4, me.core())

    def grads(self):
        me = self.me
        t = me.x * NC + me.c
        return [
            remote(self.ig.at[1 - me.x], self.igs.at[t], self.osems, 2, me.xp()),
            remote(self.ig.at[me.x], self.igs.at[t], self.osems, 3, me.core()),
        ]

    def grad_local(self, sem):
        return pltpu.make_async_copy(self.ig.at[self.me.x], self.igs.at[self.me.x * NC + self.me.c], sem)

    def grad_forward(self):
        me = self.me
        t = (1 - me.x) * NC + me.c
        return remote(self.igs.at[t], self.igs.at[t], self.osems, 5, me.core())


def step_kernel(
    x_in, cot_in, lens, tw, mw, ew, cw, b0, b1, b2, b3, b4, b5, b6, pair_in,
    outs, igs, triple_out, mixer_out, expand_out, contract_out, small_out,
    w, v, vtiles, out, ig,
    x, cot, qkv, probs, ctx, tmp, norm, scaled, hidden, act, slope, grad, low, cgrad, left, left2, vec, sums,
    unit_sums,
    rc, rb, vc, vy, vx, vz,
    gsems, gvsems, sems, vsems, osems, lsems,
):
    me = Place()
    t = lax.axis_index("tensor")
    seqs = qkv.shape[2]
    own = [w.at[p, me.c, me.x, me.z, me.y] for p in range(3)]
    load_e = pltpu.make_async_copy(ew, own[1], lsems.at[2])
    load_c = pltpu.make_async_copy(cw, own[2], lsems.at[6])
    load_x = pltpu.make_async_copy(x_in.at[t], x, lsems.at[0])
    load_cot = pltpu.make_async_copy(cot_in.at[t], cot, lsems.at[1])
    me.signal()
    for copy in (load_e, load_c, load_x, load_cot):
        copy.start()
    pack_attention(tw, mw, own[0])
    pack_vectors((b0, b1, b2, b3, b4, b5, b6), pair_in, v.at[me.c, me.x, me.z, me.y])
    gather = Gather(me, w, v, gsems, gvsems)
    layer = Layer(
        w=w, x=x, cot=cot, qkv=qkv, probs=probs, ctx=ctx, tmp=tmp, norm=norm, scaled=scaled, hidden=hidden, act=act,
        slope=slope, grad=grad, low=low, cgrad=cgrad, left=left, left2=left2, vec=vec, sums=sums, unit_sums=unit_sums,
        v=v, out=out, igrad=ig, vtiles=vtiles, lens=lens, first=t * seqs,
    )
    scatter = Scatter(me, w, vtiles, (rc, rb, vc, vy, vx, vz), sems, vsems, osems, out, outs, ig, igs)
    me.meet()
    load_e.wait()
    load_c.wait()
    gather.start(12, 0)
    gather.small_step(0)
    gather.start(13, 0)
    gather.start(2, 0)
    gather.start(5, 0)
    gather.start(4, 0)
    gather.start(12, 1)
    gather.start(0, 0)
    gather.start(3, 0)
    gather.start(1, 0)
    gather.start(8, 0)
    gather.start(2, 1)
    gather.start(7, 0)
    gather.small_step(1)
    gather.small_step(2)
    gather.start(10, 0)
    gather.start(5, 1)
    gather.start(4, 1)
    gather.start(2, 2)
    gather.start(9, 0)
    gather.start(0, 1)
    gather.start(3, 1)
    gather.start(6, 0)
    gather.small_step(3)
    gather.start(1, 1)
    gather.start(11, 0)
    gather.start(4, 2)
    layer.clear_sums()
    gather.start(3, 2)
    gather.start(8, 1)
    gather.start(0, 2)
    gather.start(10, 1)
    gather.start(7, 1)
    gather.start(1, 2)
    gather.start(6, 1)
    gather.start_core(0)
    gather.small_step(4)
    gather.start(5, 2)
    layer.vectors()
    load_x.wait()
    load_cot.wait()
    gather.start(11, 1)
    gather.arrived(0)
    gather.start(9, 1)
    layer.projections_first()
    gather.start(7, 2)
    gather.start(13, 1)
    def at_3_1():
        gather.start(6, 2)

    def at_3_4():
        gather.start(8, 2)
        gather.start_core(1)

    def at_3_5():
        gather.start(12, 2)

    def at_3_7():
        gather.start(9, 2)
        gather.arrived(1)
        gather.start(10, 2)

    layer.attention_first(hooks={1: at_3_1, 4: at_3_4, 5: at_3_5, 7: at_3_7})
    layer.projections_third()
    def at_5_1():
        gather.start_core(2)

    def at_5_2():
        gather.start(11, 2)

    layer.attention_third(hooks={1: at_5_1, 2: at_5_2})
    gather.start(13, 2)
    layer.mix()
    def at_7_4():
        gather.arrived(2)

    layer.norm_first(hooks={4: at_7_4})
    gather.start_core(3)
    layer.expand({}, (0,))
    gather.arrived(3)
    def at_9_2():
        gather.start_core(4)

    def at_9_3():
        gather.start_core(5)

    layer.expand({2: at_9_2, 3: at_9_3}, (1, 2))
    gather.arrived(4)
    layer.times_back(2, act, 0, 384, hooks={})
    gather.arrived(5)
    layer.times_back(2, act, 384, 384, True, hooks={})
    layer.norm_second(hooks={})
    for copy in scatter.outputs():
        copy.start()
    scatter.output_local(lsems.at[4]).start()
    layer.transposed(low, left)
    layer.act_back((0,), hooks={})
    gather.left(4)
    gather.left(5)
    layer.contract_grad((0,), hooks={})
    scatter.start_core(0)
    layer.act_back((1,), hooks={})
    def at_18_1():
        scatter.add_core(0)
        scatter.start(0, 0)

    layer.contract_grad((1,), hooks={1: at_18_1})
    scatter.start_core(1)
    layer.act_back((2,), hooks={})
    def at_20_1():
        scatter.add_core(1)
        scatter.start(1, 0)

    layer.contract_grad((2,), hooks={1: at_20_1})
    scatter.start_core(2)
    layer.times_back(1, slope, hooks={})
    scatter.add_core(2)
    layer.transposed(hidden, left)
    gather.left(2)
    gather.left(3)
    def at_24_3():
        scatter.start(2, 0)
        scatter.start(3, 0)

    layer.expand_grad((0,), hooks={3: at_24_3})
    def at_25_1():
        scatter.start(4, 0)
        scatter.start_core(3)

    layer.expand_grad((1, 2), hooks={1: at_25_1})
    scatter.start(0, 1)
    scatter.add_core(3)
    scatter.start_core(4)
    scatter.start(5, 0)
    layer.norm_first_back(hooks={})
    layer.transposed(low, left2)
    layer.context_back()
    scatter.add_core(4)
    scatter.start(8, 0)
    scatter.start(3, 1)
    scatter.start(7, 0)
    def at_29_2():
        scatter.start(1, 1)

    def at_29_4():
        scatter.start(2, 1)

    layer.attention_back_first(hooks={2: at_29_2, 4: at_29_4})
    scatter.start(0, 2)
    scatter.start(5, 1)
    layer.times_back(0, act, 0, 3 * CUT, hooks={})
    layer.transposed(x, left)
    scatter.start(7, 1)
    gather.left(0)
    def at_33_1():
        scatter.start(6, 0)

    layer.attention_grad_first(hooks={1: at_33_1})
    scatter.start_core(5)
    scatter.start(5, 2)
    scatter.start(8, 1)
    def at_34_3():
        scatter.start(1, 2)
        scatter.add_core(5)
        scatter.start(10, 0)
        scatter.start(7, 2)
        scatter.start(11, 0)
        scatter.start(9, 0)

    layer.attention_back_third(hooks={3: at_34_3})
    def at_35_1():
        scatter.start(8, 2)

    layer.times_back(0, act, 4 * CUT, 2 * CUT, True, hooks={1: at_35_1})
    layer.input_back()
    gather.left(1)
    def at_38_1():
        scatter.start(6, 1)

    layer.attention_grad_third(hooks={1: at_38_1})
    scatter.start_core(6)
    scatter.start(10, 1)
    scatter.outputs()[0].wait_recv()
    scatter.output_forward().start()
    scatter.add_core(6)
    scatter.start(13, 0)
    scatter.start(12, 0)
    scatter_out(scatter, 8, expand_out)
    scatter.start(11, 1)
    scatter.start(9, 1)
    for copy in scatter.grads():
        copy.start()
    scatter.grad_local(lsems.at[5]).start()
    scatter.start(10, 2)
    scatter.start(13, 1)
    layer.vector_tiles()
    scatter.start(12, 1)
    scatter_out(scatter, 0, contract_out)
    scatter.start(12, 2)
    scatter.small_step(0)
    scatter_out(scatter, 5, expand_out)
    scatter.start(4, 1)
    scatter.start(9, 2)
    scatter.small_step(1)
    scatter.small_step(2)
    scatter.start(6, 2)
    scatter.start(3, 2)
    scatter.start(2, 2)
    scatter.start(11, 2)
    scatter_out(scatter, 7, expand_out)
    scatter.start(13, 2)
    scatter_out(scatter, 1, contract_out)
    scatter.start(4, 2)
    scatter.grads()[0].wait_recv()
    scatter.grad_forward().start()
    scatter.small_step(3)
    scatter_out(scatter, 12, tmp.at[0])
    scatter_out(scatter, 3, contract_out)
    scatter_out(scatter, 10, tmp.at[0])
    scatter_out(scatter, 6, expand_out)
    scatter_out(scatter, 11, tmp.at[0])
    scatter_out(scatter, 4, contract_out)
    scatter_out(scatter, 9, tmp.at[0])
    scatter_out(scatter, 13, tmp.at[0])
    scatter_out(scatter, 2, contract_out)
    small_out[...] = scatter.small_step(4)
    unpack_attention(tmp[0], triple_out, mixer_out)
    scatter.outputs()[1].wait_recv()
    scatter.grads()[1].wait_recv()
    for copy in (scatter.output_forward(), scatter.grad_forward()):
        copy.wait()
    for copy in scatter.outputs() + scatter.grads():
        copy.wait_send()
    scatter.output_local(lsems.at[4]).wait()
    scatter.grad_local(lsems.at[5]).wait()
    gather.small_left()
    scatter.small_left()
    for group in range(len(SCATTER_GROUPS)):
        scatter.left(group)


def scatter_out(scatter, k, ref):
    _, lo, size, _ = SCATTER_PARTS[k]
    ref[:, lo:lo + size] = scatter.total(k)


def pack_attention(tw, mw, slot):
    mixer = mw[...].T
    for i in range(3):
        slot[:, CUT * i:CUT * i + CUT] = tw[i, :, 0:CUT]
    slot[:, 3 * CUT:4 * CUT] = mixer[:, 0:CUT]
    slot[:, 4 * CUT:5 * CUT] = jnp.concatenate([tw[0, :, CUT:], tw[1, :, CUT:]], axis=1)
    slot[:, 5 * CUT:6 * CUT] = jnp.concatenate([tw[2, :, CUT:], mixer[:, CUT:]], axis=1)


def pack_vectors(rows, pair, slot):
    slot[...] = jnp.zeros(slot.shape, F32)
    for i, ref in enumerate(rows):
        slot[i:i + 1, 0:ref.shape[0]] = ref[...].astype(F32).reshape(1, ref.shape[0])
    half = pair.shape[1]
    both = pair[...].astype(F32)
    slot[7:8, 0:half] = both[0:1]
    slot[7:8, half:2 * half] = both[1:2]


def unpack_attention(total, triple_out, mixer_out):
    for i in range(3):
        triple_out[i, :, 0:CUT] = total[:, CUT * i:CUT * i + CUT]
        triple_out[i, :, CUT:] = total[:, 4 * CUT + HEAD * i:4 * CUT + HEAD * i + HEAD]
    mixer_out[0:CUT] = total[:, 3 * CUT:4 * CUT].T
    mixer_out[CUT:] = total[:, 5 * CUT + HEAD:].T


def step_call(x, cot, lengths, tw, mw, ew, cw, vecs, seqs):
    pairs, length, width = x.shape
    tiles = seqs * length // TILE
    blocks = NX * NC
    nr, feat = width // (NZ * NY), width // blocks
    shape = (blocks, tiles, TILE, width)
    vmem = pl.BlockSpec(memory_space=pltpu.VMEM)
    hbm = pl.BlockSpec(memory_space=pl.ANY)
    layer = layer_scratch(seqs, length, width)
    small = (8, 128)
    return pl.pallas_call(
        step_kernel,
        out_shape=(
            jax.ShapeDtypeStruct(shape, BF16),
            jax.ShapeDtypeStruct((blocks, tiles, TILE, width // NX), BF16),
            jax.ShapeDtypeStruct((3, nr, feat), F32),
            jax.ShapeDtypeStruct((feat, nr), F32),
            jax.ShapeDtypeStruct((nr, width), F32),
            jax.ShapeDtypeStruct((nr, width), F32),
            jax.ShapeDtypeStruct(small, F32),
        ),
        in_specs=[hbm, hbm, pl.BlockSpec(memory_space=pltpu.SMEM), vmem, vmem, hbm, hbm] + [vmem] * len(vecs),
        out_specs=(hbm, hbm, vmem, vmem, vmem, vmem, vmem),
        scratch_shapes=[
            layer[0],
            pltpu.VMEM((NC, NX, NZ, NY) + small, F32),
            pltpu.VMEM((NC, NX, NZ, NY) + small, F32),
            pltpu.VMEM((tiles, TILE, width), BF16),
            pltpu.VMEM((NX, tiles, TILE, width // NX), BF16),
        ] + layer[1:] + [
            pltpu.VMEM((3, NX, NZ, NY, nr, width), BF16),
            pltpu.VMEM((3, 15, nr, width), BF16),
            pltpu.VMEM((NX, NZ, NY) + small, F32),
            pltpu.VMEM((NX, NZ) + small, F32),
            pltpu.VMEM((NZ,) + small, F32),
            pltpu.VMEM((NZ - 1,) + small, F32),
            pltpu.SemaphoreType.DMA((2, 5 * len(GATHER_PARTS) + len(GATHER_GROUPS))),
            pltpu.SemaphoreType.DMA((2, 6)),
            pltpu.SemaphoreType.DMA((2, 9 * len(SCATTER_PARTS) + len(SCATTER_GROUPS))),
            pltpu.SemaphoreType.DMA((2, 6)),
            pltpu.SemaphoreType.DMA((2, 6)),
            pltpu.SemaphoreType.DMA((7,)),
        ],
        compiler_params=pltpu.CompilerParams(
            collective_id=0, has_side_effects=True, vmem_limit_bytes=67043328
        ),
    )(x.reshape(shape), cot.reshape(shape), lengths, tw, mw, ew, cw, *vecs)


def layer_step(x_seq, lengths, cot, w, d_vec, e_bias, p_bias):
    seqs, length, width = x_seq.shape
    rows = seqs * length
    blocks = w.shape[1]
    feat = width // blocks
    heads = feat // HEAD
    mixer_shift, gain_one, shift_one, contract_shift, gain_two, shift_two = d_vec
    x = x_seq.reshape(rows, width)
    att = w[0]
    cut = 2 * HEAD
    def columns(i):
        return jnp.concatenate(
            [att[:, :, i * cut:(i + 1) * cut], att[:, :, 4 * cut + i * HEAD:4 * cut + (i + 1) * HEAD]], axis=2
        )
    wq, wk, wv, wm = (columns(i) for i in range(4))
    def project(weight, bias):
        out = jnp.einsum("rd,tde->rte", x, weight, preferred_element_type=F32)
        if bias is not None:
            out = out + bias
        return out.astype(BF16).reshape(seqs, length, blocks * heads, HEAD)
    queries = project(wq, p_bias[0])
    keys = project(wk, None)
    values = project(wv, p_bias[1])
    valid = lax.broadcasted_iota(jnp.int32, (seqs, 1, 1, length), 3) < lengths[:, None, None, None]
    raw = jnp.einsum("sqhd,skhd->shqk", queries, keys, preferred_element_type=F32) * SCALE
    raw = jnp.where(valid, raw, MASKED)
    peak = jnp.max(raw, axis=-1, keepdims=True)
    powers = jnp.exp(raw - peak)
    probs = powers / jnp.sum(powers, axis=-1, keepdims=True)
    attention = probs.astype(BF16)
    context = jnp.einsum("shqk,skhd->sqhd", attention, values, preferred_element_type=F32)
    context = context.astype(BF16).reshape(rows, blocks, feat)
    mixed = jnp.einsum("rtc,tdc->rd", context, wm, preferred_element_type=F32)
    hidden, normed_one, scaled_one = normalize(x.astype(F32) + mixed + mixer_shift, gain_one, shift_one)
    hidden_low = hidden.astype(BF16)
    before = jnp.einsum("rd,tdf->rtf", hidden_low, w[1], preferred_element_type=F32) + e_bias
    activated = jax.nn.gelu(before, approximate=False).astype(BF16)
    branch = jnp.einsum("rtf,tdf->rd", activated, w[2], preferred_element_type=F32)
    result, normed_two, scaled_two = normalize(hidden + branch + contract_shift, gain_two, shift_two)
    outputs = result.astype(BF16)
    up = cot.reshape(rows, width).astype(F32)
    gain_two_grad = jnp.sum(up * normed_two, axis=0)
    shift_two_grad = jnp.sum(up, axis=0)
    after_two = normalize_back(up, normed_two, scaled_two, gain_two)
    contract_shift_grad = jnp.sum(after_two, axis=0)
    two_low = after_two.astype(BF16)
    contract_grad = jnp.einsum("rd,rtf->tdf", two_low, activated, preferred_element_type=F32)
    act_grad = jnp.einsum("rd,tdf->rtf", two_low, w[2], preferred_element_type=F32)
    _, gelu_back = jax.vjp(partial(jax.nn.gelu, approximate=False), before)
    before_grad = gelu_back(act_grad)[0].astype(BF16)
    expand_grad = jnp.einsum("rd,rtf->tdf", hidden_low, before_grad, preferred_element_type=F32)
    e_bias_grad = jnp.sum(before_grad, axis=0, dtype=F32)
    hidden_part = jnp.einsum("rtf,tdf->rd", before_grad, w[1], preferred_element_type=F32)
    hidden_grad = after_two + hidden_part
    after_one = normalize_back(hidden_grad, normed_one, scaled_one, gain_one)
    gain_one_grad = jnp.sum(hidden_grad * normed_one, axis=0)
    shift_one_grad = jnp.sum(hidden_grad, axis=0)
    mixer_shift_grad = jnp.sum(after_one, axis=0)
    one_low = after_one.astype(BF16)
    mixer_grad = jnp.einsum("rd,rtc->tdc", one_low, context, preferred_element_type=F32)
    context_grad = jnp.einsum("rd,tdc->rtc", one_low, wm, preferred_element_type=F32).astype(BF16)
    context_grad = context_grad.reshape(seqs, length, blocks * heads, HEAD)
    value_grad = jnp.einsum("shqk,sqhd->skhd", attention, context_grad, preferred_element_type=F32)
    weight_grad = jnp.einsum("sqhd,skhd->shqk", context_grad, values, preferred_element_type=F32)
    score_grad = probs * (weight_grad - jnp.sum(probs * weight_grad, axis=-1, keepdims=True))
    score_grad = score_grad.astype(BF16)
    query_grad = jnp.einsum("shqk,skhd->sqhd", score_grad, keys, preferred_element_type=F32) * SCALE
    key_grad = jnp.einsum("shqk,sqhd->skhd", score_grad, queries, preferred_element_type=F32) * SCALE
    streams = [g.astype(BF16).reshape(rows, blocks, feat) for g in (query_grad, key_grad, value_grad)]
    p_grad = [jnp.sum(streams[i], axis=0, dtype=F32) for i in (0, 2)]
    tgrads = [jnp.einsum("rd,rte->tde", x, s, preferred_element_type=F32) for s in streams] + [mixer_grad]
    att_grad = jnp.concatenate([g[:, :, :cut] for g in tgrads] + [g[:, :, cut:] for g in tgrads], axis=2)
    part = sum(
        jnp.einsum("rte,tde->rd", s, wt, preferred_element_type=F32) for s, wt in zip(streams, (wq, wk, wv))
    )
    input_grad = (after_one + part).astype(BF16)
    grads = jnp.stack([att_grad, expand_grad, contract_grad]).astype(BF16)
    vecs = jnp.stack(
        [mixer_shift_grad, gain_one_grad, shift_one_grad, contract_shift_grad, gain_two_grad, shift_two_grad]
    )
    return outputs, input_grad, grads, vecs, e_bias_grad, jnp.stack(p_grad)


def make_on_device(sizes):
    fast = sizes == {"batch": NZ * NY, "tensor": NX * NC}

    def on_device(
        inputs, lengths, triple_weight, pair_bias, mixer_weight, mixer_bias, first_gain, first_shift,
        expand_weight, expand_bias, contract_weight, contract_bias, second_gain, second_shift, cotangent,
    ):
        pairs, length, width = inputs.shape
        n_tensor, n_batch = sizes["tensor"], sizes["batch"]
        nr = width // n_batch
        own_pairs = pairs // n_tensor
        t = lax.axis_index("tensor")
        feat = width // n_tensor
        if fast:
            vecs = [mixer_bias, first_gain, first_shift, contract_bias, second_gain, second_shift, expand_bias.reshape(-1)]
            vecs.append(pair_bias[:, :, 0])
            outs, ig, triple_grad, mixer_grad, expand_grad, contract_grad, vred = step_call(
                inputs, cotangent, lengths, triple_weight, mixer_weight, expand_weight, contract_weight.T,
                vecs, own_pairs,
            )
            ig = jnp.where(t % NC == 0, ig[..., :feat], ig[..., feat:])
            outs = outs.reshape(pairs, length, width)
            ig = ig.reshape(pairs, length, feat).astype(F32)
            contract_grad = contract_grad.T
        else:
            cut = 2 * HEAD
            four = [triple_weight[0], triple_weight[1], triple_weight[2], mixer_weight.T]
            att = jnp.concatenate([m[:, :cut] for m in four] + [m[:, cut:] for m in four], axis=1)
            pack = jnp.stack([att, expand_weight, contract_weight.T])
            def row(v):
                return jnp.pad(v.reshape(1, -1), ((0, 0), (0, 128 - v.size)))
            vec = jnp.concatenate(
                [row(v) for v in (mixer_bias, first_gain, first_shift, contract_bias, second_gain, second_shift,
                                  expand_bias, pair_bias)] + [jnp.zeros((8, 128), BF16)], axis=0
            )
            w = lax.all_gather(lax.all_gather(pack, "batch", axis=1, tiled=True), "tensor", axis=1)
            v = lax.all_gather(lax.all_gather(vec, "batch"), "tensor")
            d_vec = v[0, :, :6, :nr].transpose(1, 0, 2).reshape(6, width).astype(F32)
            e_bias = v[:, :, 6, :nr].transpose(0, 2, 1).reshape(n_tensor, width).astype(F32)
            p_bias = v[:, :, 7, :2 * feat // n_batch].reshape(n_tensor, n_batch, 2, feat // n_batch)
            p_bias = p_bias.transpose(2, 0, 3, 1).reshape(2, n_tensor, feat).astype(F32)
            mine = partial(lax.dynamic_slice_in_dim, start_index=t * own_pairs, slice_size=own_pairs, axis=0)
            outputs, input_grad, grads, vecs, e_grad, p_grad = layer_step(
                mine(inputs), mine(lengths), mine(cotangent), w, d_vec, e_bias, p_bias
            )
            rows = own_pairs * length
            dv = jnp.broadcast_to(vecs.reshape(1, 6, n_batch, nr).transpose(0, 2, 1, 3), (n_tensor, n_batch, 6, nr))
            ev = e_grad.reshape(n_tensor, nr, n_batch).transpose(0, 2, 1)[:, :, None]
            pv = p_grad.reshape(2, n_tensor, feat // n_batch, n_batch).transpose(1, 3, 0, 2)
            pv = pv.reshape(n_tensor, n_batch, 1, 2 * feat // n_batch)
            lanes = lambda a: jnp.pad(a, ((0, 0), (0, 0), (0, 0), (0, 128 - a.shape[-1])))
            tiles = jnp.concatenate([lanes(dv), lanes(ev), lanes(pv)], axis=2)
            grads = lax.psum_scatter(grads.astype(F32), "tensor", scatter_dimension=1)
            red = lax.psum_scatter(grads, "batch", scatter_dimension=1, tiled=True)
            vred = lax.psum_scatter(lax.psum_scatter(tiles, "tensor"), "batch")
            outs = lax.all_gather(outputs, "tensor").reshape(pairs, length, width)
            ig = lax.all_to_all(
                input_grad.reshape(rows, n_tensor, feat), "tensor", split_axis=1, concat_axis=0, tiled=True
            )
            ig = ig.reshape(pairs, length, feat).astype(F32)
            att_g = red[0]
            four_g = [
                jnp.concatenate([att_g[:, i * cut:(i + 1) * cut], att_g[:, 4 * cut + i * HEAD:4 * cut + (i + 1) * HEAD]], axis=1)
                for i in range(4)
            ]
            triple_grad, mixer_grad = jnp.stack(four_g[:3]), four_g[3].T
            expand_grad, contract_grad = red[1], red[2].T
        return (
            outs,
            ig,
            triple_grad,
            vred[7, :2 * feat // n_batch].reshape(pair_bias.shape),
            mixer_grad,
            vred[0, :nr],
            vred[1, :nr],
            vred[2, :nr],
            expand_grad,
            vred[6, :nr].reshape(expand_bias.shape),
            contract_grad,
            vred[3, :nr],
            vred[4, :nr],
            vred[5, :nr],
        )

    return on_device


def solution(mesh):
    return jax.shard_map(
        make_on_device(dict(mesh.shape)),
        mesh=mesh,
        in_specs=(
            P("batch", None, None),
            P("batch"),
            P(None, "batch", "tensor"),
            P(None, "tensor", "batch"),
            P("tensor", "batch"),
            P("batch"),
            P("batch"),
            P("batch"),
            P("batch", "tensor"),
            P("tensor", "batch"),
            P("tensor", "batch"),
            P("batch"),
            P("batch"),
            P("batch"),
            P("batch", None, None),
        ),
        out_specs=(
            P("batch", None, None),
            P("batch", None, "tensor"),
            P(None, "batch", "tensor"),
            P(None, "tensor", "batch"),
            P("tensor", "batch"),
            P("batch"),
            P("batch"),
            P("batch"),
            P("batch", "tensor"),
            P("tensor", "batch"),
            P("tensor", "batch"),
            P("batch"),
            P("batch"),
            P("batch"),
        ),
        check_vma=False,
    )
```

```python
from functools import partial

import jax
import jax.numpy as jnp
from jax import lax
from jax.experimental import pallas as pl
from jax.experimental.pallas import tpu as pltpu
from jax.sharding import PartitionSpec as P

HEAD = 64
EPS = 1e-12
SCALE = 0.125
MASKED = -1e30
MESH = pl.DeviceIdType.MESH
F32 = jnp.float32
BF16 = jnp.bfloat16
NZ, NY, NX, NC = 4, 2, 2, 2


class Place:
    def __init__(self):
        b = lax.axis_index("batch")
        t = lax.axis_index("tensor")
        self.z, self.y = b // NY, b % NY
        self.x, self.c = t // NC, t % NC

    def at(self, z=None, y=None, x=None, c=None):
        z = self.z if z is None else z
        y = self.y if y is None else y
        x = self.x if x is None else x
        c = self.c if c is None else c
        return (z * NY + y, x * NC + c)

    def core(self):
        return self.at(c=1 - self.c)

    def xp(self):
        return self.at(x=1 - self.x)

    def yp(self):
        return self.at(y=1 - self.y)

    def zp(self, step):
        return self.at(z=(self.z + step) % NZ)

    def peers(self):
        return [self.core(), self.xp(), self.yp()] + [self.zp(s) for s in range(1, NZ)]

    def signal(self):
        barrier = pltpu.get_barrier_semaphore()
        for peer in self.peers():
            pl.semaphore_signal(barrier, inc=1, device_id=peer, device_id_type=MESH)

    def meet(self):
        pl.semaphore_wait(pltpu.get_barrier_semaphore(), len(self.peers()))

    def own(self, axis):
        return {"x": self.x, "y": self.y, "h": self.z // 2, "l": self.z % 2}[axis]

    def along(self, axis):
        if axis == "h":
            return self.zp(2)
        if axis == "l":
            return self.at(z=self.z + 1 - 2 * (self.z % 2))
        return self.xp() if axis == "x" else self.yp()


def remote(src, dst, sems, index, peer):
    return pltpu.make_async_remote_copy(
        src_ref=src,
        dst_ref=dst,
        send_sem=sems.at[0, index],
        recv_sem=sems.at[1, index],
        device_id=peer,
        device_id_type=MESH,
    )


def normalize(value_rows, gain, shift):
    centred = value_rows - jnp.mean(value_rows, axis=-1, keepdims=True)
    scaled = lax.rsqrt(jnp.mean(centred * centred, axis=-1, keepdims=True) + EPS)
    normed = centred * scaled
    return (normed * gain + shift, normed, scaled)


def normalize_back(grad, normed, scaled, gain):
    weighted = grad * gain
    inner = jnp.mean(weighted * normed, axis=-1, keepdims=True)
    return scaled * (weighted - jnp.mean(weighted, axis=-1, keepdims=True) - normed * inner)


SQRT_HALF = 0.7071067811865476
INV_SQRT_2PI = 0.3989422804014327
LOG2_E = 1.4426950408889634
ERF_P = 0.3275911
ERF_A = (0.254829592, -0.284496736, 1.421413741, -1.453152027, 1.061405429)
TILE = 96
CUT = 2 * HEAD


def dot(a, b):
    return lax.dot_general(a, b, (((1,), (0,)), ((), ())), preferred_element_type=F32)


def dot_nt(a, b):
    return lax.dot_general(a, b, (((1,), (1,)), ((), ())), preferred_element_type=F32)


def gelu_parts(v):
    t = 1.0 / (1.0 + (ERF_P * SQRT_HALF) * jnp.abs(v))
    bell = jnp.exp2((-0.5 * LOG2_E) * (v * v))
    poly = 0.5 * ERF_A[4]
    for a in ERF_A[3::-1]:
        poly = poly * t + 0.5 * a
    tail = poly * t * bell
    phi = jnp.where(v < 0.0, tail, 1.0 - tail)
    return v * phi, phi + v * bell * INV_SQRT_2PI


def low_lanes():
    return lax.broadcasted_iota(jnp.int32, (1, CUT), 1) < HEAD


def half_rows():
    lane = lax.broadcasted_iota(jnp.int32, (1, CUT), 1)
    low = jnp.where(lane < HEAD, 1.0, 0.0)
    return low.astype(BF16), (1.0 - low).astype(BF16)


def swap(a):
    return pltpu.roll(a, HEAD, 1)


def sel_matrix(key, b):
    lane = lax.broadcasted_iota(jnp.int32, (128, key.shape[1]), 0) * (NZ * NY) + b
    return jnp.where(lane == key, 1.0, 0.0).astype(BF16)


def sel_keys(width):
    col = lax.broadcasted_iota(jnp.int32, (1, width), 1)
    nr = width // (NZ * NY)
    q = jnp.where(col < CUT, col, col - 3 * CUT)
    v = jnp.where(col < 3 * CUT, col - 2 * CUT, col - 4 * CUT)
    is_q = (col < CUT) | ((col >= 4 * CUT) & (col < 4 * CUT + HEAD))
    is_v = ((col >= 2 * CUT) & (col < 3 * CUT)) | ((col >= 5 * CUT) & (col < 5 * CUT + HEAD))
    head = jnp.where(is_q, q, jnp.where(is_v, v + 3 * HEAD, -1))
    return (col % nr) * (NZ * NY) + col // nr, col, head


def run_hooks(hooks, i):
    for k, step in (hooks or {}).items():
        pl.when(i == k)(step)


class Layer:
    def __init__(self, **refs):
        self.__dict__.update(refs)
        self.tiles = self.x.shape[0]
        self.width = self.x.shape[2]
        self.rows = self.tiles * TILE
        self.seqs = self.qkv.shape[2]
        self.length = self.qkv.shape[3]
        self.per = self.length // TILE

    def weight(self, p, t, lo, size):
        c, x = t // NX, t % NX
        return self.w[p, c, x, :, :, :, :, lo:lo + size].reshape(self.width, size)

    def put_weight(self, p, t, lo, value):
        c, x = t // NX, t % NX
        size = value.shape[1]
        nr = self.width // (NZ * NY)
        self.w[p, c, x, :, :, :, :, lo:lo + size] = value.astype(BF16).reshape(2, 2, NY, nr, size)

    def all_rows(self, ref, *at):
        a = ref[at] if at else ref[...]
        return a.reshape(self.rows, a.shape[-1])

    def seq_rows(self, ref, s, *at):
        a = ref[at + (pl.ds(self.per * s, self.per),)]
        return a.reshape(self.length, a.shape[-1])

    def transposed(self, ref, out):
        a = self.all_rows(ref)
        out[0:self.width, :] = a.T
        out[self.width:, :] = jnp.ones((out.shape[0] - self.width, self.rows), BF16)

    def vectors(self):
        keys = sel_keys(self.width)
        self.vec[...] = jnp.zeros(self.vec.shape, F32)

        @pl.loop(0, NZ * NY)
        def _(b):
            z, y = b // NY, b % NY
            own = self.v[:, :, z, y].reshape(NC * NX * 8, 128).astype(BF16)
            for i, key in enumerate(keys):
                part = dot(own, sel_matrix(key, b)).reshape(NC * NX, 8, self.width)
                self.vec[i] = self.vec[i] + part

    def row(self, i):
        return self.vec[0, 0, i:i + 1, :]

    def projected(self, t, n):
        bias = self.vec[2, t, 7:8, 256 * n:256 * n + 256]
        return dot(self.all_rows(self.x), self.weight(0, t, 256 * n, 256)) + bias

    def put_head(self, i, p, value):
        self.qkv[i, p] = value.astype(BF16).reshape(self.seqs, self.length, CUT)

    def projections_first(self):
        @pl.loop(0, NC * NX)
        def _(t):
            a = self.projected(t, 0)
            self.put_head(0, t, a[:, :CUT])
            self.put_head(1, t, a[:, CUT:])
            bias = self.vec[2, t, 7:8, 2 * CUT:3 * CUT]
            self.put_head(2, t, dot(self.all_rows(self.x), self.weight(0, t, 2 * CUT, CUT)) + bias)

    def projections_third(self):
        low = low_lanes()

        @pl.loop(0, NC)
        def _(u):
            a, b = self.projected(NX * u, 2), self.projected(NX * u + 1, 2)
            self.put_head(0, NC * NX + u, jnp.where(low, a[:, :CUT], swap(b[:, :CUT])))
            self.put_head(1, NC * NX + u, jnp.where(low, swap(a[:, :CUT]), b[:, :CUT]))
            self.put_head(2, NC * NX + u, jnp.where(low, a[:, CUT:], swap(b[:, CUT:])))

    def heads(self, p, s):
        halves = half_rows()
        q, k, v = (self.qkv[i, p, s] for i in range(3))
        valid = lax.broadcasted_iota(jnp.int32, (1, self.length), 1) < self.lens[self.first + s]
        context = []
        for j in range(2):
            scores = jnp.where(valid, dot_nt(q * halves[j], k) * SCALE, MASKED)
            powers = jnp.exp(scores - jnp.max(scores, axis=1, keepdims=True))
            probs = (powers * (1.0 / jnp.sum(powers, axis=1, keepdims=True))).astype(BF16)
            self.probs[p, s, j] = probs
            context.append(dot(probs, v))
        return jnp.where(low_lanes(), *context)

    def put_context(self, t, s, lo, value):
        value = value.astype(BF16).reshape(self.per, TILE, CUT)
        self.ctx[t, pl.ds(self.per * s, self.per), :, lo:lo + CUT] = value

    def attention_first(self, hooks=None):
        @pl.loop(0, NC * NX * self.seqs)
        def _(i):
            run_hooks(hooks, i)
            t, s = i // self.seqs, i % self.seqs
            self.put_context(t, s, 0, self.heads(t, s))

    def attention_third(self, hooks=None):
        low = low_lanes()

        @pl.loop(0, NC * self.seqs)
        def _(i):
            run_hooks(hooks, i)
            u, s = i // self.seqs, i % self.seqs
            context = self.heads(NC * NX + u, s)
            self.put_context(NX * u, s, CUT, jnp.where(low, 0.0, swap(context)))
            self.put_context(NX * u + 1, s, CUT, jnp.where(low, 0.0, context))

    def mixer_weight(self, t):
        return jnp.concatenate([self.weight(0, t, 3 * CUT, CUT), self.weight(0, t, 5 * CUT, CUT)], axis=1)

    def put_rows(self, ref, s, value):
        ref[pl.ds(self.per * s, self.per)] = value.reshape(self.per, TILE, value.shape[1])

    def mix(self):
        @pl.loop(0, self.seqs)
        def _(s):
            total = None
            for t in range(NC * NX):
                part = dot_nt(self.seq_rows(self.ctx, s, t), self.mixer_weight(t))
                total = part if total is None else total + part
            self.put_rows(self.tmp, s, total)

    def norm_first(self, hooks=None):
        @pl.loop(0, self.tiles)
        def _(i):
            run_hooks(hooks, i)
            total = self.x[i].astype(F32) + self.tmp[i] + self.row(0)
            _, normed, scaled = normalize(total, 1.0, 0.0)
            self.norm[i] = normed
            self.scaled[i] = scaled
            self.hidden[i] = (normed * self.row(1) + self.row(2)).astype(BF16)

    def expand(self, hooks, chunks):
        @pl.loop(0, NC * NX)
        def _(t):
            run_hooks(hooks, t)
            hidden = self.all_rows(self.hidden)
            for n in chunks:
                cols = slice(256 * n, 256 * n + 256)
                before = dot(hidden, self.weight(1, t, 256 * n, 256)) + self.vec[1, t, 6:7, cols]
                act, slope = gelu_parts(before)
                self.act[t, :, :, cols] = act.astype(BF16).reshape(self.tiles, TILE, 256)
                self.slope[t, :, :, cols] = slope.astype(BF16).reshape(self.tiles, TILE, 256)

    def times_back(self, p, ref, lo=0, size=None, more=False, hooks=None):
        size = self.width if size is None else size

        @pl.loop(0, self.seqs)
        def _(s):
            run_hooks(hooks, s)
            rows = pl.ds(self.per * s, self.per)
            total = self.tmp[rows].reshape(self.length, self.width) if more else None
            for t in range(NC * NX):
                left = ref[t, rows, :, lo:lo + size].reshape(self.length, size)
                part = dot_nt(left, self.weight(p, t, lo, size))
                total = part if total is None else total + part
            self.put_rows(self.tmp, s, total)

    def add_sum(self, i, value):
        self.sums[i] = self.sums[i] + jnp.sum(value.reshape(TILE // 8, 8, self.width), axis=0)

    def clear_sums(self):
        self.sums[...] = jnp.zeros(self.sums.shape, F32)

    def norm_second(self, hooks=None):
        @pl.loop(0, self.tiles)
        def _(i):
            run_hooks(hooks, i)
            hidden = self.norm[i] * self.row(1) + self.row(2)
            _, normed, scaled = normalize(hidden + self.tmp[i] + self.row(3), 1.0, 0.0)
            self.out[i] = (normed * self.row(4) + self.row(5)).astype(BF16)
            up = self.cot[i].astype(F32)
            self.add_sum(4, up * normed)
            self.add_sum(5, up)
            after = normalize_back(up, normed, scaled, self.row(4))
            self.add_sum(3, after)
            self.grad[i] = after
            self.low[i] = after.astype(BF16)

    def act_back(self, chunks, hooks=None):
        @pl.loop(0, NC * NX)
        def _(t):
            run_hooks(hooks, t)
            low = self.all_rows(self.low)
            for n in chunks:
                cols = slice(256 * n, 256 * n + 256)
                up = dot(low, self.weight(2, t, 256 * n, 256)).reshape(self.tiles, TILE, 256)
                self.slope[t, :, :, cols] = (up * self.slope[t, :, :, cols].astype(F32)).astype(BF16)

    def contract_grad(self, chunks, hooks=None):
        @pl.loop(0, NC * NX)
        def _(t):
            run_hooks(hooks, t)
            left = self.left[0:self.width, :]
            for n in chunks:
                right = self.all_rows(self.act, t, slice(None), slice(None), slice(256 * n, 256 * n + 256))
                self.put_weight(2, t, 256 * n, dot(left, right))

    def expand_grad(self, chunks, hooks=None):
        @pl.loop(0, NC * NX)
        def _(t):
            run_hooks(hooks, t)
            for n in chunks:
                cols = slice(256 * n, 256 * n + 256)
                grad = dot(self.left[...], self.all_rows(self.slope, t, slice(None), slice(None), cols))
                self.put_weight(1, t, 256 * n, grad[:self.width])
                self.unit_sums[0, t, :, cols] = grad[self.width:self.width + 8]

    def norm_first_back(self, hooks=None):
        @pl.loop(0, self.tiles)
        def _(i):
            run_hooks(hooks, i)
            grad = self.grad[i] + self.tmp[i]
            normed = self.norm[i]
            self.add_sum(1, grad * normed)
            self.add_sum(2, grad)
            after = normalize_back(grad, normed, self.scaled[i], self.row(1))
            self.add_sum(0, after)
            self.grad[i] = after
            self.low[i] = after.astype(BF16)

    def context_back(self):
        low = low_lanes()

        @pl.loop(0, NC)
        def _(u):
            third = []
            for d in range(NX):
                t = NX * u + d
                grad = dot(self.all_rows(self.low), self.mixer_weight(t))
                self.cgrad[t] = grad[:, :CUT].astype(BF16).reshape(self.seqs, self.length, CUT)
                third.append(grad[:, CUT:])
            pair = jnp.where(low, swap(third[0]), third[1])
            self.cgrad[NC * NX + u] = pair.astype(BF16).reshape(self.seqs, self.length, CUT)

    def heads_back(self, p, s):
        halves = half_rows()
        q, k, v = (self.qkv[i, p, s] for i in range(3))
        up = self.cgrad[p, s]
        up_t = up.T
        q_t = q.T
        dq, dk, dv = [], [], []
        for j in range(2):
            probs = self.probs[p, s, j]
            dv.append(dot(up_t[HEAD * j:HEAD * j + HEAD], probs))
            weight = dot_nt(up * halves[j], v)
            wide = probs.astype(F32)
            grad = wide * (weight - jnp.sum(wide * weight, axis=1, keepdims=True))
            grad = grad.astype(BF16)
            dq.append(dot(grad, k))
            dk.append(dot(q_t[HEAD * j:HEAD * j + HEAD], grad))
        dq = jnp.where(low_lanes(), *dq) * SCALE
        dk = jnp.concatenate(dk, axis=0).T * SCALE
        dv = jnp.concatenate(dv, axis=0).T
        return dq, dk, dv

    def put_stream(self, t, s, lo, value):
        value = value.astype(BF16).reshape(self.per, TILE, CUT)
        self.act[t, pl.ds(self.per * s, self.per), :, lo:lo + CUT] = value

    def attention_back_first(self, hooks=None):
        @pl.loop(0, NC * NX * self.seqs)
        def _(i):
            run_hooks(hooks, i)
            t, s = i // self.seqs, i % self.seqs
            grads = self.heads_back(t, s)
            for j in range(3):
                self.put_stream(t, s, CUT * j, grads[j])
            self.put_stream(t, s, 3 * CUT, jnp.zeros((self.length, CUT), F32))

    def attention_back_third(self, hooks=None):
        low = low_lanes()

        @pl.loop(0, NC * self.seqs)
        def _(i):
            run_hooks(hooks, i)
            u, s = i // self.seqs, i % self.seqs
            dq, dk, dv = self.heads_back(NC * NX + u, s)
            self.put_stream(NX * u, s, 4 * CUT, jnp.where(low, dq, swap(dk)))
            self.put_stream(NX * u + 1, s, 4 * CUT, jnp.where(low, swap(dq), dk))
            self.put_stream(NX * u, s, 5 * CUT, jnp.where(low, dv, 0.0))
            self.put_stream(NX * u + 1, s, 5 * CUT, jnp.where(low, swap(dv), 0.0))

    def input_back(self):
        half = self.width // NX

        @pl.loop(0, self.tiles)
        def _(i):
            total = (self.grad[i] + self.tmp[i]).astype(BF16)
            for x in range(NX):
                self.igrad[x, i] = total[:, half * x:half * x + half]

    def stream_grad(self, t, n):
        cols = slice(256 * n, 256 * n + 256)
        grad = dot(self.left[...], self.all_rows(self.act, t, slice(None), slice(None), cols))
        self.unit_sums[1, t, :, cols] = grad[self.width:self.width + 8]
        return grad[:self.width]

    def mixer_grad(self, t, h):
        cols = slice(CUT * h, CUT * h + CUT)
        return dot(self.left2[0:self.width, :], self.all_rows(self.ctx, t, slice(None), slice(None), cols))

    def attention_grad_first(self, hooks=None):
        @pl.loop(0, NC * NX)
        def _(t):
            run_hooks(hooks, t)
            self.put_weight(0, t, 0, self.stream_grad(t, 0))
            grad = self.stream_grad(t, 1)
            self.put_weight(0, t, 2 * CUT, grad[:, :CUT])
            self.put_weight(0, t, 3 * CUT, self.mixer_grad(t, 0))

    def attention_grad_third(self, hooks=None):
        @pl.loop(0, NC * NX)
        def _(t):
            run_hooks(hooks, t)
            grad = self.stream_grad(t, 2)
            self.put_weight(0, t, 4 * CUT, grad[:, :CUT])
            self.put_weight(0, t, 5 * CUT, grad[:, CUT:] + self.mixer_grad(t, 1))

    def vector_tiles(self):
        keys = sel_keys(self.width)
        rows = [jnp.sum(self.sums[i], axis=0, keepdims=True) for i in range(6)]
        rows.append(jnp.zeros((2, self.width), F32))
        parts = [jnp.concatenate(rows, axis=0)]
        for i in range(2):
            units = [self.unit_sums[i, t, 0:1, :] for t in range(NC * NX)]
            parts.append(jnp.concatenate(units + [jnp.zeros((4, self.width), F32)], axis=0))
        split = []
        for part in parts:
            high = part.astype(BF16)
            split.append(jnp.concatenate([high, (part - high.astype(F32)).astype(BF16)], axis=0))

        @pl.loop(0, NZ * NY)
        def _(b):
            z, y = b // NY, b % NY
            got = []
            for key, part in zip(keys, split):
                both = dot_nt(part, sel_matrix(key, b))
                got.append(both[:8] + both[8:])
            for t in range(NC * NX):
                self.vtiles[t // NX, t % NX, z, y] = jnp.concatenate(
                    [got[0][:6], got[1][t:t + 1], got[2][t:t + 1]], axis=0
                )


def layer_scratch(seqs, length, width):
    tiles = seqs * length // TILE
    blocks = NC * NX
    pairs = 3 * blocks // 2
    rows = seqs * length
    nr = width // (NZ * NY)
    return [
        pltpu.VMEM((3, NC, NX, 2, 2, NY, nr, width), BF16),
        pltpu.VMEM((tiles, TILE, width), BF16),
        pltpu.VMEM((tiles, TILE, width), BF16),
        pltpu.VMEM((3, pairs, seqs, length, CUT), BF16),
        pltpu.VMEM((pairs, seqs, 2, length, length), BF16),
        pltpu.VMEM((blocks, tiles, TILE, 2 * CUT), BF16),
        pltpu.VMEM((tiles, TILE, width), F32),
        pltpu.VMEM((tiles, TILE, width), F32),
        pltpu.VMEM((tiles, TILE, 1), F32),
        pltpu.VMEM((tiles, TILE, width), BF16),
        pltpu.VMEM((blocks, tiles, TILE, width), BF16),
        pltpu.VMEM((blocks, tiles, TILE, width), BF16),
        pltpu.VMEM((tiles, TILE, width), F32),
        pltpu.VMEM((tiles, TILE, width), BF16),
        pltpu.VMEM((pairs, seqs, length, CUT), BF16),
        pltpu.VMEM((width + 16, rows), BF16),
        pltpu.VMEM((width + 16, rows), BF16),
        pltpu.VMEM((3, blocks, 8, width), F32),
        pltpu.VMEM((6, 8, width), F32),
        pltpu.VMEM((2, blocks, 8, width), F32),
    ]


class Gather:
    def __init__(self, me, w, v, sems, vsems):
        self.me, self.w, self.v, self.sems, self.vsems = me, w, v, sems, vsems

    def hop(self, k, i):
        p, lo, size, route = GATHER_PARTS[k]
        me = self.me
        at = [slice(None) if axis in route[:i] else me.own(axis) for axis in "xhly"]
        slot = self.w.at[(p, me.c, *at, slice(None), pl.ds(lo, size))]
        return remote(slot, slot, self.sems, 4 * k + i, me.along(route[i]))

    def start(self, k, i):
        if i > 0:
            self.hop(k, i - 1).wait_recv()
        self.hop(k, i).start()

    def core(self, group):
        p, lo, size, parts = GATHER_GROUPS[group]
        slot = self.w.at[p, self.me.c, :, :, :, :, :, pl.ds(lo, size)]
        return remote(slot, slot, self.sems, 4 * len(GATHER_PARTS) + group, self.me.core())

    def start_core(self, group):
        for k in GATHER_GROUPS[group][3]:
            self.hop(k, 3).wait_recv()
        self.core(group).start()

    def arrived(self, group):
        self.core(group).wait_recv()

    def left(self, group):
        for k in GATHER_GROUPS[group][3]:
            for i in range(4):
                self.hop(k, i).wait_send()
        self.core(group).wait_send()

    def small(self):
        me, v = self.me, self.v
        def same(slot, index, peer):
            return remote(slot, slot, self.vsems, index, peer)
        return [
            [same(v.at[me.c, me.x, me.z, me.y], s - 1, me.zp(s)) for s in range(1, NZ)],
            [same(v.at[me.c, me.x, :, me.y], 3, me.xp())],
            [same(v.at[me.c, :, :, me.y], 4, me.yp())],
            [same(v.at[me.c], 5, me.core())],
        ]

    def small_step(self, i):
        steps = self.small()
        if i > 0:
            for copy in steps[i - 1]:
                copy.wait_recv()
        if i < len(steps):
            for copy in steps[i]:
                copy.start()

    def small_left(self):
        for copy in sum(self.small(), []):
            copy.wait_send()


GATHER_PARTS = (
    (0, 0, 128, "hyxl"),
    (0, 128, 128, "hlxy"),
    (0, 256, 128, "hlxy"),
    (0, 384, 128, "hlyx"),
    (0, 512, 128, "lhxy"),
    (0, 640, 128, "yhlx"),
    (1, 0, 256, "lhyx"),
    (1, 256, 256, "hxyl"),
    (1, 512, 128, "hyxl"),
    (1, 640, 128, "xhly"),
    (2, 0, 256, "hlyx"),
    (2, 256, 128, "hyxl"),
    (2, 384, 256, "lhxy"),
    (2, 640, 128, "yxhl"),
)
GATHER_GROUPS = (
    (0, 0, 512, (0, 1, 2, 3)), (0, 512, 256, (4, 5)), (1, 0, 256, (6,)), (1, 256, 512, (7, 8, 9)),
    (2, 0, 384, (10, 11)), (2, 384, 384, (12, 13)),
)
SCATTER_PARTS = (
    (2, 0, 256, "lxhy"),
    (2, 256, 128, "hxly"),
    (2, 384, 128, "yhlx"),
    (2, 512, 128, "xlyh"),
    (2, 640, 128, "lyhx"),
    (1, 0, 256, "ylxh"),
    (1, 256, 128, "xhyl"),
    (1, 384, 128, "hlxy"),
    (1, 512, 256, "ylxh"),
    (0, 0, 256, "yhxl"),
    (0, 256, 128, "xlyh"),
    (0, 384, 128, "ylxh"),
    (0, 512, 128, "ylxh"),
    (0, 640, 128, "xylh"),
)
SCATTER_GROUPS = (
    (2, 0, 256, (0,)), (2, 256, 256, (1, 2)), (2, 512, 256, (3, 4)), (1, 0, 256, (5,)), (1, 256, 512, (6, 7, 8)),
    (0, 0, 512, (9, 10, 11)), (0, 512, 256, (12, 13)),
)


class Scatter:
    def __init__(self, me, g, v, bufs, sems, vsems, osems, out, outs, ig, igs):
        self.me, self.g, self.v = me, g, v
        self.rc, self.vc, self.vy, self.vx, self.vz = bufs[:1] + bufs[5:]
        self.rb = bufs[1:5]
        self.sems, self.vsems, self.osems = sems, vsems, osems
        self.out, self.outs, self.ig, self.igs = out, outs, ig, igs

    def core(self, group):
        p, lo, size, _ = SCATTER_GROUPS[group]
        me, cols = self.me, pl.ds(lo, size)
        return remote(
            self.g.at[p, 1 - me.c, :, :, :, :, :, cols], self.rc.at[p, :, :, :, :, :, cols],
            self.sems, 4 * len(SCATTER_PARTS) + group, me.core(),
        )

    def start_core(self, group):
        self.core(group).start()

    def add_core(self, group):
        p, lo, size, _ = SCATTER_GROUPS[group]
        c, cols = self.me.c, slice(lo, lo + size)
        self.core(group).wait_recv()

        @pl.loop(0, NX * 2)
        def _(n):
            x, h = n // 2, n % 2
            for i in range(2):
                for k in range(NY):
                    at = (x, h, i, k, slice(None), cols)
                    self.g[(p, c) + at] = self.g[(p, c) + at] + self.rc[(p,) + at]

    def at(self, k, i, sent):
        route = SCATTER_PARTS[k][3]
        me = self.me
        spot = {axis: me.own(axis) for axis in route[:i]}
        spot[route[i]] = 1 - me.own(route[i]) if sent else me.own(route[i])
        return [spot.get(axis, slice(None)) for axis in "xhly"]

    def hop(self, k, i):
        p, lo, size, route = SCATTER_PARTS[k]
        me, cols = self.me, pl.ds(lo, size)
        src = self.g.at[(p, me.c, *self.at(k, i, True), slice(None), cols)]
        dst = self.rb[i].at[(p,) + (slice(None),) * (4 - i) + (cols,)]
        return remote(src, dst, self.sems, 4 * k + i, me.along(route[i]))

    def start(self, k, i):
        if i > 0:
            self.add(k, i - 1)
        self.hop(k, i).start()

    def add(self, k, i):
        p, lo, size, _ = SCATTER_PARTS[k]
        cols = slice(lo, lo + size)
        self.hop(k, i).wait_recv()
        at = self.at(k, i, False)
        spare = [n for n in range(4) if isinstance(at[n], slice)]
        for n in range(2 ** len(spare)):
            bits = [n >> j & 1 for j in range(len(spare))]
            spot = list(at)
            for place, bit in zip(spare, bits):
                spot[place] = bit
            ref = self.g.at[(p, self.me.c, *spot, slice(None), cols)]
            ref[...] = ref[...] + self.rb[i][(p, *bits, slice(None), cols)]

    def total(self, k):
        p, lo, size, _ = SCATTER_PARTS[k]
        cols = slice(lo, lo + size)
        self.hop(k, 3).wait_recv()
        own = self.g[(p, self.me.c, *self.at(k, 3, False), slice(None), cols)].astype(F32)
        return own + self.rb[3][p, :, cols].astype(F32)

    def left(self, group):
        self.core(group).wait_send()
        for k in SCATTER_GROUPS[group][3]:
            for i in range(4):
                self.hop(k, i).wait_send()

    def small(self, i):
        me, v, sems = self.me, self.v, self.vsems
        if i == 0:
            return [remote(v.at[1 - me.c], self.vc, sems, 0, me.core())]
        if i == 1:
            return [remote(v.at[me.c, :, :, 1 - me.y], self.vy, sems, 1, me.yp())]
        if i == 2:
            return [remote(v.at[me.c, 1 - me.x, :, me.y], self.vx, sems, 2, me.xp())]
        return [
            remote(v.at[me.c, me.x, (me.z + s) % NZ, me.y], self.vz.at[s - 1], sems, 2 + s, me.zp(s))
            for s in range(1, NZ)
        ]

    def small_step(self, i):
        me, v = self.me, self.v
        if i > 0:
            for copy in self.small(i - 1):
                copy.wait_recv()
        if i == 1:
            v[me.c] = v[me.c] + self.vc[...]
        elif i == 2:
            v[me.c, :, :, me.y] = v[me.c, :, :, me.y] + self.vy[...]
        elif i == 3:
            v[me.c, me.x, :, me.y] = v[me.c, me.x, :, me.y] + self.vx[...]
        elif i == 4:
            total = v[me.c, me.x, me.z, me.y]
            for s in range(1, NZ):
                total = total + self.vz[s - 1]
            return total
        for copy in self.small(i):
            copy.start()

    def small_left(self):
        for i in range(4):
            for copy in self.small(i):
                copy.wait_send()

    def outputs(self):
        me = self.me
        t = me.x * NC + me.c
        return [remote(self.out, self.outs.at[t], self.osems, i, peer) for i, peer in enumerate((me.xp(), me.core()))]

    def output_local(self, sem):
        return pltpu.make_async_copy(self.out, self.outs.at[self.me.x * NC + self.me.c], sem)

    def output_forward(self):
        me = self.me
        t = (1 - me.x) * NC + me.c
        return remote(self.outs.at[t], self.outs.at[t], self.osems, 4, me.core())

    def grads(self):
        me = self.me
        t = me.x * NC + me.c
        return [
            remote(self.ig.at[1 - me.x], self.igs.at[t], self.osems, 2, me.xp()),
            remote(self.ig.at[me.x], self.igs.at[t], self.osems, 3, me.core()),
        ]

    def grad_local(self, sem):
        return pltpu.make_async_copy(self.ig.at[self.me.x], self.igs.at[self.me.x * NC + self.me.c], sem)

    def grad_forward(self):
        me = self.me
        t = (1 - me.x) * NC + me.c
        return remote(self.igs.at[t], self.igs.at[t], self.osems, 5, me.core())


def step_kernel(
    x_in, cot_in, lens, tw, mw, ew, cw, b0, b1, b2, b3, b4, b5, b6, pair_in,
    outs, igs, triple_out, mixer_out, expand_out, contract_out, small_out,
    w, v, vtiles, out, ig,
    x, cot, qkv, probs, ctx, tmp, norm, scaled, hidden, act, slope, grad, low, cgrad, left, left2, vec, sums,
    unit_sums,
    rc, rb0, rb1, rb2, rb3, vc, vy, vx, vz,
    gsems, gvsems, sems, vsems, osems, lsems,
):
    me = Place()
    t = lax.axis_index("tensor")
    seqs = qkv.shape[2]
    own = [w.at[p, me.c, me.x, me.z // 2, me.z % 2, me.y] for p in range(3)]
    load_e = pltpu.make_async_copy(ew, own[1], lsems.at[2])
    load_c = pltpu.make_async_copy(cw, own[2], lsems.at[6])
    load_x = pltpu.make_async_copy(x_in.at[t], x, lsems.at[0])
    load_cot = pltpu.make_async_copy(cot_in.at[t], cot, lsems.at[1])
    me.signal()
    for copy in (load_e, load_c, load_x, load_cot):
        copy.start()
    pack_attention(tw, mw, own[0])
    pack_vectors((b0, b1, b2, b3, b4, b5, b6), pair_in, v.at[me.c, me.x, me.z, me.y])
    gather = Gather(me, w, v, gsems, gvsems)
    layer = Layer(
        w=w, x=x, cot=cot, qkv=qkv, probs=probs, ctx=ctx, tmp=tmp, norm=norm, scaled=scaled, hidden=hidden, act=act,
        slope=slope, grad=grad, low=low, cgrad=cgrad, left=left, left2=left2, vec=vec, sums=sums, unit_sums=unit_sums,
        v=v, out=out, igrad=ig, vtiles=vtiles, lens=lens, first=t * seqs,
    )
    scatter = Scatter(me, w, vtiles, (rc, rb0, rb1, rb2, rb3, vc, vy, vx, vz), sems, vsems, osems, out, outs, ig, igs)
    me.meet()
    load_e.wait()
    load_c.wait()
    gather.start(2, 0)
    gather.start(4, 0)
    gather.start(9, 0)
    gather.start(1, 0)
    gather.start(13, 0)
    gather.start(5, 0)
    gather.small_step(0)
    gather.start(0, 0)
    gather.start(3, 0)
    gather.start(2, 1)
    gather.start(11, 0)
    gather.start(1, 1)
    gather.small_step(1)
    gather.start(8, 0)
    gather.start(2, 2)
    gather.start(0, 1)
    gather.start(13, 1)
    load_x.wait()
    load_cot.wait()
    gather.start(3, 1)
    gather.start(5, 1)
    gather.start(6, 0)
    gather.small_step(2)
    gather.start(11, 1)
    layer.clear_sums()
    gather.start(9, 1)
    gather.start(12, 0)
    gather.start(0, 2)
    gather.start(3, 2)
    gather.small_step(3)
    gather.start(8, 1)
    gather.start(2, 3)
    gather.start(6, 1)
    gather.start(1, 2)
    gather.start(5, 2)
    gather.start(4, 1)
    gather.small_step(4)
    gather.start(3, 3)
    gather.start(0, 3)
    gather.start(7, 0)
    gather.start(1, 3)
    gather.start(5, 3)
    gather.start(10, 0)
    gather.start(6, 2)
    gather.start(4, 2)
    gather.start(9, 2)
    gather.start(8, 2)
    layer.vectors()
    gather.start(12, 1)
    gather.start_core(0)
    gather.start(4, 3)
    gather.start(7, 1)
    gather.start(6, 3)
    gather.start(10, 1)
    gather.arrived(0)
    layer.projections_first()
    gather.start(11, 2)
    gather.start(7, 2)
    gather.start(13, 2)
    gather.start(8, 3)
    def at_3_2():
        gather.start_core(1)

    def at_3_4():
        gather.start(12, 2)

    def at_3_5():
        gather.start(10, 2)

    def at_3_6():
        gather.start(7, 3)
        gather.start(9, 3)

    layer.attention_first(hooks={2: at_3_2, 4: at_3_4, 5: at_3_5, 6: at_3_6})
    gather.arrived(1)
    layer.projections_third()
    def at_5_2():
        gather.start_core(2)

    def at_5_3():
        gather.start(10, 3)

    layer.attention_third(hooks={2: at_5_2, 3: at_5_3})
    gather.start(11, 3)
    layer.mix()
    gather.start(12, 3)
    def at_7_2():
        gather.arrived(2)

    def at_7_4():
        gather.start(13, 3)

    layer.norm_first(hooks={2: at_7_2, 4: at_7_4})
    gather.start_core(3)
    layer.expand({}, (0,))
    gather.arrived(3)
    def at_9_2():
        gather.start_core(4)

    def at_9_3():
        gather.start_core(5)

    layer.expand({2: at_9_2, 3: at_9_3}, (1, 2))
    gather.arrived(4)
    layer.times_back(2, act, 0, 384, hooks={})
    gather.arrived(5)
    layer.times_back(2, act, 384, 384, True, hooks={})
    layer.norm_second(hooks={})
    for copy in scatter.outputs():
        copy.start()
    scatter.output_local(lsems.at[4]).start()
    layer.transposed(low, left)
    layer.act_back((0,), hooks={})
    gather.left(4)
    gather.left(5)
    layer.contract_grad((0,), hooks={})
    scatter.start_core(0)
    layer.act_back((1,), hooks={})
    def at_18_1():
        scatter.add_core(0)

    def at_18_2():
        scatter.start(0, 0)

    layer.contract_grad((1,), hooks={1: at_18_1, 2: at_18_2})
    layer.act_back((2,), hooks={})
    def at_20_1():
        scatter.start_core(1)

    layer.contract_grad((2,), hooks={1: at_20_1})
    scatter.start_core(2)
    layer.times_back(1, slope, hooks={})
    scatter.add_core(1)
    layer.transposed(hidden, left)
    gather.left(2)
    gather.left(3)
    scatter.start(2, 0)
    def at_24_3():
        scatter.start(1, 0)

    layer.expand_grad((0,), hooks={3: at_24_3})
    scatter.add_core(2)
    scatter.start_core(3)
    scatter.start(3, 0)
    def at_25_3():
        scatter.start(4, 0)

    layer.expand_grad((1, 2), hooks={3: at_25_3})
    def at_26_2():
        scatter.add_core(3)
        scatter.start(5, 0)

    def at_26_3():
        scatter.start(0, 1)
        scatter.start_core(4)
        scatter.outputs()[0].wait_recv()
        scatter.output_forward().start()
        scatter.start(2, 1)

    layer.norm_first_back(hooks={2: at_26_2, 3: at_26_3})
    layer.transposed(low, left2)
    layer.context_back()
    def at_29_2():
        scatter.add_core(4)
        scatter.start(6, 0)
        scatter.start(8, 0)
        scatter.start(3, 1)
        scatter.start(7, 0)

    layer.attention_back_first(hooks={2: at_29_2})
    scatter.start(5, 1)
    layer.times_back(0, act, 0, 3 * CUT, hooks={})
    layer.transposed(x, left)
    scatter.start(0, 2)
    gather.left(0)
    scatter.start(1, 1)
    layer.attention_grad_first(hooks={})
    scatter.start_core(5)
    scatter.start(3, 2)
    scatter.start(4, 1)
    scatter.start(2, 2)
    scatter.start(5, 2)
    scatter.start(6, 1)
    def at_34_1():
        scatter.start(8, 1)

    def at_34_2():
        scatter.add_core(5)
        scatter.start(9, 0)
        scatter.start(10, 0)
        scatter.start(3, 3)

    layer.attention_back_third(hooks={1: at_34_1, 2: at_34_2})
    layer.times_back(0, act, 4 * CUT, 2 * CUT, True, hooks={})
    layer.input_back()
    for copy in scatter.grads():
        copy.start()
    scatter.grad_local(lsems.at[5]).start()
    scatter.start(4, 2)
    scatter.start(7, 1)
    gather.left(1)
    layer.attention_grad_third(hooks={})
    scatter.start(5, 3)
    scatter.start(11, 0)
    scatter.start_core(6)
    scatter.start(10, 1)
    scatter.add_core(6)
    scatter.start(13, 0)
    scatter_out(scatter, 3, contract_out)
    scatter.start(12, 0)
    scatter.start(8, 2)
    scatter.start(9, 1)
    scatter.start(1, 2)
    scatter.start(2, 3)
    layer.vector_tiles()
    scatter.start(10, 2)
    scatter.start(6, 2)
    scatter.small_step(0)
    scatter.start(11, 1)
    scatter_out(scatter, 5, expand_out)
    scatter.small_step(1)
    scatter.start(12, 1)
    scatter.start(7, 2)
    scatter.start(1, 3)
    scatter.start(10, 3)
    scatter.start(13, 1)
    scatter.start(6, 3)
    scatter.small_step(2)
    scatter.start(11, 2)
    scatter.start(8, 3)
    scatter.grads()[0].wait_recv()
    scatter.grad_forward().start()
    scatter.start(12, 2)
    scatter.start(9, 2)
    scatter.start(13, 2)
    scatter.start(4, 3)
    scatter.start(11, 3)
    scatter.start(7, 3)
    scatter.start(12, 3)
    scatter_out(scatter, 10, tmp.at[0])
    scatter.start(0, 3)
    scatter.start(13, 3)
    scatter_out(scatter, 6, expand_out)
    scatter.small_step(3)
    scatter.start(9, 3)
    scatter_out(scatter, 11, tmp.at[0])
    scatter_out(scatter, 4, contract_out)
    scatter_out(scatter, 7, expand_out)
    scatter_out(scatter, 1, contract_out)
    scatter_out(scatter, 8, expand_out)
    scatter_out(scatter, 2, contract_out)
    scatter_out(scatter, 0, contract_out)
    scatter_out(scatter, 12, tmp.at[0])
    small_out[...] = scatter.small_step(4)
    scatter_out(scatter, 13, tmp.at[0])
    scatter_out(scatter, 9, tmp.at[0])
    unpack_attention(tmp[0], triple_out, mixer_out)
    scatter.outputs()[1].wait_recv()
    scatter.grads()[1].wait_recv()
    for copy in (scatter.output_forward(), scatter.grad_forward()):
        copy.wait()
    for copy in scatter.outputs() + scatter.grads():
        copy.wait_send()
    scatter.output_local(lsems.at[4]).wait()
    scatter.grad_local(lsems.at[5]).wait()
    gather.small_left()
    scatter.small_left()
    for group in range(len(SCATTER_GROUPS)):
        scatter.left(group)


def scatter_out(scatter, k, ref):
    _, lo, size, _ = SCATTER_PARTS[k]
    ref[:, lo:lo + size] = scatter.total(k)


def pack_attention(tw, mw, slot):
    mixer = mw[...].T
    for i in range(3):
        slot[:, CUT * i:CUT * i + CUT] = tw[i, :, 0:CUT]
    slot[:, 3 * CUT:4 * CUT] = mixer[:, 0:CUT]
    slot[:, 4 * CUT:5 * CUT] = jnp.concatenate([tw[0, :, CUT:], tw[1, :, CUT:]], axis=1)
    slot[:, 5 * CUT:6 * CUT] = jnp.concatenate([tw[2, :, CUT:], mixer[:, CUT:]], axis=1)


def pack_vectors(rows, pair, slot):
    slot[...] = jnp.zeros(slot.shape, F32)
    for i, ref in enumerate(rows):
        slot[i:i + 1, 0:ref.shape[0]] = ref[...].astype(F32).reshape(1, ref.shape[0])
    half = pair.shape[1]
    both = pair[...].astype(F32)
    slot[7:8, 0:half] = both[0:1]
    slot[7:8, half:2 * half] = both[1:2]


def unpack_attention(total, triple_out, mixer_out):
    for i in range(3):
        triple_out[i, :, 0:CUT] = total[:, CUT * i:CUT * i + CUT]
        triple_out[i, :, CUT:] = total[:, 4 * CUT + HEAD * i:4 * CUT + HEAD * i + HEAD]
    mixer_out[0:CUT] = total[:, 3 * CUT:4 * CUT].T
    mixer_out[CUT:] = total[:, 5 * CUT + HEAD:].T


def step_call(x, cot, lengths, tw, mw, ew, cw, vecs, seqs):
    pairs, length, width = x.shape
    tiles = seqs * length // TILE
    blocks = NX * NC
    nr, feat = width // (NZ * NY), width // blocks
    shape = (blocks, tiles, TILE, width)
    vmem = pl.BlockSpec(memory_space=pltpu.VMEM)
    hbm = pl.BlockSpec(memory_space=pl.ANY)
    layer = layer_scratch(seqs, length, width)
    small = (8, 128)
    return pl.pallas_call(
        step_kernel,
        out_shape=(
            jax.ShapeDtypeStruct(shape, BF16),
            jax.ShapeDtypeStruct((blocks, tiles, TILE, width // NX), BF16),
            jax.ShapeDtypeStruct((3, nr, feat), F32),
            jax.ShapeDtypeStruct((feat, nr), F32),
            jax.ShapeDtypeStruct((nr, width), F32),
            jax.ShapeDtypeStruct((nr, width), F32),
            jax.ShapeDtypeStruct(small, F32),
        ),
        in_specs=[hbm, hbm, pl.BlockSpec(memory_space=pltpu.SMEM), vmem, vmem, hbm, hbm] + [vmem] * len(vecs),
        out_specs=(hbm, hbm, vmem, vmem, vmem, vmem, vmem),
        scratch_shapes=[
            layer[0],
            pltpu.VMEM((NC, NX, NZ, NY) + small, F32),
            pltpu.VMEM((NC, NX, NZ, NY) + small, F32),
            pltpu.VMEM((tiles, TILE, width), BF16),
            pltpu.VMEM((NX, tiles, TILE, width // NX), BF16),
        ] + layer[1:] + [
            pltpu.VMEM((3, NX, 2, 2, NY, nr, width), BF16),
        ] + [pltpu.VMEM((3,) + (2,) * n + (nr, width), BF16) for n in (3, 2, 1, 0)] + [
            pltpu.VMEM((NX, NZ, NY) + small, F32),
            pltpu.VMEM((NX, NZ) + small, F32),
            pltpu.VMEM((NZ,) + small, F32),
            pltpu.VMEM((NZ - 1,) + small, F32),
            pltpu.SemaphoreType.DMA((2, 4 * len(GATHER_PARTS) + len(GATHER_GROUPS))),
            pltpu.SemaphoreType.DMA((2, 6)),
            pltpu.SemaphoreType.DMA((2, 4 * len(SCATTER_PARTS) + len(SCATTER_GROUPS))),
            pltpu.SemaphoreType.DMA((2, 6)),
            pltpu.SemaphoreType.DMA((2, 6)),
            pltpu.SemaphoreType.DMA((7,)),
        ],
        compiler_params=pltpu.CompilerParams(
            collective_id=0, has_side_effects=True, vmem_limit_bytes=67043328
        ),
    )(x.reshape(shape), cot.reshape(shape), lengths, tw, mw, ew, cw, *vecs)


def layer_step(x_seq, lengths, cot, w, d_vec, e_bias, p_bias):
    seqs, length, width = x_seq.shape
    rows = seqs * length
    blocks = w.shape[1]
    feat = width // blocks
    heads = feat // HEAD
    mixer_shift, gain_one, shift_one, contract_shift, gain_two, shift_two = d_vec
    x = x_seq.reshape(rows, width)
    att = w[0]
    cut = 2 * HEAD
    def columns(i):
        return jnp.concatenate(
            [att[:, :, i * cut:(i + 1) * cut], att[:, :, 4 * cut + i * HEAD:4 * cut + (i + 1) * HEAD]], axis=2
        )
    wq, wk, wv, wm = (columns(i) for i in range(4))
    def project(weight, bias):
        out = jnp.einsum("rd,tde->rte", x, weight, preferred_element_type=F32)
        if bias is not None:
            out = out + bias
        return out.astype(BF16).reshape(seqs, length, blocks * heads, HEAD)
    queries = project(wq, p_bias[0])
    keys = project(wk, None)
    values = project(wv, p_bias[1])
    valid = lax.broadcasted_iota(jnp.int32, (seqs, 1, 1, length), 3) < lengths[:, None, None, None]
    raw = jnp.einsum("sqhd,skhd->shqk", queries, keys, preferred_element_type=F32) * SCALE
    raw = jnp.where(valid, raw, MASKED)
    peak = jnp.max(raw, axis=-1, keepdims=True)
    powers = jnp.exp(raw - peak)
    probs = powers / jnp.sum(powers, axis=-1, keepdims=True)
    attention = probs.astype(BF16)
    context = jnp.einsum("shqk,skhd->sqhd", attention, values, preferred_element_type=F32)
    context = context.astype(BF16).reshape(rows, blocks, feat)
    mixed = jnp.einsum("rtc,tdc->rd", context, wm, preferred_element_type=F32)
    hidden, normed_one, scaled_one = normalize(x.astype(F32) + mixed + mixer_shift, gain_one, shift_one)
    hidden_low = hidden.astype(BF16)
    before = jnp.einsum("rd,tdf->rtf", hidden_low, w[1], preferred_element_type=F32) + e_bias
    activated = jax.nn.gelu(before, approximate=False).astype(BF16)
    branch = jnp.einsum("rtf,tdf->rd", activated, w[2], preferred_element_type=F32)
    result, normed_two, scaled_two = normalize(hidden + branch + contract_shift, gain_two, shift_two)
    outputs = result.astype(BF16)
    up = cot.reshape(rows, width).astype(F32)
    gain_two_grad = jnp.sum(up * normed_two, axis=0)
    shift_two_grad = jnp.sum(up, axis=0)
    after_two = normalize_back(up, normed_two, scaled_two, gain_two)
    contract_shift_grad = jnp.sum(after_two, axis=0)
    two_low = after_two.astype(BF16)
    contract_grad = jnp.einsum("rd,rtf->tdf", two_low, activated, preferred_element_type=F32)
    act_grad = jnp.einsum("rd,tdf->rtf", two_low, w[2], preferred_element_type=F32)
    _, gelu_back = jax.vjp(partial(jax.nn.gelu, approximate=False), before)
    before_grad = gelu_back(act_grad)[0].astype(BF16)
    expand_grad = jnp.einsum("rd,rtf->tdf", hidden_low, before_grad, preferred_element_type=F32)
    e_bias_grad = jnp.sum(before_grad, axis=0, dtype=F32)
    hidden_part = jnp.einsum("rtf,tdf->rd", before_grad, w[1], preferred_element_type=F32)
    hidden_grad = after_two + hidden_part
    after_one = normalize_back(hidden_grad, normed_one, scaled_one, gain_one)
    gain_one_grad = jnp.sum(hidden_grad * normed_one, axis=0)
    shift_one_grad = jnp.sum(hidden_grad, axis=0)
    mixer_shift_grad = jnp.sum(after_one, axis=0)
    one_low = after_one.astype(BF16)
    mixer_grad = jnp.einsum("rd,rtc->tdc", one_low, context, preferred_element_type=F32)
    context_grad = jnp.einsum("rd,tdc->rtc", one_low, wm, preferred_element_type=F32).astype(BF16)
    context_grad = context_grad.reshape(seqs, length, blocks * heads, HEAD)
    value_grad = jnp.einsum("shqk,sqhd->skhd", attention, context_grad, preferred_element_type=F32)
    weight_grad = jnp.einsum("sqhd,skhd->shqk", context_grad, values, preferred_element_type=F32)
    score_grad = probs * (weight_grad - jnp.sum(probs * weight_grad, axis=-1, keepdims=True))
    score_grad = score_grad.astype(BF16)
    query_grad = jnp.einsum("shqk,skhd->sqhd", score_grad, keys, preferred_element_type=F32) * SCALE
    key_grad = jnp.einsum("shqk,sqhd->skhd", score_grad, queries, preferred_element_type=F32) * SCALE
    streams = [g.astype(BF16).reshape(rows, blocks, feat) for g in (query_grad, key_grad, value_grad)]
    p_grad = [jnp.sum(streams[i], axis=0, dtype=F32) for i in (0, 2)]
    tgrads = [jnp.einsum("rd,rte->tde", x, s, preferred_element_type=F32) for s in streams] + [mixer_grad]
    att_grad = jnp.concatenate([g[:, :, :cut] for g in tgrads] + [g[:, :, cut:] for g in tgrads], axis=2)
    part = sum(
        jnp.einsum("rte,tde->rd", s, wt, preferred_element_type=F32) for s, wt in zip(streams, (wq, wk, wv))
    )
    input_grad = (after_one + part).astype(BF16)
    grads = jnp.stack([att_grad, expand_grad, contract_grad]).astype(BF16)
    vecs = jnp.stack(
        [mixer_shift_grad, gain_one_grad, shift_one_grad, contract_shift_grad, gain_two_grad, shift_two_grad]
    )
    return outputs, input_grad, grads, vecs, e_bias_grad, jnp.stack(p_grad)


def make_on_device(sizes):
    fast = sizes == {"batch": NZ * NY, "tensor": NX * NC}

    def on_device(
        inputs, lengths, triple_weight, pair_bias, mixer_weight, mixer_bias, first_gain, first_shift,
        expand_weight, expand_bias, contract_weight, contract_bias, second_gain, second_shift, cotangent,
    ):
        pairs, length, width = inputs.shape
        n_tensor, n_batch = sizes["tensor"], sizes["batch"]
        nr = width // n_batch
        own_pairs = pairs // n_tensor
        t = lax.axis_index("tensor")
        feat = width // n_tensor
        if fast:
            vecs = [mixer_bias, first_gain, first_shift, contract_bias, second_gain, second_shift, expand_bias.reshape(-1)]
            vecs.append(pair_bias[:, :, 0])
            outs, ig, triple_grad, mixer_grad, expand_grad, contract_grad, vred = step_call(
                inputs, cotangent, lengths, triple_weight, mixer_weight, expand_weight, contract_weight.T,
                vecs, own_pairs,
            )
            ig = jnp.where(t % NC == 0, ig[..., :feat], ig[..., feat:]).astype(F32)
            outs = outs.reshape(pairs, length, width)
            ig = ig.reshape(pairs, length, feat)
            contract_grad = contract_grad.T
        else:
            cut = 2 * HEAD
            four = [triple_weight[0], triple_weight[1], triple_weight[2], mixer_weight.T]
            att = jnp.concatenate([m[:, :cut] for m in four] + [m[:, cut:] for m in four], axis=1)
            pack = jnp.stack([att, expand_weight, contract_weight.T])
            def row(v):
                return jnp.pad(v.reshape(1, -1), ((0, 0), (0, 128 - v.size)))
            vec = jnp.concatenate(
                [row(v) for v in (mixer_bias, first_gain, first_shift, contract_bias, second_gain, second_shift,
                                  expand_bias, pair_bias)] + [jnp.zeros((8, 128), BF16)], axis=0
            )
            w = lax.all_gather(lax.all_gather(pack, "batch", axis=1, tiled=True), "tensor", axis=1)
            v = lax.all_gather(lax.all_gather(vec, "batch"), "tensor")
            d_vec = v[0, :, :6, :nr].transpose(1, 0, 2).reshape(6, width).astype(F32)
            e_bias = v[:, :, 6, :nr].transpose(0, 2, 1).reshape(n_tensor, width).astype(F32)
            p_bias = v[:, :, 7, :2 * feat // n_batch].reshape(n_tensor, n_batch, 2, feat // n_batch)
            p_bias = p_bias.transpose(2, 0, 3, 1).reshape(2, n_tensor, feat).astype(F32)
            mine = partial(lax.dynamic_slice_in_dim, start_index=t * own_pairs, slice_size=own_pairs, axis=0)
            outputs, input_grad, grads, vecs, e_grad, p_grad = layer_step(
                mine(inputs), mine(lengths), mine(cotangent), w, d_vec, e_bias, p_bias
            )
            rows = own_pairs * length
            dv = jnp.broadcast_to(vecs.reshape(1, 6, n_batch, nr).transpose(0, 2, 1, 3), (n_tensor, n_batch, 6, nr))
            ev = e_grad.reshape(n_tensor, nr, n_batch).transpose(0, 2, 1)[:, :, None]
            pv = p_grad.reshape(2, n_tensor, feat // n_batch, n_batch).transpose(1, 3, 0, 2)
            pv = pv.reshape(n_tensor, n_batch, 1, 2 * feat // n_batch)
            lanes = lambda a: jnp.pad(a, ((0, 0), (0, 0), (0, 0), (0, 128 - a.shape[-1])))
            tiles = jnp.concatenate([lanes(dv), lanes(ev), lanes(pv)], axis=2)
            grads = lax.psum_scatter(grads.astype(F32), "tensor", scatter_dimension=1)
            red = lax.psum_scatter(grads, "batch", scatter_dimension=1, tiled=True)
            vred = lax.psum_scatter(lax.psum_scatter(tiles, "tensor"), "batch")
            outs = lax.all_gather(outputs, "tensor").reshape(pairs, length, width)
            ig = lax.all_to_all(
                input_grad.reshape(rows, n_tensor, feat), "tensor", split_axis=1, concat_axis=0, tiled=True
            )
            ig = ig.reshape(pairs, length, feat).astype(F32)
            att_g = red[0]
            four_g = [
                jnp.concatenate([att_g[:, i * cut:(i + 1) * cut], att_g[:, 4 * cut + i * HEAD:4 * cut + (i + 1) * HEAD]], axis=1)
                for i in range(4)
            ]
            triple_grad, mixer_grad = jnp.stack(four_g[:3]), four_g[3].T
            expand_grad, contract_grad = red[1], red[2].T
        return (
            outs,
            ig,
            triple_grad,
            vred[7, :2 * feat // n_batch].reshape(pair_bias.shape),
            mixer_grad,
            vred[0, :nr],
            vred[1, :nr],
            vred[2, :nr],
            expand_grad,
            vred[6, :nr].reshape(expand_bias.shape),
            contract_grad,
            vred[3, :nr],
            vred[4, :nr],
            vred[5, :nr],
        )

    return on_device


def solution(mesh):
    return jax.shard_map(
        make_on_device(dict(mesh.shape)),
        mesh=mesh,
        in_specs=(
            P("batch", None, None),
            P("batch"),
            P(None, "batch", "tensor"),
            P(None, "tensor", "batch"),
            P("tensor", "batch"),
            P("batch"),
            P("batch"),
            P("batch"),
            P("batch", "tensor"),
            P("tensor", "batch"),
            P("tensor", "batch"),
            P("batch"),
            P("batch"),
            P("batch"),
            P("batch", None, None),
        ),
        out_specs=(
            P("batch", None, None),
            P("batch", None, "tensor"),
            P(None, "batch", "tensor"),
            P(None, "tensor", "batch"),
            P("tensor", "batch"),
            P("batch"),
            P("batch"),
            P("batch"),
            P("batch", "tensor"),
            P("tensor", "batch"),
            P("tensor", "batch"),
            P("batch"),
            P("batch"),
            P("batch"),
        ),
        check_vma=False,
    )
```
